32 devices in a mesh: dp: 16 (over z, y, core), mp: 2 (over x).
Axes of the slice: x: 2, y: 2, z: 4, core: 2. Of those that a mesh axis runs over, the one named last changes fastest.
Arguments:
- layer_input: bfloat16 [24576, 768], P(('dp', 'mp')), may hold values from -6 to 6
- gain_attn: bfloat16 [768], replicated, may hold values from 0.5 to 1.5
- w_query: bfloat16 [768, 768], P(None, 'mp'), may hold values from -0.3125 to 0.3125
- w_key: bfloat16 [768, 768], P(None, 'mp'), may hold values from -0.21875 to 0.21875
- w_value: bfloat16 [768, 768], P(None, 'mp'), may hold values from -0.21875 to 0.21875
- w_out: bfloat16 [768, 768], P('mp'), may hold values from -0.875 to 0.875
- gain_mlp: bfloat16 [768], replicated, may hold values from 0.5 to 1.5
- w_gate: bfloat16 [768, 2048], P(None, 'mp'), may hold values from -0.21875 to 0.21875
- w_up: bfloat16 [768, 2048], P(None, 'mp'), may hold values from -0.21875 to 0.21875
- w_down: bfloat16 [2048, 768], P('mp'), may hold values from -0.125 to 0.125
- segment_start: int32 [16, 7], P('dp'), may hold values from 0 to 1472, as said below
- segment_parent: int32 [16, 7], P('dp'), may hold values from 0 to 2, as said below
- out_grad: bfloat16 [24576, 768], P(('dp', 'mp')), may hold values from -6 to 6
Outputs:
- output: float32 [24576, 768], P(('dp', 'mp'))
- input_grad: float32 [24576, 768], P(('dp', 'mp'))
- gain_attn_grad: float32 [768], replicated
- w_query_grad: float32 [768, 768], P(None, 'mp')
- w_key_grad: float32 [768, 768], P(None, 'mp')
- w_value_grad: float32 [768, 768], P(None, 'mp')
- w_out_grad: float32 [768, 768], P('mp')
- gain_mlp_grad: float32 [768], replicated
- w_gate_grad: float32 [768, 2048], P(None, 'mp')
- w_up_grad: float32 [768, 2048], P(None, 'mp')
- w_down_grad: float32 [2048, 768], P('mp')
The draws below stay inside these ranges and needn't reach their ends.
Inputs may be any that keep to these rules, and one draw needn't show every extreme that they name: `segment_start`: per tree the segments are stored in order trunk, two branches, four leaves; starts rise strictly from 0, every branch or leaf has 64 to 192 tokens, and the last leaf has exactly 64. `segment_parent`: segment 0 is the trunk (entry 0), segments 1 and 2 have parent 0, and each of them is the parent of exactly two of segments 3 to 6.
All inputs are finite; a program needn't handle non-finite values.
Results may differ from the reference program's by a relative error of at most 0.018.
Values may be sent and summed in bfloat16 or wider, within the bound.
A program may use at most 192 MiB of HBM per device.

```python
import jax
import jax.numpy as jnp
from jax import lax

D = 768
H = 12
HD = 64
FF = 2048
TREE_TOK = 1536
NSEG = 7
SEG = 128
TREES = 16
TOKENS = 24576


def draw_segment_start(key, part):
    low_len = SEG // 2
    high_len = SEG + SEG // 2 + 1
    seg_lengths = jax.random.randint(key, (TREES, NSEG - 1), low_len, high_len, dtype=jnp.int32)
    seg_lengths = seg_lengths.at[:, NSEG - 2].set(low_len)
    trunk_len = TREE_TOK - jnp.sum(seg_lengths, axis=1, keepdims=True, dtype=jnp.int32)
    all_lengths = jnp.concatenate([trunk_len, seg_lengths], axis=1)
    starts = jnp.cumsum(all_lengths, axis=1, dtype=jnp.int32) - all_lengths
    return starts.astype(jnp.int32)


def draw_segment_parent(key, part):
    pattern = jnp.array([1, 1, 2, 2], dtype=jnp.int32)
    tree_keys = jax.random.split(key, TREES)
    leaf_parent = jax.vmap(lambda subkey: jax.random.permutation(subkey, pattern))(tree_keys)
    branch_rows = jnp.zeros((TREES, 3), dtype=jnp.int32)
    return jnp.concatenate([branch_rows, leaf_parent.astype(jnp.int32)], axis=1)


def block_scale(own_key, shape, cuts, low, largest):
    level = 1.0
    for dim, shards_of in cuts:
        heights = jax.random.uniform(jax.random.fold_in(jax.random.fold_in(own_key, 6), dim), (shards_of,), jnp.float32, low / len(cuts), largest / len(cuts))
        level = level * jnp.repeat(jnp.exp(heights), shape[dim] // shards_of).reshape((-1,) + (1,) * (len(shape) - 1 - dim))
    return level


def normal_values(key, shape, scale, reach, cuts=(), held_as=jnp.bfloat16):
    entries = scale * jax.random.normal(key, shape, jnp.float32)
    if cuts:
        entries = entries * block_scale(key, shape, cuts, -0.22, 0.18)
    return jnp.clip(entries, -reach, reach).astype(held_as)


def setup_inputs(seed: int = 0) -> dict:
    key_of = jax.random.split(jax.random.key(seed), 14)
    return {
        "layer_input": normal_values(key_of[0], (TOKENS, D), 1.0, 6.0, ((0, 32),)),
        "gain_attn": jnp.clip(1.0 + 0.1 * jax.random.normal(key_of[1], (D,), jnp.float32), 0.5, 1.5).astype(jnp.bfloat16),
        "w_query": normal_values(key_of[2], (D, H * HD), (D // 2) ** -0.5, 0.3125, ((1, 2),)),
        "w_key": normal_values(key_of[3], (D, H * HD), D ** -0.5, 0.21875, ((1, 2),)),
        "w_value": normal_values(key_of[4], (D, H * HD), D ** -0.5, 0.21875, ((1, 2),)),
        "w_out": normal_values(key_of[5], (H * HD, D), (H * HD // 16) ** -0.5, 0.875, ((0, 2),)),
        "gain_mlp": jnp.clip(1.0 + 0.1 * jax.random.normal(key_of[6], (D,), jnp.float32), 0.5, 1.5).astype(jnp.bfloat16),
        "w_gate": normal_values(key_of[7], (D, FF), D ** -0.5, 0.21875, ((1, 2),)),
        "w_up": normal_values(key_of[8], (D, FF), D ** -0.5, 0.21875, ((1, 2),)),
        "w_down": normal_values(key_of[9], (FF, D), FF ** -0.5, 0.125, ((0, 2),)),
        "segment_start": draw_segment_start(jax.random.fold_in(key_of[13], 71), 0),
        "segment_parent": draw_segment_parent(jax.random.fold_in(key_of[13], 71), 0),
        "out_grad": normal_values(key_of[12], (TOKENS, D), 1.0, 6.0, ((0, 32),)),
    }


EPSILON = 1e-05
ROPE_BASE = 10000.0
HIGHEST = lax.Precision.HIGHEST

@jax.custom_vjp
def low(v):
    return lax.optimization_barrier(v.astype(jnp.bfloat16)).astype(jnp.float32)

@jax.custom_vjp
def low_back(v):
    return v

def low_keep(v):
    return (low(v), None)

def low_pass(kept, grad):
    return (grad,)

def back_keep(v):
    return (v, None)

def back_low(kept, grad):
    return (low(grad),)
low.defvjp(low_keep, low_pass)
low_back.defvjp(back_keep, back_low)

def tree_tables(starts, parents, length):
    seg_count = starts.shape[0]
    tok_index = jnp.arange(length, dtype=jnp.int32)
    labels = jnp.arange(seg_count, dtype=jnp.int32)
    segment = lax.optimization_barrier(jnp.sum((tok_index[:, None] >= starts[None, 1:]).astype(jnp.int32), axis=1, dtype=jnp.int32))
    seg_ends = jnp.concatenate([starts[1:], jnp.full((1,), length, dtype=jnp.int32)])
    seg_lengths = seg_ends - starts
    same_seg = (labels[:, None] == labels[None, :]).astype(jnp.int32)
    parent_hot = (parents[:, None] == labels[None, :]).astype(jnp.int32)
    reaches = same_seg + parent_hot + jnp.dot(parent_hot, parent_hot)
    ancestry = (reaches > 0).astype(jnp.int32)
    offset = jnp.dot(ancestry * (1 - same_seg), seg_lengths)
    onehot = (segment[:, None] == labels[None, :]).astype(jnp.int32)
    position = tok_index - jnp.dot(onehot, starts) + jnp.dot(onehot, offset)
    visible = jnp.dot(onehot, ancestry)
    return (position, visible, onehot)

def rotary_tables(position, head_size):
    half_size = head_size // 2
    inv_freq = ROPE_BASE ** (-2.0 * jnp.arange(half_size, dtype=jnp.float32) / head_size)
    angles = position.astype(jnp.float32)[:, None] * inv_freq[None, :]
    return (jnp.cos(angles), jnp.sin(angles))

def rotate(vectors, cosine, sine_tab):
    half_size = vectors.shape[-1] // 2
    first_half = vectors[..., :half_size]
    second = vectors[..., half_size:]
    cos_b = cosine[:, None, :]
    sin_b = sine_tab[:, None, :]
    return jnp.concatenate([first_half * cos_b - second * sin_b, second * cos_b + first_half * sin_b], axis=-1)

def tree_attention(query, key_rot, values, visible, onehot):
    length = query.shape[0]
    block_rows = min(512, length)
    block_count = length // block_rows
    key_index = jnp.arange(length, dtype=jnp.int32)
    score_scale = HD ** (-0.5)

    def one_block(first_row):
        q_block = lax.dynamic_slice_in_dim(query, first_row, block_rows, 0)
        vis_block = lax.dynamic_slice_in_dim(visible, first_row, block_rows, 0)
        q_index = first_row + jnp.arange(block_rows, dtype=jnp.int32)
        allowed = (jnp.dot(vis_block, onehot.T) > 0) & (key_index[None, :] <= q_index[:, None])
        scores = low_back(jnp.einsum('qhd,khd->hqk', q_block, key_rot, precision=HIGHEST) * score_scale)
        masked = jnp.where(allowed[None], scores, -1e+30)
        row_max = lax.optimization_barrier(jnp.max(masked, axis=-1, keepdims=True))
        exp_terms = jnp.exp(masked - row_max)
        prob_rows = exp_terms / lax.optimization_barrier(jnp.sum(exp_terms, axis=-1, keepdims=True))
        return jnp.einsum('hqk,khd->qhd', low(prob_rows), values, precision=HIGHEST)
    block_starts = jnp.arange(block_count, dtype=jnp.int32) * block_rows
    result = lax.map(jax.checkpoint(one_block), block_starts)
    return result.reshape(length, query.shape[1], query.shape[2])

def rms_scale(vectors):
    return lax.rsqrt(lax.optimization_barrier(jnp.mean(vectors * vectors, axis=-1, keepdims=True)) + EPSILON)

def reference(layer_input, gain_attn, w_query, w_key, w_value, w_out, gain_mlp, w_gate, w_up, w_down, segment_start, segment_parent, out_grad):
    position, visible, onehot = jax.vmap(lambda starts, parents: tree_tables(starts, parents, TREE_TOK))(segment_start, segment_parent)
    cosine, sine_tab = rotary_tables(position.reshape(-1), HD)
    tree_shape = (TREES, TREE_TOK, H, HD)

    def forward(block_in, gain_one, query_mat, key_mat, value_mat, out_mat, gain_two, gate_mat, up_mat, down_mat):
        normed = low(block_in * rms_scale(block_in) * gain_one)
        q_pre = low_back(jnp.dot(normed, query_mat, precision=HIGHEST))
        k_pre = low_back(jnp.dot(normed, key_mat, precision=HIGHEST))
        values = low_back(low(jnp.dot(normed, value_mat, precision=HIGHEST)))
        query = low(rotate(q_pre.reshape(-1, H, HD), cosine, sine_tab)).reshape(tree_shape)
        key_rot = low(rotate(k_pre.reshape(-1, H, HD), cosine, sine_tab)).reshape(tree_shape)
        head_out = lax.map(lambda block_items: tree_attention(block_items[0], block_items[1], block_items[2], block_items[3], block_items[4]), (query, key_rot, values.reshape(tree_shape), visible, onehot))
        head_out = low_back(low(head_out.reshape(-1, H * HD)))
        attn_out = low_back(jnp.dot(head_out, out_mat, precision=HIGHEST))
        residual = block_in + attn_out
        normed_two = low(residual * rms_scale(residual) * gain_two)
        gate_pre = low_back(jnp.dot(normed_two, gate_mat, precision=HIGHEST))
        up_pre = low_back(jnp.dot(normed_two, up_mat, precision=HIGHEST))
        hidden = low(jax.nn.silu(gate_pre) * up_pre)
        return residual + jnp.dot(hidden, down_mat, precision=HIGHEST)
    output, pullback = jax.vjp(forward, layer_input.astype(jnp.float32), gain_attn.astype(jnp.float32), w_query.astype(jnp.float32), w_key.astype(jnp.float32), w_value.astype(jnp.float32), w_out.astype(jnp.float32), gain_mlp.astype(jnp.float32), w_gate.astype(jnp.float32), w_up.astype(jnp.float32), w_down.astype(jnp.float32))
    gradients = pullback(out_grad.astype(jnp.float32))
    return (output, gradients[0], gradients[1], gradients[2], gradients[3], gradients[4], gradients[5], gradients[6], gradients[7], gradients[8], gradients[9])
```

```python
import functools
import math

import jax
import jax.numpy as jnp
from jax import lax
from jax.experimental import pallas as pl
from jax.experimental.pallas import tpu as pltpu
from jax.sharding import Mesh
from jax.sharding import PartitionSpec as P

BF = jnp.bfloat16
F32 = jnp.float32
HD=64; EPS=1e-5; BIG=-1e30
C_Q = (HD**-0.5)*math.log2(math.e)
LN2 = math.log(2.0)
NT=(((1,),(1,)),((),())); NN=(((1,),(0,)),((),())); TN=(((0,),(0,)),((),()))
def dot(a,b,dims=NN): return lax.dot_general(a,b,dims,preferred_element_type=F32)
def lanes(shape): return lax.broadcasted_iota(jnp.int32, shape, 1)

def split3(x):
    hi=x.astype(BF).astype(F32); r=x-hi; mid=r.astype(BF).astype(F32); lo=r-mid
    return hi,mid,lo

def tables(starts, parents, row0, rows, nseg, tree_len):
    sh=(rows,128)
    t = row0 + lax.broadcasted_iota(jnp.int32, sh, 0)
    st=[starts[0,s] for s in range(nseg)]+[tree_len]
    par=[parents[0,s] for s in range(nseg)]
    ln=[st[s+1]-st[s] for s in range(nseg)]
    def pick(vals, idx):
        r = vals[0]
        for s in range(1,nseg): r = jnp.where(idx==s, vals[s], r)
        return r
    D=[]
    gps=[]
    for s in range(nseg):
        p=par[s]; gp=pick(par,p); gps.append(gp)
        off=jnp.where(p!=s, pick(ln,p), 0)+jnp.where((gp!=s)&(gp!=p), pick(ln,gp), 0)
        D.append(off-st[s])
    seg=jnp.zeros(sh,jnp.int32); pos=t+D[0]
    for s in range(1,nseg):
        ge=t>=st[s]
        seg=seg+ge.astype(jnp.int32)
        pos=pos+jnp.where(ge, D[s]-D[s-1], 0)
    f=lanes(sh)-64
    parl=jnp.zeros((1,128),jnp.int32)-1; gpl=parl
    fl=lanes((1,128))-64
    for s in range(nseg):
        parl=jnp.where(fl==s, par[s], parl); gpl=jnp.where(fl==s, gps[s], gpl)
    vis=(f==seg)|(parl==seg)|(gpl==seg)|(f<0)|(f>=nseg)
    qf=jnp.where(f==seg,1.0,0.0)
    kf=jnp.where(vis,0.0,BIG)
    kf=jnp.where((f>=8)&(f<11),1.0,kf)
    return pos.astype(F32), qf, kf

def rot_tables(posf):
    l=lax.broadcasted_iota(jnp.int32,(1,128),1)
    fr=jnp.exp((l%32).astype(F32)*(-2.0*math.log(10000.0)/HD))
    ang=posf*fr
    sg=jnp.where((l%64)<32,-1.0,1.0)
    return jnp.cos(ang), jnp.sin(ang)*sg

def swap32(x):
    l=lanes(x.shape)
    return jnp.where((l&32)==0, pltpu.roll(x,96,1), pltpu.roll(x,32,1))

def fwd_kernel(nseg, starts, parents, x_ref, gain, wq, wk, wv, normed, heads, qe, ke, ve, cos_o, sin_o):
    T=x_ref.shape[0]; R=256; nh=wq.shape[1]//HD
    def proj(c,_):
        r0=pl.multiple_of(c*R,R); rows=pl.ds(r0,R)
        x=x_ref[rows,:].astype(F32)
        r1=lax.rsqrt(jnp.mean(x*x,axis=1,keepdims=True)+EPS)
        n=(x*r1*gain[...].astype(F32)).astype(BF)
        normed[rows,:]=n
        posf,qf,kf=tables(starts,parents,r0,R,nseg,T)
        co,si=rot_tables(posf)
        cos_o[rows,:]=co; sin_o[rows,:]=si
        l=lanes((R,128)); low=l<64
        vone=jnp.where((l>=64)&(l<67),1.0,0.0)
        for p in range(nh//2):
            cs=slice(128*p,128*p+128)
            q=dot(n,wq[:,cs]); k=dot(n,wk[:,cs]); v=dot(n,wv[:,cs])
            q=(q*co+swap32(q)*si)*C_Q; k=k*co+swap32(k)*si
            for hh in range(2):
                if hh: q=pltpu.roll(q,64,1); k=pltpu.roll(k,64,1); v=pltpu.roll(v,64,1)
                qe[2*p+hh,rows,:]=jnp.where(low,q,qf).astype(BF)
                ke[2*p+hh,rows,:]=jnp.where(low,k,kf).astype(BF)
                ve[2*p+hh,rows,:]=jnp.where(low,v,vone).astype(BF)
        return 0
    lax.fori_loop(0,T//R,proj,0)
    B=256
    causal=lax.broadcasted_iota(jnp.int32,(B,B),1)<=lax.broadcasted_iota(jnp.int32,(B,B),0)
    l=lanes((B,128))
    def attend(p,_):
        for i in range(T//B):
            n=(i+1)*B; rows=slice(i*B,(i+1)*B)
            outs=[]
            for hh in range(2):
                h=2*p+hh
                q=qe[h,rows,:]
                s=dot(q,ke[h,0:n,:],NT)
                sd=jnp.where(causal,s[:,n-B:],BIG)
                s=sd if i==0 else jnp.concatenate([s[:,:n-B],sd],axis=1)
                m=jnp.max(s,axis=1,keepdims=True)
                pr=jnp.exp2(s-m).astype(BF)
                o=dot(pr,ve[h,0:n,:])
                den=o[:,64:65]
                o=o*(1.0/den)
                lse=m+jnp.log2(den)
                a,b,c=split3(-lse)
                qq=jnp.where(l==72,a,jnp.where(l==73,b,jnp.where(l==74,c,q.astype(F32))))
                qe[h,rows,:]=qq.astype(BF)
                outs.append(o)
            heads_p=jnp.where(l<64,outs[0],pltpu.roll(outs[1],64,1)).astype(BF)
            heads[rows,pl.ds(pl.multiple_of(p*128,128),128)]=heads_p
        return 0
    lax.fori_loop(0,nh//2,attend,0)

def attn_fwd(x_all, gain, wq, wk, wv, starts, parents):
    T,Dm=x_all.shape; H=wq.shape[1]; nh=H//HD; nseg=starts.shape[1]
    V=pl.BlockSpec(memory_space=pltpu.VMEM); S=pl.BlockSpec(memory_space=pltpu.SMEM)
    sd=jax.ShapeDtypeStruct
    return pl.pallas_call(functools.partial(fwd_kernel,nseg),
        out_shape=(sd((T,Dm),BF), sd((T,H),BF), sd((nh,T,128),BF), sd((nh,T,128),BF), sd((nh,T,128),BF), sd((T,128),F32), sd((T,128),F32)),
        in_specs=[S,S,V,V,V,V,V], out_specs=(V,)*7,
        compiler_params=pltpu.CompilerParams(vmem_limit_bytes=60*2**20), name="attn_fwd",
        )(starts, parents, x_all, gain.reshape(1,-1), wq, wk, wv)

def bwd_kernel(heads, dh_ref, qe, ke, ve, cos_o, sin_o, dq_ref, dk_ref, dv_ref, doe, kt, dqt):
    T=qe.shape[1]; nh=qe.shape[0]; B=256; nb=T//B
    l=lanes((B,128)); low=l<64
    causal=lax.broadcasted_iota(jnp.int32,(B,B),0)<=lax.broadcasted_iota(jnp.int32,(B,B),1)
    def pair(p,_):
        cols=pl.ds(pl.multiple_of(p*128,128),128)
        for i in range(nb):
            rows=slice(i*B,(i+1)*B)
            d=dh_ref[rows,cols].astype(F32); o=heads[rows,cols].astype(F32)
            t=d*o
            for hh in range(2):
                if hh: t=pltpu.roll(t,64,1); d=pltpu.roll(d,64,1)
                delta=jnp.sum(jnp.where(low,t,0.0),axis=1,keepdims=True)
                a,b,c=split3(-delta)
                doe[hh,rows,:]=jnp.where(low,d,jnp.where(l==64,a,jnp.where(l==65,b,jnp.where(l==66,c,0.0)))).astype(BF)
                kt[hh,:,rows]=ke[2*p+hh,rows,:].T[0:64]
        dqt[...]=jnp.zeros_like(dqt)
        for j in range(nb):
            ks=slice(j*B,(j+1)*B); n0=j*B
            res=[]
            for hh in range(2):
                h=2*p+hh
                s=dot(ke[h,ks,:],qe[h,n0:,:],NT)
                dp=dot(ve[h,ks,:],doe[hh,n0:,:],NT)
                sd=jnp.where(causal,s[:,:B],BIG)
                s=sd if j==nb-1 else jnp.concatenate([sd,s[:,B:]],axis=1)
                pt=jnp.exp2(s)
                ds=(pt*dp).astype(BF)
                pt=pt.astype(BF)
                dv=dot(pt,doe[hh,n0:,:])
                dk=dot(ds,qe[h,n0:,:])*LN2
                dqt[64*hh:64*hh+64,n0:]+=dot(kt[hh,:,ks],ds)
                res.append((dk,dv))
            dk=jnp.where(low,res[0][0],pltpu.roll(res[1][0],64,1))
            dv=jnp.where(low,res[0][1],pltpu.roll(res[1][1],64,1))
            co=cos_o[ks,:]; si=sin_o[ks,:]
            dk_ref[ks,cols]=(dk*co-swap32(dk)*si).astype(BF)
            dv_ref[ks,cols]=dv.astype(BF)
        for i in range(nb):
            rows=slice(i*B,(i+1)*B)
            dq=dqt[:,rows].T*(HD**-0.5)
            co=cos_o[rows,:]; si=sin_o[rows,:]
            dq_ref[rows,cols]=(dq*co-swap32(dq)*si).astype(BF)
        return 0
    lax.fori_loop(0,nh//2,pair,0)

def attn_bwd(heads, dh, qe, ke, ve, co, si):
    nh,T,_=qe.shape
    V=pl.BlockSpec(memory_space=pltpu.VMEM); sd=jax.ShapeDtypeStruct
    return pl.pallas_call(bwd_kernel,
        out_shape=(sd(heads.shape,BF),)*3,
        in_specs=[V]*7, out_specs=(V,)*3,
        scratch_shapes=[pltpu.VMEM((2,T,128),BF),pltpu.VMEM((2,64,T),BF),pltpu.VMEM((128,T),F32)],
        compiler_params=pltpu.CompilerParams(vmem_limit_bytes=60*2**20), name="attn_bwd",
        )(heads, dh, qe, ke, ve, co, si)

MESH=pl.DeviceIdType.MESH
RING=8
def ring_chip(r):
    half=RING//2
    return jnp.where(r<half, 2*r, 2*(RING-1-r)+1)
def chip_ring(n):
    return jnp.where(n%2==0, n//2, RING-1-n//2)

class Reducer:
    def __init__(self, own, peer, r1o, r1p, asend, r2, bs, slots, fin, outs, sems, segs):
        self.__dict__.update(locals())
        self.core=lax.axis_index("core"); self.mp=lax.axis_index("mp"); self.chip=lax.axis_index("chip")
        self.pos=chip_ring(self.chip)
        self.nxt=[ring_chip(lax.rem(self.pos+1,RING)), ring_chip(lax.rem(self.pos+RING-1,RING))]
        self.na=len(own)
    def barrier(self):
        b=pltpu.get_barrier_semaphore()
        for d in self.peers(): pl.semaphore_signal(b, inc=1, device_id=d, device_id_type=MESH)
        pl.semaphore_wait(b, len(self.peers()))
    def peers(self):
        p=[{"core":1-self.core},{"chip":self.nxt[0]},{"chip":self.nxt[1]}]
        if self.peer: p.append({"mp":1-self.mp})
        return p
    def cp(self, src, dst, k, dev):
        s=self.sems
        return pltpu.make_async_remote_copy(src,dst,s.at[0,k],s.at[1,k],device_id=dev,device_id_type=MESH)
    def c_core(self,a,which):
        o=1-self.core
        src=(self.own if which==0 else self.peer)[a].at[o]; dst=(self.r1o if which==0 else self.r1p)[a]
        return self.cp(src,dst,which*self.na+a,{"core":o})
    def c_x(self,a): return self.cp(self.asend[a],self.r2[a],2*self.na+a,{"mp":1-self.mp})
    def chunk(self,d,t):
        return lax.rem(self.pos-t+2*RING,RING) if d==0 else lax.rem(self.pos+t,RING)
    def c_rs(self,i,t):
        a,r0,nr,d=self.segs[i]
        ch=self.chunk(d,t+1)
        src=self.bs[a].at[ch,pl.ds(r0,nr)] if t==0 else self.slots[i].at[t-1]
        return self.cp(src,self.slots[i].at[t],3*self.na+i*14+t,{"chip":self.nxt[d]})
    def c_ag(self,i,t):
        a,r0,nr,d=self.segs[i]
        ch=self.chunk(d,t)
        ref=self.fin[a].at[self.core,ch,pl.ds(r0,nr)]
        return self.cp(ref,ref,3*self.na+i*14+7+t,{"chip":self.nxt[d]})
    def c_fin(self,a):
        ref=self.fin[a].at[self.core]
        return self.cp(ref,ref,3*self.na+len(self.segs)*14+a,{"core":1-self.core})
    @staticmethod
    def nsem(na,nseg): return 3*na+nseg*14+na
    def ticks(self):
        na=self.na; R=range(na); I=range(len(self.segs)); out=[]
        def start():
            for a in R:
                if self.peer: self.c_core(a,1).start()
            for a in R: self.c_core(a,0).start()
        out.append(start)
        if self.peer:
            def x(a):
                def f():
                    self.c_core(a,1).wait()
                    self.asend[a][...]=(self.peer[a][self.core].astype(F32)+self.r1p[a][...].astype(F32)).astype(BF)
                    self.c_x(a).start()
                return f
            out+= [x(a) for a in R]
        def b(a):
            def f():
                self.c_core(a,0).wait()
                v=self.own[a][self.core].astype(F32)+self.r1o[a][...].astype(F32)
                if self.peer:
                    self.c_x(a).wait()
                    v=v+self.r2[a][...].astype(F32)
                self.bs[a][...]=v.astype(BF)
            return f
        def first():
            for a in R: b(a)()
            for i in I: self.c_rs(i,0).start()
        out.append(first)
        def rs(t):
            def f():
                for i in I:
                    a,r0,nr,d=self.segs[i]
                    self.c_rs(i,t).wait()
                    ch=self.chunk(d,t+2)
                    v=(self.slots[i][t].astype(F32)+self.bs[a][ch,pl.ds(r0,nr)].astype(F32)).astype(BF)
                    if t<RING-2:
                        self.slots[i][t]=v
                        self.c_rs(i,t+1).start()
                    else:
                        self.fin[a][self.core,self.pos,pl.ds(r0,nr)]=v
                        self.c_ag(i,0).start()
            return f
        out+=[rs(t) for t in range(RING-1)]
        def ag(t):
            def f():
                for i in I:
                    self.c_ag(i,t).wait()
                    if t<RING-2: self.c_ag(i,t+1).start()
            return f
        out+=[ag(t) for t in range(RING-1)]
        def fin():
            for a in R: self.c_fin(a).start()
            def put(a,c):
                self.outs[a][c]=self.fin[a][c].astype(F32)
            for a in R: put(a,self.core)
            for a in R:
                self.c_fin(a).wait(); put(a,1-self.core)
        out.append(fin)
        return out

def scratch(shapes, segs, peer):
    V=lambda s,d=BF: pltpu.VMEM(s,d)
    n=len(shapes); sc=[]
    sc+=[V((RING,r,c)) for r,c in shapes]
    if peer:
        sc+=[V((RING,r,c)) for r,c in shapes]*3
    sc+=[V((RING,r,c)) for r,c in shapes]
    sc+=[V((RING-1,nr,shapes[a][1])) for a,_,nr,_ in segs]
    sc+=[V((2,RING,r,c)) for r,c in shapes]
    sc+=[pltpu.SemaphoreType.DMA((2,Reducer.nsem(n,len(segs))))]
    return sc
def unpack(own,peer,outs,sc,segs):
    n=len(own); sc=list(sc)
    def take(k):
        r=sc[:k]; del sc[:k]; return r
    r1o=take(n)
    r1p=asend=r2=None
    if peer: r1p=take(n); asend=take(n); r2=take(n)
    bs=take(n); slots=take(len(segs)); fin=take(n); sems=sc[0]
    return Reducer(own,peer,r1o,r1p,asend,r2,bs,slots,fin,outs,sems,segs)

def ar_kernel(n,has_peer,segs,*refs):
    own=refs[:n]; k=n
    peer=refs[n:2*n] if has_peer else None
    if has_peer: k=2*n
    outs=refs[k:k+n]; sc=refs[k+n:]
    rd=unpack(own,peer,outs,sc,segs)
    rd.barrier()
    for t in rd.ticks(): t()

def all_reduce(own, peer, segs, cid):
    n=len(own); shapes=[a.shape[2:] for a in own]
    V=pl.BlockSpec(memory_space=pltpu.VMEM)
    args=list(own)+(list(peer) if peer else [])
    return pl.pallas_call(functools.partial(ar_kernel,n,bool(peer),segs),
        out_shape=tuple(jax.ShapeDtypeStruct(a.shape,F32) for a in own),
        in_specs=[V]*len(args), out_specs=(V,)*n,
        scratch_shapes=scratch(shapes,segs,bool(peer)),
        compiler_params=pltpu.CompilerParams(collective_id=cid,has_side_effects=True,vmem_limit_bytes=63*2**20),
        name="grad_reduce")(*args)
SEG1=[(0,0,48,0),(1,0,48,1),(2,0,32,0),(2,32,32,1),(3,0,48,0)]
SEG2=[(0,0,48,0),(1,0,48,1),(2,0,16,0),(2,16,32,1),(3,0,16,0)]

PAIR = [(0, 1), (1, 0)]


def swap(v, axis):
    return lax.ppermute(v, axis, PAIR)


def rms_scale(vectors):
    return lax.rsqrt(jnp.mean(vectors * vectors, axis=-1, keepdims=True) + EPS)


def on_device(layer_input, gain_attn, w_query, w_key, w_value, w_out, gain_mlp, w_gate, w_up, w_down,
              segment_start, segment_parent, out_grad):
    rows, width = layer_input.shape
    core, mp = lax.axis_index("core"), lax.axis_index("mp")
    x_peer = swap(layer_input, "mp")
    first = mp == 0
    x_all = jnp.where(first, jnp.concatenate([layer_input, x_peer]), jnp.concatenate([x_peer, layer_input]))

    def other_half(w):
        half = w.shape[0] // 2
        mine = lax.dynamic_slice_in_dim(w, core * half, half, 0)
        mine, _ = lax.optimization_barrier((mine, x_peer))
        got = swap(mine, "mp")
        rest = swap(got, "core")
        return jnp.where(core == 0, jnp.concatenate([got, rest]), jnp.concatenate([rest, got]))

    peer_out, peer_gate, peer_up, peer_down = (other_half(w) for w in (w_out, w_gate, w_up, w_down))

    normed, heads, qe, ke, ve, cosine, sine = attn_fwd(
        x_all, gain_attn, w_query, w_key, w_value, segment_start, segment_parent
    )
    mine_at, peer_at = mp * rows, (1 - mp) * rows
    heads_own = lax.dynamic_slice_in_dim(heads, mine_at, rows, 0)
    heads_peer = swap(lax.dynamic_slice_in_dim(heads, peer_at, rows, 0), "mp")
    inputs = layer_input.astype(F32)
    residual = inputs + dot(heads_own, w_out) + dot(heads_peer, peer_out)
    inv_two = rms_scale(residual)
    normed_two = (residual * inv_two * gain_mlp).astype(BF)
    output = residual
    d_norm_two = 0.0
    grads = []
    for gate_w, up_w, down_w in ((w_gate, w_up, w_down), (peer_gate, peer_up, peer_down)):
        gate, up = dot(normed_two, gate_w), dot(normed_two, up_w)
        sig = jax.nn.sigmoid(gate)
        silu = gate * sig
        hidden = (silu * up).astype(BF)
        output = output + dot(hidden, down_w)
        d_hidden = dot(out_grad, down_w, NT)
        d_gate = (d_hidden * up * sig * (1.0 + gate * (1.0 - sig))).astype(BF)
        d_up = (d_hidden * silu).astype(BF)
        d_norm_two = d_norm_two + dot(d_gate, gate_w, NT) + dot(d_up, up_w, NT)
        grads.append([dot(normed_two, d_gate, TN), dot(normed_two, d_up, TN), dot(hidden, out_grad, TN)])
    scaled_two = gain_mlp * d_norm_two
    gain_mlp_part = jnp.sum(d_norm_two * residual * inv_two, axis=0)
    d_resid = (
        out_grad.astype(F32)
        + inv_two * scaled_two
        - residual * inv_two**3 * jnp.mean(scaled_two * residual, axis=-1, keepdims=True)
    )
    d_attn = d_resid.astype(BF)
    dh_peer = swap(dot(d_attn, peer_out, NT).astype(BF), "mp")
    dh_own = dot(d_attn, w_out, NT).astype(BF)
    grads[0].append(dot(d_attn, heads_own, TN))
    grads[1].append(dot(d_attn, heads_peer, TN))
    d_heads = jnp.where(first, jnp.concatenate([dh_own, dh_peer]), jnp.concatenate([dh_peer, dh_own]))
    d_qpre, d_kpre, d_value = attn_bwd(heads, d_heads, qe, ke, ve, cosine, sine)
    partial = dot(d_qpre, w_query, NT) + dot(d_kpre, w_key, NT) + dot(d_value, w_value, NT)
    theirs = lax.dynamic_slice_in_dim(partial, peer_at, rows, 0).astype(BF)
    d_norm_one = lax.dynamic_slice_in_dim(partial, mine_at, rows, 0) + swap(theirs, "mp").astype(F32)
    inv_one = rms_scale(inputs)
    scaled_one = gain_attn * d_norm_one
    gain_attn_part = jnp.sum(d_norm_one * inputs * inv_one, axis=0)
    input_grad = (
        d_resid
        + inv_one * scaled_one
        - inputs * inv_one**3 * jnp.mean(scaled_one * inputs, axis=-1, keepdims=True)
    )

    def blocks(g):
        if lax.axis_size("grp") > 1:
            g = lax.psum(g, "grp")
        return g.astype(BF).reshape(2, RING, -1, g.shape[-1])

    def whole(g):
        return g.reshape(-1, g.shape[-1])

    mlp = all_reduce([blocks(g) for g in grads[0]], [blocks(g) for g in grads[1]], SEG1, 1)
    gains = jnp.concatenate([gain_attn_part, gain_mlp_part])
    gains = gains + swap(gains, "mp")
    if lax.axis_size("grp") > 1:
        gains = lax.psum(gains, "grp")
    gains = jnp.pad(gains.reshape(2, RING, 1, -1), ((0, 0), (0, 0), (0, 15), (0, 0)))
    gains = jnp.pad(gains, ((0, 0), (0, 0), (0, 0), (0, 128 - gains.shape[-1]))).astype(BF)
    qkv = [dot(normed, d, TN) for d in (d_qpre, d_kpre, d_value)]
    qkv = all_reduce([blocks(g) for g in qkv] + [gains], None, SEG2, 2)
    gains = qkv[3][:, :, 0, : 2 * width // (2 * RING)].reshape(2, width)
    return (
        output, input_grad, gains[0], whole(qkv[0]), whole(qkv[1]), whole(qkv[2]), whole(mlp[3]).T,
        gains[1], whole(mlp[0]), whole(mlp[1]), whole(mlp[2]),
    )


def solution(mesh):
    fine = Mesh(mesh.devices.reshape(-1, RING, 2, mesh.shape["mp"]), ("grp", "chip", "core", "mp"))
    dp = ("grp", "chip", "core")
    tok, col, row, tree = P(dp + ("mp",), None), P(None, "mp"), P("mp", None), P(dp, None)
    in_specs = (tok, P(), col, col, col, row, P(), col, col, row, tree, tree, tok)
    out_specs = (tok, tok, P(), col, col, col, row, P(), col, col, row)
    return jax.shard_map(on_device, mesh=fine, in_specs=in_specs, out_specs=out_specs, check_vma=False)
```

```python
import functools
import math

import jax
import jax.numpy as jnp
from jax import lax
from jax.experimental import pallas as pl
from jax.experimental.pallas import tpu as pltpu
from jax.sharding import Mesh
from jax.sharding import PartitionSpec as P

BF = jnp.bfloat16
F32 = jnp.float32
HD=64; EPS=1e-5; BIG=-1e30
C_Q = (HD**-0.5)*math.log2(math.e)
LN2 = math.log(2.0)
NT=(((1,),(1,)),((),())); NN=(((1,),(0,)),((),())); TN=(((0,),(0,)),((),()))
def dot(a,b,dims=NN): return lax.dot_general(a,b,dims,preferred_element_type=F32)
def lanes(shape): return lax.broadcasted_iota(jnp.int32, shape, 1)

def split3(x):
    hi=x.astype(BF).astype(F32); r=x-hi; mid=r.astype(BF).astype(F32); lo=r-mid
    return hi,mid,lo

def tables(starts, parents, row0, rows, nseg, tree_len):
    sh=(rows,128)
    t = row0 + lax.broadcasted_iota(jnp.int32, sh, 0)
    st=[starts[0,s] for s in range(nseg)]+[tree_len]
    par=[parents[0,s] for s in range(nseg)]
    ln=[st[s+1]-st[s] for s in range(nseg)]
    def pick(vals, idx):
        r = vals[0]
        for s in range(1,nseg): r = jnp.where(idx==s, vals[s], r)
        return r
    D=[]
    gps=[]
    for s in range(nseg):
        p=par[s]; gp=pick(par,p); gps.append(gp)
        off=jnp.where(p!=s, pick(ln,p), 0)+jnp.where((gp!=s)&(gp!=p), pick(ln,gp), 0)
        D.append(off-st[s])
    seg=jnp.zeros(sh,jnp.int32); pos=t+D[0]
    for s in range(1,nseg):
        ge=t>=st[s]
        seg=seg+ge.astype(jnp.int32)
        pos=pos+jnp.where(ge, D[s]-D[s-1], 0)
    f=lanes(sh)-64
    parl=jnp.zeros((1,128),jnp.int32)-1; gpl=parl
    fl=lanes((1,128))-64
    for s in range(nseg):
        parl=jnp.where(fl==s, par[s], parl); gpl=jnp.where(fl==s, gps[s], gpl)
    vis=(f==seg)|(parl==seg)|(gpl==seg)|(f<0)|(f>=nseg)
    qf=jnp.where(f==seg,1.0,0.0)
    kf=jnp.where(vis,0.0,BIG)
    kf=jnp.where((f>=8)&(f<11),1.0,kf)
    return pos.astype(F32), qf, kf

def rot_tables(posf):
    l=lax.broadcasted_iota(jnp.int32,(1,128),1)
    fr=jnp.exp((l%32).astype(F32)*(-2.0*math.log(10000.0)/HD))
    ang=posf*fr
    sg=jnp.where((l%64)<32,-1.0,1.0)
    return jnp.cos(ang), jnp.sin(ang)*sg

def swap32(x):
    l=lanes(x.shape)
    return jnp.where((l&32)==0, pltpu.roll(x,96,1), pltpu.roll(x,32,1))

def fwd_kernel(nseg, starts, parents, x_ref, gain, wq, wk, wv, normed, heads, qe, ke, ve, cos_o, sin_o):
    T=x_ref.shape[0]; R=256; nh=wq.shape[1]//HD
    def proj(c,_):
        r0=pl.multiple_of(c*R,R); rows=pl.ds(r0,R)
        x=x_ref[rows,:].astype(F32)
        r1=lax.rsqrt(jnp.mean(x*x,axis=1,keepdims=True)+EPS)
        n=(x*r1*gain[...].astype(F32)).astype(BF)
        normed[rows,:]=n
        posf,qf,kf=tables(starts,parents,r0,R,nseg,T)
        co,si=rot_tables(posf)
        cos_o[rows,:]=co; sin_o[rows,:]=si
        l=lanes((R,128)); low=l<64
        vone=jnp.where((l>=64)&(l<67),1.0,0.0)
        for p in range(nh//2):
            cs=slice(128*p,128*p+128)
            q=dot(n,wq[:,cs]); k=dot(n,wk[:,cs]); v=dot(n,wv[:,cs])
            q=(q*co+swap32(q)*si)*C_Q; k=k*co+swap32(k)*si
            for hh in range(2):
                if hh: q=pltpu.roll(q,64,1); k=pltpu.roll(k,64,1); v=pltpu.roll(v,64,1)
                qe[2*p+hh,rows,:]=jnp.where(low,q,qf).astype(BF)
                ke[2*p+hh,rows,:]=jnp.where(low,k,kf).astype(BF)
                ve[2*p+hh,rows,:]=jnp.where(low,v,vone).astype(BF)
        return 0
    lax.fori_loop(0,T//R,proj,0)
    B=256
    causal=lax.broadcasted_iota(jnp.int32,(B,B),1)<=lax.broadcasted_iota(jnp.int32,(B,B),0)
    l=lanes((B,128))
    def attend(p,_):
        for i in range(T//B):
            n=(i+1)*B; rows=slice(i*B,(i+1)*B)
            outs=[]
            for hh in range(2):
                h=2*p+hh
                q=qe[h,rows,:]
                s=dot(q,ke[h,0:n,:],NT)
                sd=jnp.where(causal,s[:,n-B:],BIG)
                s=sd if i==0 else jnp.concatenate([s[:,:n-B],sd],axis=1)
                m=jnp.max(s,axis=1,keepdims=True)
                pr=jnp.exp2(s-m).astype(BF)
                o=dot(pr,ve[h,0:n,:])
                den=o[:,64:65]
                o=o*(1.0/den)
                lse=m+jnp.log2(den)
                a,b,c=split3(-lse)
                qq=jnp.where(l==72,a,jnp.where(l==73,b,jnp.where(l==74,c,q.astype(F32))))
                qe[h,rows,:]=qq.astype(BF)
                outs.append(o)
            heads_p=jnp.where(l<64,outs[0],pltpu.roll(outs[1],64,1)).astype(BF)
            heads[rows,pl.ds(pl.multiple_of(p*128,128),128)]=heads_p
        return 0
    lax.fori_loop(0,nh//2,attend,0)

def attn_fwd(x_all, gain, wq, wk, wv, starts, parents):
    T,Dm=x_all.shape; H=wq.shape[1]; nh=H//HD; nseg=starts.shape[1]
    V=pl.BlockSpec(memory_space=pltpu.VMEM); S=pl.BlockSpec(memory_space=pltpu.SMEM)
    sd=jax.ShapeDtypeStruct
    return pl.pallas_call(functools.partial(fwd_kernel,nseg),
        out_shape=(sd((T,Dm),BF), sd((T,H),BF), sd((nh,T,128),BF), sd((nh,T,128),BF), sd((nh,T,128),BF), sd((T,128),F32), sd((T,128),F32)),
        in_specs=[S,S,V,V,V,V,V], out_specs=(V,)*7,
        compiler_params=pltpu.CompilerParams(vmem_limit_bytes=60*2**20), name="attn_fwd",
        )(starts, parents, x_all, gain.reshape(1,-1), wq, wk, wv)

def bwd_kernel(heads, dh_ref, qe, ke, ve, cos_o, sin_o, dq_ref, dk_ref, dv_ref, doe, kt, dqt):
    T=qe.shape[1]; nh=qe.shape[0]; B=256; nb=T//B
    l=lanes((B,128)); low=l<64
    causal=lax.broadcasted_iota(jnp.int32,(B,B),0)<=lax.broadcasted_iota(jnp.int32,(B,B),1)
    def pair(p,_):
        cols=pl.ds(pl.multiple_of(p*128,128),128)
        for i in range(nb):
            rows=slice(i*B,(i+1)*B)
            d=dh_ref[rows,cols].astype(F32); o=heads[rows,cols].astype(F32)
            t=d*o
            for hh in range(2):
                if hh: t=pltpu.roll(t,64,1); d=pltpu.roll(d,64,1)
                delta=jnp.sum(jnp.where(low,t,0.0),axis=1,keepdims=True)
                a,b,c=split3(-delta)
                doe[hh,rows,:]=jnp.where(low,d,jnp.where(l==64,a,jnp.where(l==65,b,jnp.where(l==66,c,0.0)))).astype(BF)
                kt[hh,:,rows]=ke[2*p+hh,rows,:].T[0:64]
        dqt[...]=jnp.zeros_like(dqt)
        for j in range(nb):
            ks=slice(j*B,(j+1)*B); n0=j*B
            res=[]
            for hh in range(2):
                h=2*p+hh
                s=dot(ke[h,ks,:],qe[h,n0:,:],NT)
                dp=dot(ve[h,ks,:],doe[hh,n0:,:],NT)
                sd=jnp.where(causal,s[:,:B],BIG)
                s=sd if j==nb-1 else jnp.concatenate([sd,s[:,B:]],axis=1)
                pt=jnp.exp2(s)
                ds=(pt*dp).astype(BF)
                pt=pt.astype(BF)
                dv=dot(pt,doe[hh,n0:,:])
                dk=dot(ds,qe[h,n0:,:])*LN2
                dqt[64*hh:64*hh+64,n0:]+=dot(kt[hh,:,ks],ds)
                res.append((dk,dv))
            dk=jnp.where(low,res[0][0],pltpu.roll(res[1][0],64,1))
            dv=jnp.where(low,res[0][1],pltpu.roll(res[1][1],64,1))
            co=cos_o[ks,:]; si=sin_o[ks,:]
            dk_ref[ks,cols]=(dk*co-swap32(dk)*si).astype(BF)
            dv_ref[ks,cols]=dv.astype(BF)
        for i in range(nb):
            rows=slice(i*B,(i+1)*B)
            dq=dqt[:,rows].T*(HD**-0.5)
            co=cos_o[rows,:]; si=sin_o[rows,:]
            dq_ref[rows,cols]=(dq*co-swap32(dq)*si).astype(BF)
        return 0
    lax.fori_loop(0,nh//2,pair,0)

def attn_bwd(heads, dh, qe, ke, ve, co, si):
    nh,T,_=qe.shape
    V=pl.BlockSpec(memory_space=pltpu.VMEM); sd=jax.ShapeDtypeStruct
    return pl.pallas_call(bwd_kernel,
        out_shape=(sd(heads.shape,BF),)*3,
        in_specs=[V]*7, out_specs=(V,)*3,
        scratch_shapes=[pltpu.VMEM((2,T,128),BF),pltpu.VMEM((2,64,T),BF),pltpu.VMEM((128,T),F32)],
        compiler_params=pltpu.CompilerParams(vmem_limit_bytes=60*2**20), name="attn_bwd",
        )(heads, dh, qe, ke, ve, co, si)

MESH=pl.DeviceIdType.MESH
RING=8
def ring_chip(r):
    return jnp.where(r<RING//2, 2*r, 2*(RING-1-r)+1)
def chip_ring(n):
    return jnp.where(n%2==0, n//2, RING-1-n//2)

class Place:
    def __init__(self):
        self.core=lax.axis_index("core"); self.mp=lax.axis_index("mp")
        self.pos=chip_ring(lax.axis_index("chip"))
        self.nxt=[ring_chip(lax.rem(self.pos+1,RING)), ring_chip(lax.rem(self.pos+RING-1,RING))]
    def barrier(self):
        b=pltpu.get_barrier_semaphore()
        ds=[{"core":1-self.core},{"mp":1-self.mp},{"chip":self.nxt[0]},{"chip":self.nxt[1]}]
        for d in ds: pl.semaphore_signal(b, inc=1, device_id=d, device_id_type=MESH)
        pl.semaphore_wait(b, len(ds))

def copy_to(src,dst,sems,k,dev):
    return pltpu.make_async_remote_copy(src,dst,sems.at[0,k],sems.at[1,k],device_id=dev,device_id_type=MESH)

class Stream:
    def __init__(self, shapes, cuts, halves):
        self.shapes,self.halves=shapes,halves
        self.segs=[(h,a,c0,nc,d) for h in range(halves) for a in range(len(shapes)) for d,(c0,nc) in enumerate(cuts[a])]
        self.nseg=len(self.segs); self.na=len(shapes); self.pairs=[(h,a) for h in range(halves) for a in range(self.na)]
        self.nown=self.nseg//halves
    def scratch(self):
        s=[pltpu.VMEM((RING,)+self.shapes[a],BF) for h,a in self.pairs]*2
        s+=[pltpu.VMEM((RING,self.shapes[a][0],nc),BF) for h,a,c0,nc,d in self.segs]
        if self.halves==2: s+=[pltpu.VMEM((self.shapes[a][0],nc),BF) for h,a,c0,nc,d in self.segs[self.nown:]]
        n=2*len(self.pairs)+self.nseg*7+self.nown*(1+7+8+1)
        return s+[pltpu.SemaphoreType.DMA((2,n))]
    def bind(self, place, src, out, sc):
        self.p,self.src,self.out=place,src,out
        n=len(self.pairs); sc=list(sc)
        self.r1=sc[:n]; self.bs=sc[n:2*n]; self.slots=sc[2*n:2*n+self.nseg]
        self.xr=sc[2*n+self.nseg:-1]; self.sems=sc[-1]
        self.o_loc=n; self.o_rs=2*n; self.o_x=self.o_rs+7*self.nseg; self.o_ag=self.o_x+self.nown; self.o_fc=self.o_ag+7*self.nown; self.o_put=self.o_fc+8*self.nown
        return self
    def chunk(self,d,t):
        return lax.rem(self.p.pos-t+2*RING,RING) if d==0 else lax.rem(self.p.pos+t,RING)
    def c1(self,i):
        h,a=self.pairs[i]
        return copy_to(self.src[h][a].at[1-self.p.core],self.r1[i],self.sems,i,{"core":1-self.p.core})
    def cl(self,i):
        h,a=self.pairs[i]
        return pltpu.make_async_copy(self.src[h][a].at[self.p.core],self.bs[i],self.sems.at[0,self.o_loc+i])
    def start(self):
        for i in range(len(self.pairs)): self.c1(i).start()
        for i in range(len(self.pairs)): self.cl(i).start()
    def first(self):
        for i in range(len(self.pairs)):
            self.cl(i).wait(); self.c1(i).wait()
            b,r=self.bs[i],self.r1[i]
            def add(s,_):
                b[s]=(b[s].astype(F32)+r[s].astype(F32)).astype(BF); return 0
            lax.fori_loop(0,RING,add,0)
        for k,(h,a,c0,nc,d) in enumerate(self.segs):
            self.slots[k][0]=self.bs[h*self.na+a][self.chunk(d,1),:,pl.ds(c0,nc)]
            self.crs(k,0).start()
    def crs(self,k,t):
        d=self.segs[k][4]
        return copy_to(self.slots[k].at[t],self.slots[k].at[t+1],self.sems,self.o_rs+7*k+t,{"chip":self.p.nxt[d]})
    def rs(self,t,last=False):
        for k,(h,a,c0,nc,d) in enumerate(self.segs):
            self.crs(k,t).wait()
            self.slots[k][t+1]=(self.slots[k][t+1].astype(F32)+self.bs[h*self.na+a][self.chunk(d,t+2),:,pl.ds(c0,nc)].astype(F32)).astype(BF)
            if not last: self.crs(k,t+1).start()
    def cx(self,k): return copy_to(self.slots[self.nown+k].at[RING-1],self.xr[k],self.sems,self.o_x+k,{"mp":1-self.p.mp})
    def xstart(self):
        for k in range(self.nown): self.cx(k).start()
    def cag(self,k,t):
        h,a,c0,nc,d=self.segs[k]
        dst=self.out[a].at[self.p.core,self.chunk(d,t),:,pl.ds(c0,nc)]
        src=self.slots[k].at[RING-1] if t==0 else dst
        return copy_to(src,dst,self.sems,self.o_ag+7*k+t,{"chip":self.p.nxt[d]})
    def cfc(self,k,t):
        h,a,c0,nc,d=self.segs[k]
        dst=self.out[a].at[self.p.core,self.chunk(d,t),:,pl.ds(c0,nc)]
        src=self.slots[k].at[RING-1] if t==0 else dst
        return copy_to(src,dst,self.sems,self.o_fc+8*k+t,{"core":1-self.p.core})
    def put(self,k):
        h,a,c0,nc,d=self.segs[k]
        return pltpu.make_async_copy(self.slots[k].at[RING-1],self.out[a].at[self.p.core,self.p.pos,:,pl.ds(c0,nc)],self.sems.at[0,self.o_put+k])
    def agstart(self):
        for k in range(self.nown):
            if self.halves==2:
                self.cx(k).wait()
                self.slots[k][RING-1]=(self.slots[k][RING-1].astype(F32)+self.xr[k][...].astype(F32)).astype(BF)
            self.cag(k,0).start()
            self.cfc(k,0).start(); self.put(k).start()
    def ag(self,t):
        for k in range(self.nown):
            self.cag(k,t).wait()
            if t<RING-2: self.cag(k,t+1).start()
            self.cfc(k,t+1).start()
    def finish(self):
        for k in range(self.nown):
            self.put(k).wait()
            for t in range(RING): self.cfc(k,t).wait()

STREAM_A=Stream([(48,1024),(48,384)],[((0,512),(512,512)),((0,256),(256,128))],2)
STREAM_B=Stream([(48,1024),(64,768)],[((0,512),(512,512)),((0,384),(384,384))],2)
STREAM_C=Stream([(48,384)]*3,[((0,256),(256,128)),((0,128),(128,256)),((0,256),(256,128))],1)


def tail_kernel(nA,nB,nC,*refs):
    refs=list(refs)
    def take(n):
        r=refs[:n]; del refs[:n]; return r
    heads,dh_own,dh_send,qe,ke,ve,cos_o,sin_o,normed,x_all,wq,wk,wv,gain_part=take(14)
    srcA=[take(2),take(2)]; srcB=[take(2),take(2)]
    outA=take(2); outB=take(2); outC=take(3); dn_out,gains_out=take(2)
    scA=take(nA); scB=take(nB); scC=take(nC)
    dh,doe,kt,dqt,nt,dq_s,dk_s,dv_s,g0,g1,g2,snd,rcv,gx,gring,sems=take(16)
    at=Place(); mp=at.mp
    R,Dm=dn_out.shape; T=2*R; nh=qe.shape[0]; B=256; nb=T//B
    A=STREAM_A.bind(at,srcA,outA,scA); S2=STREAM_B.bind(at,srcB,outB,scB); C=STREAM_C.bind(at,[[g0,g1,g2]],outC,scC)
    at.barrier()
    mine=pl.multiple_of(mp*R,R)
    c_dh=copy_to(dh_send,dh.at[pl.ds(mine,R)],sems,0,{"mp":1-mp})
    c_dh.start()
    A.start(); S2.start()
    dh[pl.ds(mine,R)]=dh_own[...]
    def tr(i,_):
        c=pl.ds(pl.multiple_of(i*B,B),B)
        nt[:,c]=normed[c,:].T
        return 0
    lax.fori_loop(0,nb,tr,0)
    A.first(); S2.first()
    c_dh.wait()
    l=lanes((B,128)); low=l<64
    causal=lax.broadcasted_iota(jnp.int32,(B,B),0)<=lax.broadcasted_iota(jnp.int32,(B,B),1)
    def pair(p,_):
        cols=pl.ds(pl.multiple_of(p*128,128),128)
        for i in range(nb):
            rows=slice(i*B,(i+1)*B)
            d=dh[rows,cols].astype(F32); o=heads[rows,cols].astype(F32)
            t=d*o
            for hh in range(2):
                if hh: t=pltpu.roll(t,64,1); d=pltpu.roll(d,64,1)
                delta=jnp.sum(jnp.where(low,t,0.0),axis=1,keepdims=True)
                a,b,c=split3(-delta)
                doe[hh,rows,:]=jnp.where(low,d,jnp.where(l==64,a,jnp.where(l==65,b,jnp.where(l==66,c,0.0)))).astype(BF)
                kt[hh,:,rows]=ke[2*p+hh,rows,:].T[0:64]
        dqt[...]=jnp.zeros_like(dqt)
        for j in range(nb):
            ks=slice(j*B,(j+1)*B); n0=j*B
            res=[]
            for hh in range(2):
                h=2*p+hh
                s=dot(ke[h,ks,:],qe[h,n0:,:],NT)
                dp=dot(ve[h,ks,:],doe[hh,n0:,:],NT)
                sd=jnp.where(causal,s[:,:B],BIG)
                s=sd if j==nb-1 else jnp.concatenate([sd,s[:,B:]],axis=1)
                pt=jnp.exp2(s)
                ds=(pt*dp).astype(BF)
                pt=pt.astype(BF)
                dv=dot(pt,doe[hh,n0:,:])
                dk=dot(ds,qe[h,n0:,:])*LN2
                dqt[64*hh:64*hh+64,n0:]+=dot(kt[hh,:,ks],ds)
                res.append((dk,dv))
            dk=jnp.where(low,res[0][0],pltpu.roll(res[1][0],64,1))
            dv=jnp.where(low,res[0][1],pltpu.roll(res[1][1],64,1))
            co=cos_o[ks,:]; si=sin_o[ks,:]
            dk_s[ks,cols]=(dk*co-swap32(dk)*si).astype(BF)
            dv_s[ks,cols]=dv.astype(BF)
            if j==0: A.rs(2*p)
            if j==2: S2.rs(p)
        for i in range(nb):
            rows=slice(i*B,(i+1)*B)
            dq=dqt[:,rows].T*(HD**-0.5)
            co=cos_o[rows,:]; si=sin_o[rows,:]
            dq_s[rows,cols]=(dq*co-swap32(dq)*si).astype(BF)
        A.rs(2*p+1)
        return 0
    lax.fori_loop(0,nh//2,pair,0)
    n=2*RING*48
    for g,d in ((g0,dq_s),(g1,dk_s),(g2,dv_s)):
        for c in range(2):
            for q in range(2):
                r0=c*(Dm//2)+q*(Dm//4)
                v=dot(nt[r0:r0+Dm//4,:],d[...])
                g[c,4*q:4*q+4]=v.reshape(4,Dm//16,-1).astype(BF)
    C.start()
    A.rs(6,True); A.xstart()
    S2.rs(3)
    gsum=jnp.zeros((1,Dm),F32)
    theirs=pl.multiple_of((1-mp)*R,R)
    W=R//3
    def c_dn(c): return copy_to(snd.at[pl.ds(c*W,W)],rcv.at[pl.ds(c*W,W)],sems,1+c,{"mp":1-mp})
    def part(r0):
        rows=pl.ds(pl.multiple_of(r0,W),W)
        v=dot(dq_s[rows,:],wq[...],NT)+dot(dk_s[rows,:],wk[...],NT)+dot(dv_s[rows,:],wv[...],NT)
        x=x_all[rows,:].astype(F32)
        xr=x*lax.rsqrt(jnp.mean(x*x,axis=1,keepdims=True)+EPS)
        return v, jnp.sum(v*xr,axis=0,keepdims=True)
    for c in range(3):
        v,gs=part(theirs+c*W); gsum=gsum+gs
        snd[c*W:(c+1)*W]=v.astype(BF); c_dn(c).start()
    C.first()
    S2.rs(4)
    for c in range(3):
        v,gs=part(mine+c*W); gsum=gsum+gs
        dn_out[c*W:(c+1)*W]=v
    gx[0,0:1]=gsum; gx[0,1:2]=gain_part[...]
    c_gx=copy_to(gx.at[0],gx.at[1],sems,4,{"mp":1-mp}); c_gx.start()
    S2.rs(5)
    A.agstart()
    c_gx.wait(); gx[2]=gx[0]+gx[1]
    c_gc=copy_to(gx.at[2],gx.at[3],sems,5,{"core":1-at.core}); c_gc.start()
    C.rs(0)
    S2.rs(6,True); S2.xstart()
    c_gc.wait(); gring[0]=gx[2]+gx[3]
    def c_gr(t): return copy_to(gring.at[t],gring.at[t+1],sems,6+t,{"chip":at.nxt[0]})
    c_gr(0).start()
    gtot=gring[0]
    for t in range(RING-1):
        A.ag(t)
        if t==1: S2.agstart()
        if t>=2: S2.ag(t-2)
        if t<RING-2: C.rs(t+1,t==RING-3)
        c_gr(t).wait()
        if t<RING-2: c_gr(t+1).start()
        gtot=gtot+gring[t+1]
    gains_out[...]=gtot
    C.agstart()
    for c in range(3):
        c_dn(c).wait()
        r=slice(c*W,(c+1)*W)
        dn_out[r]=dn_out[r]+rcv[r].astype(F32)
    for t in range(RING-1):
        if t+5<RING-1: S2.ag(t+5)
        C.ag(t)
    A.finish(); S2.finish(); C.finish()

def tail(heads,dh_own,dh_send,qe,ke,ve,co,si,normed,x_all,wq,wk,wv,gain_part,own,peer,cid):
    nh,T,_=qe.shape; R,H=dh_own.shape; Dm=normed.shape[1]
    V=pl.BlockSpec(memory_space=pltpu.VMEM); N=pl.BlockSpec(memory_space=pl.ANY); sd=jax.ShapeDtypeStruct
    scs=[s.scratch() for s in (STREAM_A,STREAM_B,STREAM_C)]
    G=pltpu.VMEM((2,RING,Dm//16,H),BF)
    local=[pltpu.VMEM((T,H),BF),pltpu.VMEM((2,T,128),BF),pltpu.VMEM((2,64,T),BF),pltpu.VMEM((128,T),F32),pltpu.VMEM((Dm,T),BF)]
    local+=[pltpu.VMEM((T,H),BF)]*3+[G]*3+[pltpu.VMEM((R,Dm),BF)]*2+[pltpu.VMEM((4,8,Dm),F32),pltpu.VMEM((RING,8,Dm),F32),pltpu.SemaphoreType.DMA((2,6+RING))]
    outs=[sd((2,RING)+s,BF) for st in (STREAM_A,STREAM_B,STREAM_C) for s in st.shapes]
    outs+=[sd((R,Dm),F32),sd((8,Dm),F32)]
    return pl.pallas_call(functools.partial(tail_kernel,*[len(s) for s in scs]),
        out_shape=tuple(outs), in_specs=[V]*14+[N]*8, out_specs=(N,)*7+(V,V),
        scratch_shapes=scs[0]+scs[1]+scs[2]+local,
        compiler_params=pltpu.CompilerParams(collective_id=cid,has_side_effects=True,vmem_limit_bytes=67043328),
        name="backward_tail")(heads,dh_own,dh_send,qe,ke,ve,co,si,normed,x_all,wq,wk,wv,gain_part,*own[:2],*peer[:2],*own[2:],*peer[2:])

PAIR = [(0, 1), (1, 0)]


def swap(v, axis):
    return lax.ppermute(v, axis, PAIR)


def rms_scale(vectors):
    return lax.rsqrt(jnp.mean(vectors * vectors, axis=-1, keepdims=True) + EPS)


def on_device(layer_input, gain_attn, w_query, w_key, w_value, w_out, gain_mlp, w_gate, w_up, w_down,
              segment_start, segment_parent, out_grad):
    rows, width = layer_input.shape
    core, mp = lax.axis_index("core"), lax.axis_index("mp")
    x_peer = swap(layer_input, "mp")
    first = mp == 0
    x_all = jnp.where(first, jnp.concatenate([layer_input, x_peer]), jnp.concatenate([x_peer, layer_input]))

    def other_half(w):
        half = w.shape[0] // 2
        mine = lax.dynamic_slice_in_dim(w, core * half, half, 0)
        mine, _ = lax.optimization_barrier((mine, x_peer))
        got = swap(mine, "mp")
        rest = swap(got, "core")
        return jnp.where(core == 0, jnp.concatenate([got, rest]), jnp.concatenate([rest, got]))

    peer_out, peer_gate, peer_up, peer_down = (other_half(w) for w in (w_out, w_gate, w_up, w_down))

    normed, heads, qe, ke, ve, cosine, sine = attn_fwd(
        x_all, gain_attn, w_query, w_key, w_value, segment_start, segment_parent
    )
    mine_at, peer_at = mp * rows, (1 - mp) * rows
    heads_own = lax.dynamic_slice_in_dim(heads, mine_at, rows, 0)
    heads_peer = swap(lax.dynamic_slice_in_dim(heads, peer_at, rows, 0), "mp")
    inputs = layer_input.astype(F32)
    residual = inputs + dot(heads_own, w_out) + dot(heads_peer, peer_out)
    inv_two = rms_scale(residual)
    normed_two = (residual * inv_two * gain_mlp).astype(BF)
    output = residual
    d_norm_two = 0.0
    grads = []
    for gate_w, up_w, down_w in ((w_gate, w_up, w_down), (peer_gate, peer_up, peer_down)):
        gate, up = dot(normed_two, gate_w), dot(normed_two, up_w)
        sig = jax.nn.sigmoid(gate)
        silu = gate * sig
        hidden = (silu * up).astype(BF)
        output = output + dot(hidden, down_w)
        d_hidden = dot(out_grad, down_w, NT)
        d_gate = (d_hidden * up * sig * (1.0 + gate * (1.0 - sig))).astype(BF)
        d_up = (d_hidden * silu).astype(BF)
        d_norm_two = d_norm_two + dot(d_gate, gate_w, NT) + dot(d_up, up_w, NT)
        grads.append([dot(normed_two, d_gate, TN), dot(normed_two, d_up, TN), dot(hidden, out_grad, TN)])
    scaled_two = gain_mlp * d_norm_two
    gain_mlp_part = jnp.sum(d_norm_two * residual * inv_two, axis=0)
    d_resid = (
        out_grad.astype(F32)
        + inv_two * scaled_two
        - residual * inv_two**3 * jnp.mean(scaled_two * residual, axis=-1, keepdims=True)
    )
    d_attn = d_resid.astype(BF)
    dh_send = dot(d_attn, peer_out, NT).astype(BF)
    dh_own = dot(d_attn, w_out, NT).astype(BF)
    grads[0].append(dot(d_attn, heads_own, TN))
    grads[1].append(dot(d_attn, heads_peer, TN))

    def blocks(g):
        if lax.axis_size("grp") > 1:
            g = lax.psum(g, "grp")
        return g.astype(BF).reshape(2, RING, -1, g.shape[-1])

    def whole(g):
        return g.reshape(-1, g.shape[-1])

    own, peer = ([blocks(h[i]) for i in (0, 3, 1, 2)] for h in grads)
    gate_g, out_g, up_g, down_g, query_g, key_g, value_g, d_norm_one, gains = tail(
        heads, dh_own, dh_send, qe, ke, ve, cosine, sine, normed, x_all, w_query, w_key, w_value,
        gain_mlp_part.reshape(1, -1), own, peer, 1,
    )
    inv_one = rms_scale(inputs)
    scaled_one = gain_attn * d_norm_one
    input_grad = (
        d_resid
        + inv_one * scaled_one
        - inputs * inv_one**3 * jnp.mean(scaled_one * inputs, axis=-1, keepdims=True)
    )
    query_g, key_g, value_g = whole(query_g), whole(key_g), whole(value_g)
    gain_attn_grad, gain_mlp_grad = gains[0], gains[1]
    if lax.axis_size("grp") > 1:
        query_g, key_g, value_g, gain_attn_grad, gain_mlp_grad = lax.psum(
            (query_g.astype(F32), key_g.astype(F32), value_g.astype(F32), gain_attn_grad, gain_mlp_grad), "grp"
        )
    return (
        output, input_grad, gain_attn_grad, query_g.astype(F32), key_g.astype(F32), value_g.astype(F32),
        whole(out_g).T.astype(F32), gain_mlp_grad, whole(gate_g).astype(F32), whole(up_g).astype(F32),
        whole(down_g).astype(F32),
    )


def solution(mesh):
    fine = Mesh(mesh.devices.reshape(-1, RING, 2, mesh.shape["mp"]), ("grp", "chip", "core", "mp"))
    dp = ("grp", "chip", "core")
    tok, col, row, tree = P(dp + ("mp",), None), P(None, "mp"), P("mp", None), P(dp, None)
    in_specs = (tok, P(), col, col, col, row, P(), col, col, row, tree, tree, tok)
    out_specs = (tok, tok, P(), col, col, col, row, P(), col, col, row)
    return jax.shard_map(on_device, mesh=fine, in_specs=in_specs, out_specs=out_specs, check_vma=False)
```

```python
import functools
import math

import jax
import jax.numpy as jnp
from jax import lax
from jax.experimental import pallas as pl
from jax.experimental.pallas import tpu as pltpu
from jax.sharding import Mesh
from jax.sharding import PartitionSpec as P

BF = jnp.bfloat16
F32 = jnp.float32
HD=64; EPS=1e-5; BIG=-1e30
C_Q = (HD**-0.5)*math.log2(math.e)
LN2 = math.log(2.0)
NT=(((1,),(1,)),((),())); NN=(((1,),(0,)),((),())); TN=(((0,),(0,)),((),()))
def dot(a,b,dims=NN): return lax.dot_general(a,b,dims,preferred_element_type=F32)
def lanes(shape): return lax.broadcasted_iota(jnp.int32, shape, 1)

def split3(x):
    hi=x.astype(BF).astype(F32); r=x-hi; mid=r.astype(BF).astype(F32); lo=r-mid
    return hi,mid,lo

def tables(starts, parents, row0, rows, nseg, tree_len):
    sh=(rows,128)
    t = row0 + lax.broadcasted_iota(jnp.int32, sh, 0)
    st=[starts[0,s] for s in range(nseg)]+[tree_len]
    par=[parents[0,s] for s in range(nseg)]
    ln=[st[s+1]-st[s] for s in range(nseg)]
    def pick(vals, idx):
        r = vals[0]
        for s in range(1,nseg): r = jnp.where(idx==s, vals[s], r)
        return r
    D=[]
    gps=[]
    for s in range(nseg):
        p=par[s]; gp=pick(par,p); gps.append(gp)
        off=jnp.where(p!=s, pick(ln,p), 0)+jnp.where((gp!=s)&(gp!=p), pick(ln,gp), 0)
        D.append(off-st[s])
    seg=jnp.zeros(sh,jnp.int32); pos=t+D[0]
    for s in range(1,nseg):
        ge=t>=st[s]
        seg=seg+ge.astype(jnp.int32)
        pos=pos+jnp.where(ge, D[s]-D[s-1], 0)
    f=lanes(sh)-64
    parl=jnp.zeros((1,128),jnp.int32)-1; gpl=parl
    fl=lanes((1,128))-64
    for s in range(nseg):
        parl=jnp.where(fl==s, par[s], parl); gpl=jnp.where(fl==s, gps[s], gpl)
    vis=(f==seg)|(parl==seg)|(gpl==seg)|(f<0)|(f>=nseg)
    qf=jnp.where(f==seg,1.0,0.0)
    kf=jnp.where(vis,0.0,BIG)
    kf=jnp.where((f>=8)&(f<11),1.0,kf)
    return pos.astype(F32), qf, kf

def rot_tables(posf):
    l=lax.broadcasted_iota(jnp.int32,(1,128),1)
    fr=jnp.exp((l%32).astype(F32)*(-2.0*math.log(10000.0)/HD))
    ang=posf*fr
    sg=jnp.where((l%64)<32,-1.0,1.0)
    return jnp.cos(ang), jnp.sin(ang)*sg

def swap32(x):
    l=lanes(x.shape)
    return jnp.where((l&32)==0, pltpu.roll(x,96,1), pltpu.roll(x,32,1))


MESH=pl.DeviceIdType.MESH
RING=8
def ring_chip(r):
    return jnp.where(r<RING//2, 2*r, 2*(RING-1-r)+1)
def chip_ring(n):
    return jnp.where(n%2==0, n//2, RING-1-n//2)

class Place:
    def __init__(self):
        self.core=lax.axis_index("core"); self.mp=lax.axis_index("mp")
        self.pos=chip_ring(lax.axis_index("chip"))
        self.nxt=[ring_chip(lax.rem(self.pos+1,RING)), ring_chip(lax.rem(self.pos+RING-1,RING))]
    def barrier(self):
        b=pltpu.get_barrier_semaphore()
        ds=[{"core":1-self.core},{"mp":1-self.mp},{"chip":self.nxt[0]},{"chip":self.nxt[1]}]
        for d in ds: pl.semaphore_signal(b, inc=1, device_id=d, device_id_type=MESH)
        pl.semaphore_wait(b, len(ds))

def copy_to(src,dst,sems,k,dev):
    return pltpu.make_async_remote_copy(src,dst,sems.at[0,k],sems.at[1,k],device_id=dev,device_id_type=MESH)

class Gather:
    def __init__(self,p,src,out,kinds,sems):
        self.p,self.src,self.out,self.kinds,self.sems=p,src,out,kinds,sems
    def ref(self,x,a,ch,core=None):
        n=self.out[a].shape[0]//(2*RING)
        return x[a].at[pl.ds(pl.multiple_of((self.p.core*RING+ch)*n,n),n)]
    def at(self,d,dist): return lax.rem(self.p.pos+(dist if d==0 else RING-dist),RING)
    def hops(self,a,d): return 4-self.kinds[a] if d==0 else 3+self.kinds[a]
    def cp(self,src,dst,a,k,dev):
        return pltpu.make_async_remote_copy(src,dst,self.sems.at[0,a,k],self.sems.at[1,a,k],device_id=dev,device_id_type=MESH)
    def cx(self,a): return self.cp(self.ref(self.src,a,self.p.pos),self.ref(self.out,a,self.p.pos),a,0,{"mp":1-self.p.mp})
    def cag(self,a,d,t):
        r=self.ref(self.out,a,self.at(1-d,t))
        return self.cp(r,r,a,1+4*d+t,{"chip":self.p.nxt[d]})
    def cfc(self,a,d,t):
        r=self.ref(self.out,a,self.at(1-d,t+1))
        return self.cp(r,r,a,9+4*d+t,{"core":1-self.p.core})
    def cfo(self,a):
        r=self.ref(self.out,a,self.p.pos)
        return self.cp(r,r,a,17,{"core":1-self.p.core})
    def agstart(self,a):
        self.cx(a).wait()
        for d in range(2): self.cag(a,d,0).start()
        self.cfo(a).start()
    def ag(self,a,t):
        for d in range(2):
            if t<self.hops(a,d):
                self.cag(a,d,t).wait()
                if t+1<self.hops(a,d): self.cag(a,d,t+1).start()
                self.cfc(a,d,t).start()
    def finish(self,a):
        self.cfo(a).wait()
        for d in range(2):
            for t in range(self.hops(a,d)): self.cfc(a,d,t).wait()

def front_kernel(nseg,starts,parents,x_ref,gain,wq,wk,wv,*refs):
    refs=list(refs)
    def take(n):
        r=refs[:n]; del refs[:n]; return r
    NW=(len(refs)-13)//2
    src=take(NW)
    x_peer,normed,heads,hrecv,qe,ke,ve,cos_o,sin_o=take(9); out=take(NW)
    qf_s,kf_s,sems,wsems=take(4)
    at=Place(); mp=at.mp
    R=x_ref.shape[0]; T=2*R; B=256; nh=wq.shape[1]//HD
    G=Gather(at,src,out,[a%2 for a in range(NW)],wsems)
    mine=pl.multiple_of(mp*R,R); theirs=pl.multiple_of((1-mp)*R,R)
    at.barrier()
    peer={"mp":1-mp}
    for a in range(2): G.cx(a).start()
    c_x=copy_to(x_ref,x_peer,sems,0,peer); c_x.start()
    for a in range(2,NW): G.cx(a).start()
    def tab(c,_):
        r0=pl.multiple_of(c*B,B); rows=pl.ds(r0,B)
        posf,qf,kf=tables(starts,parents,r0,B,nseg,T)
        co,si=rot_tables(posf)
        cos_o[rows,:]=co; sin_o[rows,:]=si
        qf_s[rows,:]=qf.astype(BF); kf_s[rows,:]=kf.astype(BF)
        return 0
    lb=lanes((B,128)); low=lb<64
    vone=jnp.where((lb>=64)&(lb<67),1.0,0.0)
    def proj(xr,base):
        def f(c,_):
            rows=pl.ds(pl.multiple_of(base+c*B,B),B)
            x=xr[pl.ds(pl.multiple_of(c*B,B),B),:].astype(F32)
            r1=lax.rsqrt(jnp.mean(x*x,axis=1,keepdims=True)+EPS)
            n=(x*r1*gain[...].astype(F32)).astype(BF)
            normed[rows,:]=n
            co=cos_o[rows,:]; si=sin_o[rows,:]; qf=qf_s[rows,:].astype(F32); kf=kf_s[rows,:].astype(F32)
            qq=dot(n,wq[...]); kk=dot(n,wk[...]); vv=dot(n,wv[...])
            for p in range(nh//2):
                cs=slice(128*p,128*p+128)
                q=qq[:,cs]; k=kk[:,cs]; v=vv[:,cs]
                q=(q*co+swap32(q)*si)*C_Q; k=k*co+swap32(k)*si
                for hh in range(2):
                    if hh: q=pltpu.roll(q,64,1); k=pltpu.roll(k,64,1); v=pltpu.roll(v,64,1)
                    qe[2*p+hh,rows,:]=jnp.where(low,q,qf).astype(BF)
                    ke[2*p+hh,rows,:]=jnp.where(low,k,kf).astype(BF)
                    ve[2*p+hh,rows,:]=jnp.where(low,v,vone).astype(BF)
            return 0
        lax.fori_loop(0,R//B,f,0)
    for a in range(2): G.agstart(a)
    lax.fori_loop(0,T//B,tab,0)
    for a in range(2): G.ag(a,0)
    proj(x_ref,mine)
    for t in range(1,4):
        for a in range(2): G.ag(a,t)
    c_x.wait()
    proj(x_peer,theirs)
    for a in range(2,NW): G.agstart(a)
    causal=lax.broadcasted_iota(jnp.int32,(B,B),1)<=lax.broadcasted_iota(jnp.int32,(B,B),0)
    def c_h(p):
        cs=pl.ds(pl.multiple_of(p*128,128),128)
        return pltpu.make_async_remote_copy(heads.at[pl.ds(theirs,R),cs],hrecv.at[:,cs],sems.at[0,1+p],sems.at[1,1+p],device_id=peer,device_id_type=MESH)
    def attend(p,_):
        cs=pl.ds(pl.multiple_of(p*128,128),128)
        for i in range(T//B):
            n=(i+1)*B; rows=slice(i*B,(i+1)*B)
            outs=[]
            for hh in range(2):
                h=2*p+hh
                q=qe[h,rows,:]
                s=dot(q,ke[h,0:n,:],NT)
                sd=jnp.where(causal,s[:,n-B:],BIG)
                s=sd if i==0 else jnp.concatenate([s[:,:n-B],sd],axis=1)
                m=jnp.max(s,axis=1,keepdims=True)
                pr=jnp.exp2(s-m).astype(BF)
                o=dot(pr,ve[h,0:n,:])
                den=o[:,64:65]
                o=o*(1.0/den)
                a,b,c=split3(-(m+jnp.log2(den)))
                qe[h,rows,:]=jnp.where(lb==72,a,jnp.where(lb==73,b,jnp.where(lb==74,c,q.astype(F32)))).astype(BF)
                outs.append(o)
            heads[rows,cs]=jnp.where(low,outs[0],pltpu.roll(outs[1],64,1)).astype(BF)
            if i==3:
                @pl.when(p==0)
                def _():
                    for a in range(2,NW): G.ag(a,0)
                @pl.when(p==1)
                def _():
                    for a in range(2,NW): G.ag(a,2)
        c_h(p).start()
        @pl.when(p==0)
        def _():
            for a in range(2,NW): G.ag(a,1)
        @pl.when(p==1)
        def _():
            for a in range(2,NW): G.ag(a,3)
        return 0
    lax.fori_loop(0,nh//2,attend,0)
    for a in range(NW): G.finish(a)
    for p in range(nh//2): c_h(p).wait()

def front(x,gain,wq,wk,wv,starts,parents,weights,cid):
    R,Dm=x.shape; T=2*R; H=wq.shape[1]; nh=H//HD; nseg=starts.shape[1]; NW=len(weights)
    Vs=pl.BlockSpec(memory_space=pltpu.VMEM); S=pl.BlockSpec(memory_space=pltpu.SMEM); N=pl.BlockSpec(memory_space=pl.ANY)
    sd=jax.ShapeDtypeStruct; hT=sd((nh,T,128),BF)
    return pl.pallas_call(functools.partial(front_kernel,nseg),
        out_shape=(sd((R,Dm),BF),sd((T,Dm),BF),sd((T,H),BF),sd((R,H),BF),hT,hT,hT,sd((T,128),F32),sd((T,128),F32))+tuple(sd(w.shape,BF) for w in weights),
        in_specs=[S,S]+[Vs]*5+[N]*NW, out_specs=(Vs,)*9+(N,)*NW,
        scratch_shapes=[pltpu.VMEM((T,128),BF),pltpu.VMEM((T,128),BF),pltpu.SemaphoreType.DMA((2,1+nh//2)),pltpu.SemaphoreType.DMA((2,NW,18))],
        compiler_params=pltpu.CompilerParams(collective_id=cid,has_side_effects=True,vmem_limit_bytes=67043328),
        name="attention_forward")(starts,parents,x,gain.reshape(1,-1),wq,wk,wv,*weights)

class Ring:
    def __init__(self, shapes, kinds, count, gslots, swaps):
        self.shapes,self.count,self.gslots,self.swaps=shapes,count,gslots,swaps
        self.na=len(shapes); self.flows=[]
        for a,parts in enumerate(kinds):
            for c0,nc,k in parts:
                self.flows+=[(a,c0,nc,0,4-k),(a,c0,nc,1,3+k)]
        self.nf=len(self.flows)
        self.own=[s[0] for s in swaps] if swaps else list(range(count))
        self.nv=len(self.own)
        na,nf=self.na,self.nf
        self.k_rs=na; self.k_x=0; self.k_ag=na; self.k_fc=self.k_ag+4*nf; self.k_fo=self.k_fc+4*nf; self.k_put=self.k_fo+na
        self.n1=na+4*nf; self.n2=self.k_put+na
    def scratch(self):
        V=pltpu.VMEM; U=self.count
        s=[V((self.gslots,2,RING)+x,BF) for x in self.shapes]
        s+=[V((U,RING)+x,BF) for x in self.shapes]
        s+=[V((U,)+x,BF) for x in self.shapes]
        s+=[V((self.nv,)+x,BF) for x in self.shapes] if self.swaps else []
        s+=[V((U,h,self.shapes[a][0],nc),BF) for a,c0,nc,d,h in self.flows]
        return s+[pltpu.SemaphoreType.DMA((2,U,self.n1)),pltpu.SemaphoreType.DMA((2,self.nv,self.n2))]
    def bind(self,p,dst,sc):
        self.p,self.dst=p,dst
        sc=list(sc); na=self.na
        self.g=sc[:na]; self.r=sc[na:2*na]; self.fin=sc[2*na:3*na]; sc=sc[3*na:]
        if self.swaps: self.xr=sc[:na]; sc=sc[na:]
        self.arr=sc[:self.nf]; self.sem,self.sem2=sc[self.nf:]
        return self
    def at(self,d,dist):
        return lax.rem(self.p.pos+(dist if d==0 else RING-dist),RING)
    def cp(self,src,dst,u,k,dev):
        return pltpu.make_async_remote_copy(src,dst,self.sem.at[0,u,k],self.sem.at[1,u,k],device_id=dev,device_id_type=MESH)
    def cp2(self,src,dst,v,k,dev):
        return pltpu.make_async_remote_copy(src,dst,self.sem2.at[0,v,k],self.sem2.at[1,v,k],device_id=dev,device_id_type=MESH)
    def c1(self,u,a): return self.cp(self.g[a].at[lax.rem(u,self.gslots),1-self.p.core],self.r[a].at[u],u,a,{"core":1-self.p.core})
    def start(self,u):
        for a in range(self.na): self.c1(u,a).start()
    def crs(self,u,f,t):
        a,c0,nc,d,h=self.flows[f]
        src=self.r[a].at[u,self.at(d,h),:,pl.ds(c0,nc)] if t==0 else self.arr[f].at[u,t-1]
        return self.cp(src,self.arr[f].at[u,t],u,self.k_rs+4*f+t,{"chip":self.p.nxt[d]})
    def first(self,u):
        for a in range(self.na):
            self.c1(u,a).wait()
            r,g=self.r[a],self.g[a]
            def add(s,_):
                r[u,s]=(r[u,s].astype(F32)+g[lax.rem(u,self.gslots),self.p.core,s].astype(F32)).astype(BF); return 0
            lax.fori_loop(0,RING,add,0)
            for f in range(self.nf):
                if self.flows[f][0]==a: self.crs(u,f,0).start()
    def rs(self,u,t):
        for f,(a,c0,nc,d,h) in enumerate(self.flows):
            if t<h:
                self.crs(u,f,t).wait()
                if t+1<h:
                    self.arr[f][u,t]=(self.arr[f][u,t].astype(F32)+self.r[a][u,self.at(d,h-t-1),:,pl.ds(c0,nc)].astype(F32)).astype(BF)
                    self.crs(u,f,t+1).start()
        if t==3:
            for f in range(0,self.nf,2):
                a,c0,nc,d,h=self.flows[f]; h2=self.flows[f+1][4]
                v=self.r[a][u,self.p.pos,:,pl.ds(c0,nc)].astype(F32)+self.arr[f][u,h-1].astype(F32)+self.arr[f+1][u,h2-1].astype(F32)
                self.fin[a][u,:,pl.ds(c0,nc)]=v.astype(BF)
    def cx(self,v,a): return self.cp2(self.fin[a].at[self.swaps[v][1]],self.xr[a].at[v],v,self.k_x+a,{"mp":1-self.p.mp})
    def xstart(self,v):
        for a in range(self.na): self.cx(v,a).start()
    def uown(self,v): return self.own[v] if self.swaps else v
    def cag(self,v,f,t):
        a,c0,nc,d,h=self.flows[f]
        dst=self.dst(v,a,self.at(1-d,t)).at[:,pl.ds(c0,nc)]
        src=self.fin[a].at[self.uown(v),:,pl.ds(c0,nc)] if t==0 else dst
        return self.cp2(src,dst,v,self.k_ag+4*f+t,{"chip":self.p.nxt[d]})
    def cfc(self,v,f,t):
        a,c0,nc,d,h=self.flows[f]
        ref=self.dst(v,a,self.at(1-d,t+1)).at[:,pl.ds(c0,nc)]
        return self.cp2(ref,ref,v,self.k_fc+4*f+t,{"core":1-self.p.core})
    def cfo(self,v,a): return self.cp2(self.fin[a].at[self.uown(v)],self.dst(v,a,self.p.pos),v,self.k_fo+a,{"core":1-self.p.core})
    def put(self,v,a): return pltpu.make_async_copy(self.fin[a].at[self.uown(v)],self.dst(v,a,self.p.pos),self.sem2.at[0,v,self.k_put+a])
    def agstart(self,v):
        for a in range(self.na):
            if self.swaps:
                u=self.uown(v)
                self.cx(v,a).wait()
                self.fin[a][u]=(self.fin[a][u].astype(F32)+self.xr[a][v].astype(F32)).astype(BF)
            for f in range(self.nf):
                if self.flows[f][0]==a: self.cag(v,f,0).start()
            self.cfo(v,a).start(); self.put(v,a).start()
    def ag(self,v,t):
        for f,(a,c0,nc,d,h) in enumerate(self.flows):
            if t<h:
                self.cag(v,f,t).wait()
                if t+1<h: self.cag(v,f,t+1).start()
                self.cfc(v,f,t).start()
    def finish(self,v):
        for a in range(self.na):
            self.put(v,a).wait(); self.cfo(v,a).wait()
        for f,(a,c0,nc,d,h) in enumerate(self.flows):
            for t in range(h): self.cfc(v,f,t).wait()

RING_M=Ring([(48,512),(48,512),(32,768)],[[(0,512,0)],[(0,512,1)],[(0,384,0),(384,384,1)]],4,2,[(2,0),(3,1)])
RING_O=Ring([(48,384)],[[(0,256,0),(256,128,1)]],2,2,[(1,0)])
RING_C=Ring([(48,128)]*3,[[(0,128,0)],[(0,128,1)],[(0,128,0)]],3,3,[])
def main_kernel(nM,nO,nC,*refs):
    refs=list(refs)
    def take(n):
        r=refs[:n]; del refs[:n]; return r
    x_ref,og,heads,hrecv,wo,wop,gain_a,gain_m=take(8)
    wg_h,wu_h,wd_h,wgp_h,wup_h,wdp_h,qe_h,ke_h,ve_h,co_h,si_h,norm_h,xp_h,wq_h,wk_h,wv_h=take(16)
    out_h,ig_h=take(2); outM=take(3); outO=take(1); outC=take(3); gains_out,=take(1)
    scM=take(nM); scO=take(nO); scC=take(nC)
    dhs,dh,res,snd,rcv,gx,gring,sems,lsem,wsem=take(10)
    at=Place(); mp=at.mp
    R,Dm=x_ref.shape; T=2*R; nh=qe_h.shape[0]; B=256; nb=T//B; H=wo.shape[0]; F=512
    core=at.core
    def dst_m(v,a,ch):
        if a<2: return outM[a].at[core,ch,:,pl.ds(pl.multiple_of(v*F,F),F)]
        return outM[2].at[v,core,ch]
    def dst_c(v,a,ch): return outC[a].at[core,ch,:,pl.ds(pl.multiple_of(v*128,128),128)]
    M=RING_M.bind(at,dst_m,scM); O=RING_O.bind(at,lambda v,a,ch: outO[0].at[core,ch],scO); C=RING_C.bind(at,dst_c,scC)
    mine=pl.multiple_of(mp*R,R); theirs=pl.multiple_of((1-mp)*R,R)
    W=R//3
    def blk(i): return pl.ds(i*W,W)
    at.barrier()
    c_dh=copy_to(dhs,dh.at[pl.ds(mine,R)],sems,0,{"mp":1-mp})

    def mlp(n2,n2t,acc,dn2,hid,dg,du,wgb,wub,wdb):
        def loads(g,u,d,q,slot):
            cs=pl.ds(pl.multiple_of(q*F,F),F)
            return [pltpu.make_async_copy(g.at[:,cs],wgb.at[slot],wsem.at[slot,0]),
                    pltpu.make_async_copy(u.at[:,cs],wub.at[slot],wsem.at[slot,1]),
                    pltpu.make_async_copy(d.at[cs,:],wdb.at[slot],wsem.at[slot,2])]
        for q in loads(wgp_h,wup_h,wdp_h,0,0): q.start()
        def pre(i,_):
            rows=pl.ds(pl.multiple_of(i*W,W),W); mr=pl.ds(pl.multiple_of(mine+i*W,W),W)
            r=x_ref[rows,:].astype(F32)+dot(heads[mr,:],wo[...])+dot(hrecv[rows,:],wop[...])
            res[rows,:]=r
            n=(r*lax.rsqrt(jnp.mean(r*r,axis=1,keepdims=True)+EPS)*gain_m[...].astype(F32)).astype(BF)
            n2[rows,:]=n
            n2t[:,rows]=n.T
            return 0
        lax.fori_loop(0,3,pre,0)
        acc[...]=jnp.zeros_like(acc); dn2[...]=jnp.zeros_like(dn2)
        def step(c,_):
            slot=lax.rem(c,2)
            for q in loads(wg_h,wu_h,wd_h,0,slot): q.wait()
            @pl.when(c==0)
            def _():
                for q in loads(wgp_h,wup_h,wdp_h,1,1): q.start()
            @pl.when((c>0)&(c<3))
            def _():
                for q in loads(wg_h,wu_h,wd_h,c-1,1-slot): q.start()
            wg,wu,wd=wgb[slot],wub[slot],wdb[slot]
            def half(i,_):
                rows=pl.ds(pl.multiple_of(i*W,W),W)
                gate=dot(n2[rows,:],wgb[slot]); up=dot(n2[rows,:],wub[slot]); dhid=dot(og[rows,:],wdb[slot],NT)
                sg=1.0/(1.0+jnp.exp(-gate)); silu=gate*sg
                hid[rows,:]=(silu*up).astype(BF)
                dg[rows,:]=(dhid*up*sg*(1.0+gate*(1.0-sg))).astype(BF)
                du[rows,:]=(dhid*silu).astype(BF)
                return 0
            lax.fori_loop(0,3,half,0)
            @pl.when(c>=1)
            def _(): M.first(c-1)
            acc[...]+=dot(hid[...],wdb[slot])
            @pl.when(c>=2)
            def _(): M.rs(c-2,2)
            dn2[...]+=dot(dg[...],wgb[slot],NT)
            @pl.when(c>=1)
            def _(): M.rs(c-1,0)
            dn2[...]+=dot(du[...],wub[slot],NT)
            @pl.when(c>=2)
            def _(): M.rs(c-2,3)
            M.g[0][slot]=dot(n2t[...],dg[...]).reshape(2,RING,48,F).astype(BF)
            M.g[1][slot]=dot(n2t[...],du[...]).reshape(2,RING,48,F).astype(BF)
            @pl.when(c>=1)
            def _(): M.rs(c-1,1)
            M.g[2][slot]=dot(hid[...].T,og[...]).reshape(2,RING,32,Dm).astype(BF)
            M.start(c)
            return 0
        lax.fori_loop(0,4,step,0)
        gpart=jnp.zeros((1,Dm),F32)
        for i in range(3):
            rows=blk(i)
            r=res[rows,:]; d=dn2[rows,:]
            acc[rows,:]=acc[rows,:]+r
            i2=lax.rsqrt(jnp.mean(r*r,axis=1,keepdims=True)+EPS)
            gpart=gpart+jnp.sum(d*r*i2,axis=0,keepdims=True)
            s=gain_m[...].astype(F32)*d
            dr=og[rows,:].astype(F32)+i2*s-r*(i2*i2*i2)*jnp.mean(s*r,axis=1,keepdims=True)
            res[rows,:]=dr
            da=dr.astype(BF)
            n2[rows,:]=da
            n2t[:,rows]=da.T
            dhs[rows,:]=dot(da,wop[...],NT).astype(BF)
        c_dh.start()
        c_out=pltpu.make_async_copy(acc,out_h,lsem.at[10]); c_out.start()
        gx[0,1:2]=gpart
        M.xstart(0); M.xstart(1)
        M.rs(2,2)
        def own(i,_):
            rows=pl.ds(pl.multiple_of(i*W,W),W)
            dh[pl.ds(pl.multiple_of(mine+i*W,W),W),:]=dot(n2[rows,:],wo[...],NT).astype(BF)
            return 0
        lax.fori_loop(0,3,own,0)
        M.first(3)
        O.g[0][0]=dot(n2t[...],hrecv[...]).reshape(2,RING,48,H).astype(BF)
        O.start(0)
        O.g[0][1]=dot(n2t[...],heads[pl.ds(mine,R),:]).reshape(2,RING,48,H).astype(BF)
        O.start(1)
        M.rs(2,3); M.rs(3,0)
        c_out.wait()
    V=pltpu.VMEM
    pl.run_scoped(mlp,V((R,Dm),BF),V((Dm,R),BF),V((R,Dm),F32),V((R,Dm),F32),V((R,F),BF),V((R,F),BF),V((R,F),BF),
                  V((2,Dm,F),BF),V((2,Dm,F),BF),V((2,F,Dm),BF))

    def attn(qe,ke,ve,cos_o,sin_o,nrm,x_p,wc,nt,doe,kt,dqt,ds_s,dn):
        ld=[pltpu.make_async_copy(s,d,lsem.at[i]) for i,(s,d) in enumerate(((norm_h,nrm),(ke_h,ke),(qe_h,qe),(ve_h,ve),(co_h,cos_o),(si_h,sin_o),(xp_h,x_p)))]
        ld+=[pltpu.make_async_copy(s.at[:,pl.ds(128*q,128)],wc.at[q,:,pl.ds(128*i,128)],lsem.at[12+3*q+i]) for q in range(nh//2) for i,s in enumerate((wq_h,wk_h,wv_h))]
        for q in ld: q.start()
        M.agstart(0); O.first(0); O.first(1)
        ld[0].wait()
        def tr(i,_):
            c=pl.ds(pl.multiple_of(i*B,B),B)
            nt[:,c]=nrm[c,:].T
            return 0
        lax.fori_loop(0,nb,tr,0)
        M.rs(3,1); M.ag(0,0); O.rs(0,0); O.rs(1,0)
        for q in ld[1:]: q.wait()
        c_dh.wait()
        l=lanes((B,128)); low=l<64
        causal=lax.broadcasted_iota(jnp.int32,(B,B),0)<=lax.broadcasted_iota(jnp.int32,(B,B),1)
        def pair(p,_):
            cols=pl.ds(pl.multiple_of(p*128,128),128)
            for i in range(nb):
                rows=slice(i*B,(i+1)*B)
                d=dh[rows,cols].astype(F32); o=heads[rows,cols].astype(F32)
                t=d*o
                for hh in range(2):
                    if hh: t=pltpu.roll(t,64,1); d=pltpu.roll(d,64,1)
                    delta=jnp.sum(jnp.where(low,t,0.0),axis=1,keepdims=True)
                    a,b,c=split3(-delta)
                    doe[hh,rows,:]=jnp.where(low,d,jnp.where(l==64,a,jnp.where(l==65,b,jnp.where(l==66,c,0.0)))).astype(BF)
                    kt[hh,:,rows]=ke[2*p+hh,rows,:].T[0:64]
            dqt[...]=jnp.zeros_like(dqt)
            @pl.when(p==0)
            def _(): M.rs(3,2)
            @pl.when(p>0)
            def _(): C.first(p-1)
            for j in range(nb):
                ks=slice(j*B,(j+1)*B); n0=j*B
                outs=[]
                for hh in range(2):
                    h=2*p+hh
                    s=dot(ke[h,ks,:],qe[h,n0:,:],NT)
                    dp=dot(ve[h,ks,:],doe[hh,n0:,:],NT)
                    sd=jnp.where(causal,s[:,:B],BIG)
                    s=sd if j==nb-1 else jnp.concatenate([sd,s[:,B:]],axis=1)
                    pt=jnp.exp2(s)
                    ds=(pt*dp).astype(BF)
                    pt=pt.astype(BF)
                    dv=dot(pt,doe[hh,n0:,:])
                    dk=dot(ds,qe[h,n0:,:])*LN2
                    dqt[64*hh:64*hh+64,n0:]+=dot(kt[hh,:,ks],ds)
                    outs.append((dk,dv))
                dk=jnp.where(low,outs[0][0],pltpu.roll(outs[1][0],64,1))
                dv=jnp.where(low,outs[0][1],pltpu.roll(outs[1][1],64,1))
                co=cos_o[ks,:]; si=sin_o[ks,:]
                ds_s[p,ks,128:256]=(dk*co-swap32(dk)*si).astype(BF)
                ds_s[p,ks,256:384]=dv.astype(BF)
                if j==0:
                    @pl.when(p==0)
                    def _(): M.ag(0,1); O.rs(0,1); O.rs(1,1)
                    @pl.when(p==1)
                    def _(): M.ag(1,0); C.rs(0,0)
                    @pl.when(p==2)
                    def _(): M.ag(1,3); C.rs(1,0)
                if j==1:
                    @pl.when(p==0)
                    def _(): M.rs(3,3); M.agstart(1)
                    @pl.when(p==1)
                    def _(): M.ag(1,1); O.rs(0,3); O.rs(1,3); O.xstart(0)
                    @pl.when(p==2)
                    def _(): O.ag(0,0); C.rs(0,3); C.agstart(0)
                if j==3:
                    @pl.when(p==0)
                    def _(): M.ag(0,2); O.rs(0,2); O.rs(1,2)
                    @pl.when(p==1)
                    def _(): C.rs(0,1); O.agstart(0)
                    @pl.when(p==2)
                    def _(): C.rs(1,1); O.ag(0,1)
            for i in range(nb):
                rows=slice(i*B,(i+1)*B)
                dq=dqt[:,rows].T*(HD**-0.5)
                co=cos_o[rows,:]; si=sin_o[rows,:]
                ds_s[p,rows,0:128]=(dq*co-swap32(dq)*si).astype(BF)
            for c in range(2):
                v=dot(nt[c*(Dm//2):(c+1)*(Dm//2),:],ds_s[p])
                for i in range(3): C.g[i][p,c]=v[:,128*i:128*i+128].reshape(RING,Dm//16,128).astype(BF)
            C.start(p)
            @pl.when(p==0)
            def _(): M.ag(0,3)
            @pl.when(p==1)
            def _(): M.ag(1,2); C.rs(0,2)
            return 0
        lax.fori_loop(0,nh//2,pair,0)
        C.ag(0,0); C.rs(1,2); O.ag(0,2)
        def c_dn(c): return copy_to(snd.at[blk(c)],rcv.at[blk(c)],sems,2+c,{"mp":1-mp})
        def part(r0,xr,c):
            rows=pl.ds(pl.multiple_of(r0,W),W)
            v=dot(ds_s[0,rows,:],wc[0],NT)+dot(ds_s[1,rows,:],wc[1],NT)+dot(ds_s[2,rows,:],wc[2],NT)
            x=xr[blk(c)].astype(F32)
            xr=x*lax.rsqrt(jnp.mean(x*x,axis=1,keepdims=True)+EPS)
            return v, jnp.sum(v*xr,axis=0,keepdims=True)
        gsum=jnp.zeros((1,Dm),F32)
        for c in range(3):
            v,gs=part(theirs+c*W,x_p,c); gsum=gsum+gs
            snd[blk(c)]=v.astype(BF); c_dn(c).start()
            if c==0: C.first(2)
            if c==1: C.rs(1,3); C.agstart(1)
            if c==2: C.rs(2,0); C.ag(0,1)
        for c in range(3):
            v,gs=part(mine+c*W,x_ref,c); gsum=gsum+gs
            dn[blk(c)]=v
            if c==1: C.rs(2,1); C.ag(1,0); O.ag(0,3)
        gx[0,0:1]=gsum
        c_gx=copy_to(gx.at[0],gx.at[1],sems,5,{"mp":1-mp}); c_gx.start()
        C.rs(2,2); C.ag(0,2)
        c_gx.wait(); gx[2]=gx[0]+gx[1]
        c_gc=copy_to(gx.at[2],gx.at[3],sems,6,{"core":1-at.core}); c_gc.start()
        C.ag(1,1); C.rs(2,3); C.agstart(2)
        c_gc.wait(); gring[0]=gx[2]+gx[3]
        def c_gr(d,t): return copy_to(gring.at[0 if t==0 else 4*d+t],gring.at[4*d+t+1],sems,7+4*d+t,{"chip":at.nxt[d]})
        c_gr(0,0).start(); c_gr(1,0).start()
        gtot=gring[0]
        for t in range(4):
            for d in range(2):
                if t<4-d:
                    c_gr(d,t).wait()
                    if t+1<4-d: c_gr(d,t+1).start()
                    gtot=gtot+gring[4*d+t+1]
            C.ag(2,t)
            if t==0: C.ag(0,3); C.ag(1,2)
            if t==1: C.ag(1,3)
        gains_out[...]=gtot
        for c in range(3):
            c_dn(c).wait()
            r=blk(c)
            d=dn[r]+rcv[r].astype(F32)
            x=x_ref[r].astype(F32)
            i1=lax.rsqrt(jnp.mean(x*x,axis=1,keepdims=True)+EPS)
            s=gain_a[...].astype(F32)*d
            res[r]=res[r]+i1*s-x*(i1*i1*i1)*jnp.mean(s*x,axis=1,keepdims=True)
        c_ig=pltpu.make_async_copy(res,ig_h,lsem.at[11]); c_ig.start()
        M.finish(0); M.finish(1); O.finish(0)
        for v in range(3): C.finish(v)
        c_ig.wait()
    hT=V((nh,T,128),BF)
    pl.run_scoped(attn,hT,hT,hT,V((T,128),F32),V((T,128),F32),V((T,Dm),BF),V((R,Dm),BF),V((nh//2,Dm,H),BF),
                  V((Dm,T),BF),V((2,T,128),BF),V((2,64,T),BF),V((128,T),F32),V((nh//2,T,H),BF),V((R,Dm),F32))

def main_call(x,og,heads,hrecv,wo,wop,gain_a,gain_m,hbm,cid):
    R,Dm=x.shape; T,H=heads.shape
    Vs=pl.BlockSpec(memory_space=pltpu.VMEM); N=pl.BlockSpec(memory_space=pl.ANY); sd=jax.ShapeDtypeStruct; V=pltpu.VMEM
    scs=[s.scratch() for s in (RING_M,RING_O,RING_C)]
    local=[V((R,H),BF),V((T,H),BF),V((R,Dm),F32)]+[V((R,Dm),BF)]*2
    local+=[V((4,8,Dm),F32),V((RING,8,Dm),F32),pltpu.SemaphoreType.DMA((2,7+RING)),pltpu.SemaphoreType.DMA((21,)),pltpu.SemaphoreType.DMA((2,3))]
    outs=[sd((R,Dm),F32)]*2+[sd((2,RING,48,1024),BF)]*2+[sd((2,2,RING,32,Dm),BF)]+[sd((2,RING,48,H),BF)]*4+[sd((8,Dm),F32)]
    return pl.pallas_call(functools.partial(main_kernel,*[len(s) for s in scs]),
        out_shape=tuple(outs), in_specs=[Vs]*8+[N]*len(hbm), out_specs=(N,)*9+(Vs,),
        scratch_shapes=scs[0]+scs[1]+scs[2]+local,
        compiler_params=pltpu.CompilerParams(collective_id=cid,has_side_effects=True,vmem_limit_bytes=67043328),
        name="mlp_and_backward")(x,og,heads,hrecv,wo,wop,gain_a.reshape(1,-1),gain_m.reshape(1,-1),*hbm)

def on_device(layer_input, gain_attn, w_query, w_key, w_value, w_out, gain_mlp, w_gate, w_up, w_down,
              segment_start, segment_parent, out_grad):
    weights = (w_out, w_gate, w_up, w_down)
    x_peer, normed, heads, heads_peer, qe, ke, ve, cosine, sine, peer_out, peer_gate, peer_up, peer_down = front(
        layer_input, gain_attn, w_query, w_key, w_value, segment_start, segment_parent, weights, 2
    )
    (output, input_grad, gate_g, up_g, down_g, out_g, query_g, key_g, value_g, gains) = main_call(
        layer_input, out_grad, heads, heads_peer, w_out, peer_out, gain_attn, gain_mlp,
        (w_gate, w_up, w_down, peer_gate, peer_up, peer_down, qe, ke, ve, cosine, sine, normed, x_peer,
         w_query, w_key, w_value), 1,
    )
    sums = [g.reshape(-1, g.shape[-1]) for g in (query_g, key_g, value_g, out_g, gate_g, up_g, down_g)]
    sums += [gains[0], gains[1]]
    if lax.axis_size("grp") > 1:
        sums = lax.psum([s.astype(F32) for s in sums], "grp")
    query_g, key_g, value_g, out_g, gate_g, up_g, down_g, gain_attn_grad, gain_mlp_grad = [s.astype(F32) for s in sums]
    return (
        output, input_grad, gain_attn_grad, query_g, key_g, value_g, out_g.T, gain_mlp_grad, gate_g, up_g, down_g,
    )


def solution(mesh):
    fine = Mesh(mesh.devices.reshape(-1, RING, 2, mesh.shape["mp"]), ("grp", "chip", "core", "mp"))
    dp = ("grp", "chip", "core")
    tok, col, row, tree = P(dp + ("mp",), None), P(None, "mp"), P("mp", None), P(dp, None)
    in_specs = (tok, P(), col, col, col, row, P(), col, col, row, tree, tree, tok)
    out_specs = (tok, tok, P(), col, col, col, row, P(), col, col, row)
    return jax.shard_map(on_device, mesh=fine, in_specs=in_specs, out_specs=out_specs, check_vma=False)
```

```python
import functools
import math

import jax
import jax.numpy as jnp
from jax import lax
from jax.experimental import pallas as pl
from jax.experimental.pallas import tpu as pltpu
from jax.sharding import Mesh
from jax.sharding import PartitionSpec as P

BF = jnp.bfloat16
F32 = jnp.float32
HD=64; EPS=1e-5; BIG=-1e30
C_Q = (HD**-0.5)*math.log2(math.e)
LN2 = math.log(2.0)
NT=(((1,),(1,)),((),())); NN=(((1,),(0,)),((),())); TN=(((0,),(0,)),((),()))
def dot(a,b,dims=NN): return lax.dot_general(a,b,dims,preferred_element_type=F32)
def lanes(shape): return lax.broadcasted_iota(jnp.int32, shape, 1)

def split3(x):
    hi=x.astype(BF).astype(F32); r=x-hi; mid=r.astype(BF).astype(F32); lo=r-mid
    return hi,mid,lo

def tables(starts, parents, row0, rows, nseg, tree_len):
    sh=(rows,128)
    t = row0 + lax.broadcasted_iota(jnp.int32, sh, 0)
    st=[starts[0,s] for s in range(nseg)]+[tree_len]
    par=[parents[0,s] for s in range(nseg)]
    ln=[st[s+1]-st[s] for s in range(nseg)]
    def pick(vals, idx):
        r = vals[0]
        for s in range(1,nseg): r = jnp.where(idx==s, vals[s], r)
        return r
    D=[]
    gps=[]
    for s in range(nseg):
        p=par[s]; gp=pick(par,p); gps.append(gp)
        off=jnp.where(p!=s, pick(ln,p), 0)+jnp.where((gp!=s)&(gp!=p), pick(ln,gp), 0)
        D.append(off-st[s])
    seg=jnp.zeros(sh,jnp.int32); pos=t+D[0]
    for s in range(1,nseg):
        ge=t>=st[s]
        seg=seg+ge.astype(jnp.int32)
        pos=pos+jnp.where(ge, D[s]-D[s-1], 0)
    f=lanes(sh)-64
    parl=jnp.zeros((1,128),jnp.int32)-1; gpl=parl
    fl=lanes((1,128))-64
    for s in range(nseg):
        parl=jnp.where(fl==s, par[s], parl); gpl=jnp.where(fl==s, gps[s], gpl)
    vis=(f==seg)|(parl==seg)|(gpl==seg)|(f<0)|(f>=nseg)
    qf=jnp.where(f==seg,1.0,0.0)
    kf=jnp.where(vis,0.0,BIG)
    kf=jnp.where((f>=8)&(f<11),1.0,kf)
    return pos.astype(F32), qf, kf

def rot_tables(posf):
    l=lax.broadcasted_iota(jnp.int32,(1,128),1)
    fr=jnp.exp((l%32).astype(F32)*(-2.0*math.log(10000.0)/HD))
    ang=posf*fr
    sg=jnp.where((l%64)<32,-1.0,1.0)
    return jnp.cos(ang), jnp.sin(ang)*sg

def swap32(x):
    l=lanes(x.shape)
    return jnp.where((l&32)==0, pltpu.roll(x,96,1), pltpu.roll(x,32,1))


MESH=pl.DeviceIdType.MESH
RING=8
def ring_chip(r):
    return jnp.where(r<RING//2, 2*r, 2*(RING-1-r)+1)
def chip_ring(n):
    return jnp.where(n%2==0, n//2, RING-1-n//2)

class Place:
    def __init__(self):
        self.core=lax.axis_index("core"); self.mp=lax.axis_index("mp")
        self.pos=chip_ring(lax.axis_index("chip"))
        self.nxt=[ring_chip(lax.rem(self.pos+1,RING)), ring_chip(lax.rem(self.pos+RING-1,RING))]
    def barrier(self):
        b=pltpu.get_barrier_semaphore()
        ds=[{"core":1-self.core},{"mp":1-self.mp},{"chip":self.nxt[0]},{"chip":self.nxt[1]}]
        for d in ds: pl.semaphore_signal(b, inc=1, device_id=d, device_id_type=MESH)
        pl.semaphore_wait(b, len(ds))

def copy_to(src,dst,sems,k,dev):
    return pltpu.make_async_remote_copy(src,dst,sems.at[0,k],sems.at[1,k],device_id=dev,device_id_type=MESH)

class Gather:
    def __init__(self,p,src,out,kinds,sems):
        self.p,self.src,self.out,self.kinds,self.sems=p,src,out,kinds,sems
    def ref(self,x,a,ch,core=None):
        n=self.out[a].shape[0]//(2*RING)
        return x[a].at[pl.ds(pl.multiple_of((self.p.core*RING+ch)*n,n),n)]
    def at(self,d,dist): return lax.rem(self.p.pos+(dist if d==0 else RING-dist),RING)
    def hops(self,a,d): return 4-self.kinds[a] if d==0 else 3+self.kinds[a]
    def cp(self,src,dst,a,k,dev):
        return pltpu.make_async_remote_copy(src,dst,self.sems.at[0,a,k],self.sems.at[1,a,k],device_id=dev,device_id_type=MESH)
    def cx(self,a): return self.cp(self.ref(self.src,a,self.p.pos),self.ref(self.out,a,self.p.pos),a,0,{"mp":1-self.p.mp})
    def cag(self,a,d,t):
        r=self.ref(self.out,a,self.at(1-d,t))
        return self.cp(r,r,a,1+4*d+t,{"chip":self.p.nxt[d]})
    def cfc(self,a,d,t):
        r=self.ref(self.out,a,self.at(1-d,t+1))
        return self.cp(r,r,a,9+4*d+t,{"core":1-self.p.core})
    def cfo(self,a):
        r=self.ref(self.out,a,self.p.pos)
        return self.cp(r,r,a,17,{"core":1-self.p.core})
    def agstart(self,a):
        self.cx(a).wait()
        for d in range(2): self.cag(a,d,0).start()
        self.cfo(a).start()
    def ag(self,a,t):
        for d in range(2):
            if t<self.hops(a,d):
                self.cag(a,d,t).wait()
                if t+1<self.hops(a,d): self.cag(a,d,t+1).start()
                self.cfc(a,d,t).start()
    def finish(self,a):
        self.cfo(a).wait()
        for d in range(2):
            for t in range(self.hops(a,d)): self.cfc(a,d,t).wait()

def front_kernel(nseg,starts,parents,x_ref,gain,wq,wk,wv,*refs):
    refs=list(refs)
    def take(n):
        r=refs[:n]; del refs[:n]; return r
    NW=(len(refs)-13)//2
    src=take(NW)
    x_peer,normed,heads,hrecv,qe,ke,ve,cos_o,sin_o=take(9); out=take(NW)
    qf_s,kf_s,sems,wsems=take(4)
    at=Place(); mp=at.mp
    R=x_ref.shape[0]; T=2*R; B=256; nh=wq.shape[1]//HD
    G=Gather(at,src,out,[a%2 for a in range(NW)],wsems)
    mine=pl.multiple_of(mp*R,R); theirs=pl.multiple_of((1-mp)*R,R)
    at.barrier()
    peer={"mp":1-mp}
    NG=3
    for a in range(NG): G.cx(a).start()
    c_x=copy_to(x_ref,x_peer,sems,0,peer); c_x.start()
    for a in range(NG,NW): G.cx(a).start()
    def tab(c,_):
        r0=pl.multiple_of(c*B,B); rows=pl.ds(r0,B)
        posf,qf,kf=tables(starts,parents,r0,B,nseg,T)
        co,si=rot_tables(posf)
        cos_o[rows,:]=co; sin_o[rows,:]=si
        qf_s[rows,:]=qf.astype(BF); kf_s[rows,:]=kf.astype(BF)
        return 0
    lb=lanes((B,128)); low=lb<64
    vone=jnp.where((lb>=64)&(lb<67),1.0,0.0)
    def proj(xr,base):
        def f(c,_):
            rows=pl.ds(pl.multiple_of(base+c*B,B),B)
            x=xr[pl.ds(pl.multiple_of(c*B,B),B),:].astype(F32)
            r1=lax.rsqrt(jnp.mean(x*x,axis=1,keepdims=True)+EPS)
            n=(x*r1*gain[...].astype(F32)).astype(BF)
            normed[rows,:]=n
            co=cos_o[rows,:]; si=sin_o[rows,:]; qf=qf_s[rows,:].astype(F32); kf=kf_s[rows,:].astype(F32)
            qq=dot(n,wq[...]); kk=dot(n,wk[...]); vv=dot(n,wv[...])
            for p in range(nh//2):
                cs=slice(128*p,128*p+128)
                q=qq[:,cs]; k=kk[:,cs]; v=vv[:,cs]
                q=(q*co+swap32(q)*si)*C_Q; k=k*co+swap32(k)*si
                for hh in range(2):
                    if hh: q=pltpu.roll(q,64,1); k=pltpu.roll(k,64,1); v=pltpu.roll(v,64,1)
                    qe[2*p+hh,rows,:]=jnp.where(low,q,qf).astype(BF)
                    ke[2*p+hh,rows,:]=jnp.where(low,k,kf).astype(BF)
                    ve[2*p+hh,rows,:]=jnp.where(low,v,vone).astype(BF)
            return 0
        lax.fori_loop(0,R//B,f,0)
    for a in range(NG): G.agstart(a)
    lax.fori_loop(0,T//B,tab,0)
    for a in range(NG): G.ag(a,0)
    proj(x_ref,mine)
    for a in range(NG): G.ag(a,1)
    c_x.wait()
    proj(x_peer,theirs)
    for a in range(NG): G.ag(a,2)
    for a in range(NG,NW): G.agstart(a)
    causal=lax.broadcasted_iota(jnp.int32,(B,B),1)<=lax.broadcasted_iota(jnp.int32,(B,B),0)
    def c_h(p):
        cs=pl.ds(pl.multiple_of(p*128,128),128)
        return pltpu.make_async_remote_copy(heads.at[pl.ds(theirs,R),cs],hrecv.at[:,cs],sems.at[0,1+p],sems.at[1,1+p],device_id=peer,device_id_type=MESH)
    def attend(p,_):
        cs=pl.ds(pl.multiple_of(p*128,128),128)
        for i in range(T//B):
            n=(i+1)*B; rows=slice(i*B,(i+1)*B)
            outs=[]
            for hh in range(2):
                h=2*p+hh
                q=qe[h,rows,:]
                s=dot(q,ke[h,0:n,:],NT)
                sd=jnp.where(causal,s[:,n-B:],BIG)
                s=sd if i==0 else jnp.concatenate([s[:,:n-B],sd],axis=1)
                m=jnp.max(s,axis=1,keepdims=True)
                pr=jnp.exp2(s-m).astype(BF)
                o=dot(pr,ve[h,0:n,:])
                den=o[:,64:65]
                o=o*(1.0/den)
                a,b,c=split3(-(m+jnp.log2(den)))
                qe[h,rows,:]=jnp.where(lb==72,a,jnp.where(lb==73,b,jnp.where(lb==74,c,q.astype(F32)))).astype(BF)
                outs.append(o)
            heads[rows,cs]=jnp.where(low,outs[0],pltpu.roll(outs[1],64,1)).astype(BF)
            if i==3:
                @pl.when(p==0)
                def _():
                    for a in range(NG): G.ag(a,3)
                @pl.when(p==1)
                def _():
                    for a in range(NG,NW): G.ag(a,1)
                @pl.when(p==2)
                def _():
                    for a in range(NG,NW): G.ag(a,3)
        c_h(p).start()
        @pl.when(p==0)
        def _():
            for a in range(NG,NW): G.ag(a,0)
        @pl.when(p==1)
        def _():
            for a in range(NG,NW): G.ag(a,2)
        return 0
    lax.fori_loop(0,nh//2,attend,0)
    for a in range(NW): G.finish(a)
    for p in range(nh//2): c_h(p).wait()

def front(x,gain,wq,wk,wv,starts,parents,weights,cid):
    R,Dm=x.shape; T=2*R; H=wq.shape[1]; nh=H//HD; nseg=starts.shape[1]; NW=len(weights)
    Vs=pl.BlockSpec(memory_space=pltpu.VMEM); S=pl.BlockSpec(memory_space=pltpu.SMEM); N=pl.BlockSpec(memory_space=pl.ANY)
    sd=jax.ShapeDtypeStruct; hT=sd((nh,T,128),BF)
    return pl.pallas_call(functools.partial(front_kernel,nseg),
        out_shape=(sd((R,Dm),BF),sd((T,Dm),BF),sd((T,H),BF),sd((R,H),BF),hT,hT,hT,sd((T,128),F32),sd((T,128),F32))+tuple(sd(w.shape,BF) for w in weights),
        in_specs=[S,S]+[Vs]*5+[N]*NW, out_specs=(Vs,)*9+(N,)*NW,
        scratch_shapes=[pltpu.VMEM((T,128),BF),pltpu.VMEM((T,128),BF),pltpu.SemaphoreType.DMA((2,1+nh//2)),pltpu.SemaphoreType.DMA((2,NW,18))],
        compiler_params=pltpu.CompilerParams(collective_id=cid,has_side_effects=True,vmem_limit_bytes=67043328),
        name="attention_forward")(starts,parents,x,gain.reshape(1,-1),wq,wk,wv,*weights)

class Ring:
    def __init__(self, shapes, kinds, count, gslots, swaps, early=True, slot=None):
        self.shapes,self.count,self.gslots,self.swaps,self.early=shapes,count,gslots,swaps,early
        self.slot=slot or (lambda u: lax.rem(u,gslots))
        self.nr=(len(swaps) if early else count) if swaps else count
        self.na=len(shapes); self.flows=[]
        for a,parts in enumerate(kinds):
            for c0,nc,k in parts:
                self.flows+=[(a,c0,nc,0,4-k),(a,c0,nc,1,3+k)]
        self.nf=len(self.flows)
        self.own=[s[0] for s in swaps] if swaps else list(range(count))
        self.nv=len(self.own)
        na,nf=self.na,self.nf
        self.k_rs=na; self.k_x=0; self.k_ag=na; self.k_fc=self.k_ag+4*nf; self.k_fo=self.k_fc+4*nf; self.k_put=self.k_fo+na
        self.n1=na+4*nf; self.n2=self.k_put+na
    def scratch(self):
        V=pltpu.VMEM; U=self.count
        s=[V((self.gslots,2,RING)+x,BF) for x in self.shapes] if self.gslots else []
        s+=[V((U,RING)+x,BF) for x in self.shapes]
        s+=[V((self.nr,)+x,BF) for x in self.shapes]
        s+=[V((self.nv,)+((RING,)+x if self.early else x),BF) for x in self.shapes] if self.swaps else []
        s+=[V((self.nr,h,self.shapes[a][0],nc),BF) for a,c0,nc,d,h in self.flows]
        return s+[pltpu.SemaphoreType.DMA((2,U,self.n1)),pltpu.SemaphoreType.DMA((2,self.nv,self.n2))]
    def bind(self,p,dst,sc,g=None):
        self.p,self.dst=p,dst
        sc=list(sc); na=self.na
        if g is None: g,sc=sc[:na],sc[na:]
        self.g=g; self.r=sc[:na]; self.fin=sc[na:2*na]; sc=sc[2*na:]
        if self.swaps: self.xr=sc[:na]; sc=sc[na:]
        self.arr=sc[:self.nf]; self.sem,self.sem2=sc[self.nf:]
        return self
    def at(self,d,dist):
        return lax.rem(self.p.pos+(dist if d==0 else RING-dist),RING)
    def cp(self,src,dst,u,k,dev):
        return pltpu.make_async_remote_copy(src,dst,self.sem.at[0,u,k],self.sem.at[1,u,k],device_id=dev,device_id_type=MESH)
    def cp2(self,src,dst,v,k,dev):
        return pltpu.make_async_remote_copy(src,dst,self.sem2.at[0,v,k],self.sem2.at[1,v,k],device_id=dev,device_id_type=MESH)
    def c1(self,u,a): return self.cp(self.g[a].at[self.slot(u),1-self.p.core],self.r[a].at[u],u,a,{"core":1-self.p.core})
    def start(self,u):
        for a in range(self.na): self.c1(u,a).start()
    def uown(self,v): return self.own[v] if self.swaps else v
    def u_of(self,w): return self.uown(w) if self.early else w
    def w_own(self,v): return v if self.early else self.uown(v)
    def crs(self,w,f,t):
        a,c0,nc,d,h=self.flows[f]
        src=self.r[a].at[self.u_of(w),self.at(d,h),:,pl.ds(c0,nc)] if t==0 else self.arr[f].at[w,t-1]
        return self.cp(src,self.arr[f].at[w,t],self.u_of(w),self.k_rs+4*f+t,{"chip":self.p.nxt[d]})
    def cx(self,v,a): return self.cp2(self.r[a].at[self.swaps[v][1]] if self.early else self.fin[a].at[self.swaps[v][1]],self.xr[a].at[v],v,self.k_x+a,{"mp":1-self.p.mp})
    def push(self,v):
        u=self.swaps[v][1]
        for a in range(self.na):
            self.c1(u,a).wait()
            r,g=self.r[a],self.g[a]
            def add(s,_):
                r[u,s]=r[u,s]+g[self.slot(u),self.p.core,s]; return 0
            lax.fori_loop(0,RING,add,0)
            self.cx(v,a).start()
    def xstart(self,v):
        for a in range(self.na): self.cx(v,a).start()
    def first(self,v):
        u=self.u_of(v)
        for a in range(self.na):
            self.c1(u,a).wait()
            if self.swaps and self.early: self.cx(v,a).wait()
            r,g=self.r[a],self.g[a]
            def add(s,_):
                t=r[u,s].astype(F32)+g[self.slot(u),self.p.core,s].astype(F32)
                if self.swaps and self.early: t=t+self.xr[a][v,s].astype(F32)
                r[u,s]=t.astype(BF); return 0
            lax.fori_loop(0,RING,add,0)
            for f in range(self.nf):
                if self.flows[f][0]==a: self.crs(v,f,0).start()
    def rs(self,v,t):
        u=self.u_of(v)
        for f,(a,c0,nc,d,h) in enumerate(self.flows):
            if t<h:
                self.crs(v,f,t).wait()
                if t+1<h:
                    self.arr[f][v,t]=self.arr[f][v,t]+self.r[a][u,self.at(d,h-t-1),:,pl.ds(c0,nc)]
                    self.crs(v,f,t+1).start()
        if t==3:
            for f in range(0,self.nf,2):
                a,c0,nc,d,h=self.flows[f]; h2=self.flows[f+1][4]
                w=self.r[a][u,self.p.pos,:,pl.ds(c0,nc)].astype(F32)+self.arr[f][v,h-1].astype(F32)+self.arr[f+1][v,h2-1].astype(F32)
                self.fin[a][v,:,pl.ds(c0,nc)]=w.astype(BF)
    def cag(self,v,f,t):
        a,c0,nc,d,h=self.flows[f]
        dst=self.dst(v,a,self.at(1-d,t)).at[:,pl.ds(c0,nc)]
        src=self.fin[a].at[self.w_own(v),:,pl.ds(c0,nc)] if t==0 else dst
        return self.cp2(src,dst,v,self.k_ag+4*f+t,{"chip":self.p.nxt[d]})
    def cfc(self,v,f,t):
        a,c0,nc,d,h=self.flows[f]
        ref=self.dst(v,a,self.at(1-d,t+1)).at[:,pl.ds(c0,nc)]
        return self.cp2(ref,ref,v,self.k_fc+4*f+t,{"core":1-self.p.core})
    def cfo(self,v,a): return self.cp2(self.fin[a].at[self.w_own(v)],self.dst(v,a,self.p.pos),v,self.k_fo+a,{"core":1-self.p.core})
    def put(self,v,a): return pltpu.make_async_copy(self.fin[a].at[self.w_own(v)],self.dst(v,a,self.p.pos),self.sem2.at[0,v,self.k_put+a])
    def agstart(self,v):
        for a in range(self.na):
            if not self.early:
                u=self.uown(v)
                self.cx(v,a).wait()
                self.fin[a][u]=self.fin[a][u]+self.xr[a][v]
            for f in range(self.nf):
                if self.flows[f][0]==a: self.cag(v,f,0).start()
            self.cfo(v,a).start(); self.put(v,a).start()
    def ag(self,v,t):
        for f,(a,c0,nc,d,h) in enumerate(self.flows):
            if t<h:
                self.cag(v,f,t).wait()
                if t+1<h: self.cag(v,f,t+1).start()
                self.cfc(v,f,t).start()
    def finish(self,v):
        for a in range(self.na):
            self.put(v,a).wait(); self.cfo(v,a).wait()
        for f,(a,c0,nc,d,h) in enumerate(self.flows):
            for t in range(h): self.cfc(v,f,t).wait()

SHAPES_M,KINDS_M=[(48,512),(48,512),(32,768)],[[(0,512,0)],[(0,512,1)],[(0,384,0),(384,384,1)]]
RING_M=Ring(SHAPES_M,KINDS_M,2,2,[(1,0)],True,lambda u: 0)
RING_N=Ring(SHAPES_M,KINDS_M,2,0,[(1,0)],False,lambda u: 1)
RING_O=Ring([(48,384)],[[(0,256,0),(256,128,1)]],2,2,[(1,0)])
RING_C=Ring([(48,128)]*3,[[(0,128,0)],[(0,128,1)],[(0,128,0)]],3,3,[])
def main_kernel(nM,nN,nO,nC,*refs):
    refs=list(refs)
    def take(n):
        r=refs[:n]; del refs[:n]; return r
    x_ref,og,heads,hrecv,wo,wop,gain_a,gain_m=take(8)
    wg_h,wu_h,wd_h,wgp_h,wup_h,wdp_h,qe_h,ke_h,ve_h,co_h,si_h,norm_h,xp_h,wq_h,wk_h,wv_h=take(16)
    out_h,ig_h=take(2); outM=take(3); outO=take(1); outC=take(3); gains_out,=take(1)
    scM=take(nM); scN=take(nN); scO=take(nO); scC=take(nC)
    dhs,dh,res,snd,rcv,gx,gring,sems,lsem,wsem=take(10)
    at=Place(); mp=at.mp
    R,Dm=x_ref.shape; T=2*R; nh=qe_h.shape[0]; B=256; nb=T//B; H=wo.shape[0]; F=512
    core=at.core
    def dst_m(q):
        def dst(v,a,ch):
            if a<2: return outM[a].at[core,ch,:,pl.ds(q*F,F)]
            return outM[2].at[q,core,ch]
        return dst
    def dst_c(v,a,ch): return outC[a].at[core,ch,:,pl.ds(pl.multiple_of(v*128,128),128)]
    M=RING_M.bind(at,dst_m(0),scM); N=RING_N.bind(at,dst_m(1),scN,M.g); O=RING_O.bind(at,lambda v,a,ch: outO[0].at[core,ch],scO); C=RING_C.bind(at,dst_c,scC)
    mine=pl.multiple_of(mp*R,R); theirs=pl.multiple_of((1-mp)*R,R)
    W=R//3
    def blk(i): return pl.ds(i*W,W)
    at.barrier()
    c_dh=copy_to(dhs,dh.at[pl.ds(mine,R)],sems,0,{"mp":1-mp})

    def mlp(n2,n2t,acc,dn2,hid,dg,du,wgb,wub,wdb):
        def loads(g,u,d,q,slot):
            cs=pl.ds(pl.multiple_of(q*F,F),F)
            return [pltpu.make_async_copy(g.at[:,cs],wgb.at[slot],wsem.at[slot,0]),
                    pltpu.make_async_copy(u.at[:,cs],wub.at[slot],wsem.at[slot,1]),
                    pltpu.make_async_copy(d.at[cs,:],wdb.at[slot],wsem.at[slot,2])]
        for q in loads(wgp_h,wup_h,wdp_h,0,0): q.start()
        def pre(i,_):
            rows=pl.ds(pl.multiple_of(i*W,W),W); mr=pl.ds(pl.multiple_of(mine+i*W,W),W)
            r=x_ref[rows,:].astype(F32)+dot(heads[mr,:],wo[...])+dot(hrecv[rows,:],wop[...])
            res[rows,:]=r
            n=(r*lax.rsqrt(jnp.mean(r*r,axis=1,keepdims=True)+EPS)*gain_m[...].astype(F32)).astype(BF)
            n2[rows,:]=n
            n2t[:,rows]=n.T
            return 0
        lax.fori_loop(0,3,pre,0)
        acc[...]=jnp.zeros_like(acc); dn2[...]=jnp.zeros_like(dn2)
        def step(c,_):
            slot=lax.rem(c,2)
            for q in loads(wg_h,wu_h,wd_h,0,slot): q.wait()
            @pl.when(c==0)
            def _():
                for q in loads(wgp_h,wup_h,wdp_h,1,1): q.start()
            @pl.when((c>0)&(c<3))
            def _():
                for q in loads(wg_h,wu_h,wd_h,c-1,1-slot): q.start()
            wg,wu,wd=wgb[slot],wub[slot],wdb[slot]
            def half(i,_):
                rows=pl.ds(pl.multiple_of(i*W,W),W)
                gate=dot(n2[rows,:],wgb[slot]); up=dot(n2[rows,:],wub[slot]); dhid=dot(og[rows,:],wdb[slot],NT)
                sg=1.0/(1.0+jnp.exp(-gate)); silu=gate*sg
                hid[rows,:]=(silu*up).astype(BF)
                dg[rows,:]=(dhid*up*sg*(1.0+gate*(1.0-sg))).astype(BF)
                du[rows,:]=(dhid*silu).astype(BF)
                return 0
            lax.fori_loop(0,3,half,0)
            @pl.when(c==1)
            def _(): M.push(0)
            @pl.when(c==2)
            def _(): N.first(0)
            def back(i,_):
                rows=pl.ds(pl.multiple_of(i*W,W),W)
                acc[rows,:]=acc[rows,:]+dot(hid[rows,:],wdb[slot])
                dn2[rows,:]=dn2[rows,:]+(dot(dg[rows,:],wgb[slot],NT)+dot(du[rows,:],wub[slot],NT))
                return 0
            lax.fori_loop(0,3,back,0)
            @pl.when(c==3)
            def _(): N.rs(0,1)
            def wgrad(k,_):
                rr=pl.ds(pl.multiple_of(k*(Dm//2),Dm//2),Dm//2)
                M.g[0][slot,k]=dot(n2t[rr,:],dg[...]).reshape(RING,48,F).astype(BF)
                M.g[1][slot,k]=dot(n2t[rr,:],du[...]).reshape(RING,48,F).astype(BF)
                return 0
            lax.fori_loop(0,2,wgrad,0)
            M.g[2][slot]=dot(hid[...].T,og[...]).reshape(2,RING,32,Dm).astype(BF)
            @pl.when(lax.rem(c,2)==0)
            def _(): M.start(c//2)
            @pl.when(lax.rem(c,2)==1)
            def _(): N.start(c//2)
            @pl.when(c==2)
            def _(): N.rs(0,0)
            return 0
        lax.fori_loop(0,4,step,0)
        gx[...]=jnp.zeros_like(gx)
        def post(i,gpart):
            rows=pl.ds(pl.multiple_of(i*W,W),W)
            r=res[rows,:]; d=dn2[rows,:]
            acc[rows,:]=acc[rows,:]+r
            i2=lax.rsqrt(jnp.mean(r*r,axis=1,keepdims=True)+EPS)
            s=gain_m[...].astype(F32)*d
            dr=og[rows,:].astype(F32)+i2*s-r*(i2*i2*i2)*jnp.mean(s*r,axis=1,keepdims=True)
            res[rows,:]=dr
            da=dr.astype(BF)
            n2[rows,:]=da
            dhs[rows,:]=dot(da,wop[...],NT).astype(BF)
            return gpart+jnp.sum(d*r*i2,axis=0,keepdims=True)
        gpart=lax.fori_loop(0,3,post,jnp.zeros((1,Dm),F32))
        c_dh.start()
        c_out=pltpu.make_async_copy(acc,out_h,lsem.at[10]); c_out.start()
        gx[0,1:2]=gpart
        N.rs(0,2); M.first(0)
        def own(i,_):
            rows=pl.ds(pl.multiple_of(i*W,W),W)
            n2t[:,rows]=n2[rows,:].T
            dh[pl.ds(pl.multiple_of(mine+i*W,W),W),:]=dot(n2[rows,:],wo[...],NT).astype(BF)
            return 0
        lax.fori_loop(0,3,own,0)
        def ograd(k,_):
            rr=pl.ds(pl.multiple_of(k*(Dm//2),Dm//2),Dm//2)
            O.g[0][0,k]=dot(n2t[rr,:],hrecv[...]).reshape(RING,48,H).astype(BF)
            O.g[0][1,k]=dot(n2t[rr,:],heads[pl.ds(mine,R),:]).reshape(RING,48,H).astype(BF)
            return 0
        lax.fori_loop(0,2,ograd,0)
        O.start(0); O.start(1)
        N.rs(0,3); N.xstart(0); N.first(1)
        c_out.wait()
    V=pltpu.VMEM
    pl.run_scoped(mlp,V((R,Dm),BF),V((Dm,R),BF),V((R,Dm),F32),V((R,Dm),F32),V((R,F),BF),V((R,F),BF),V((R,F),BF),
                  V((2,Dm,F),BF),V((2,Dm,F),BF),V((2,F,Dm),BF))

    def attn(qe,ke,ve,cos_o,sin_o,nrm,x_p,wc,nt,doe,kt,dqt,ds_s,dn):
        ld=[pltpu.make_async_copy(s,d,lsem.at[i]) for i,(s,d) in enumerate(((norm_h,nrm),(ke_h,ke),(qe_h,qe),(ve_h,ve),(co_h,cos_o),(si_h,sin_o),(xp_h,x_p)))]
        ld+=[pltpu.make_async_copy(s.at[:,pl.ds(128*q,128)],wc.at[q,:,pl.ds(128*i,128)],lsem.at[12+3*q+i]) for q in range(nh//2) for i,s in enumerate((wq_h,wk_h,wv_h))]
        for q in ld: q.start()
        M.rs(0,0); O.push(0)
        ld[0].wait()
        def tr(i,_):
            c=pl.ds(pl.multiple_of(i*B,B),B)
            nt[:,c]=nrm[c,:].T
            return 0
        lax.fori_loop(0,nb,tr,0)
        N.rs(1,0); M.rs(0,1)
        for q in ld[1:]: q.wait()
        c_dh.wait(); N.rs(1,1)
        l=lanes((B,128)); low=l<64
        causal=lax.broadcasted_iota(jnp.int32,(B,B),0)<=lax.broadcasted_iota(jnp.int32,(B,B),1)
        def pair(p,_):
            cols=pl.ds(pl.multiple_of(p*128,128),128)
            for i in range(nb):
                rows=slice(i*B,(i+1)*B)
                d=dh[rows,cols].astype(F32); o=heads[rows,cols].astype(F32)
                t=d*o
                for hh in range(2):
                    if hh: t=pltpu.roll(t,64,1); d=pltpu.roll(d,64,1)
                    delta=jnp.sum(jnp.where(low,t,0.0),axis=1,keepdims=True)
                    a,b,c=split3(-delta)
                    doe[hh,rows,:]=jnp.where(low,d,jnp.where(l==64,a,jnp.where(l==65,b,jnp.where(l==66,c,0.0)))).astype(BF)
                    kt[hh,:,rows]=ke[2*p+hh,rows,:].T[0:64]
            dqt[...]=jnp.zeros_like(dqt)
            @pl.when(p==0)
            def _(): M.rs(0,2)
            @pl.when(p==2)
            def _(): M.ag(0,1)
            for j in range(nb):
                ks=slice(j*B,(j+1)*B); n0=j*B
                outs=[]
                for hh in range(2):
                    h=2*p+hh
                    s=dot(ke[h,ks,:],qe[h,n0:,:],NT)
                    dp=dot(ve[h,ks,:],doe[hh,n0:,:],NT)
                    sd=jnp.where(causal,s[:,:B],BIG)
                    s=sd if j==nb-1 else jnp.concatenate([sd,s[:,B:]],axis=1)
                    pt=jnp.exp2(s)
                    ds=(pt*dp).astype(BF)
                    pt=pt.astype(BF)
                    dv=dot(pt,doe[hh,n0:,:])
                    dk=dot(ds,qe[h,n0:,:])*LN2
                    dqt[64*hh:64*hh+64,n0:]+=dot(kt[hh,:,ks],ds)
                    outs.append((dk,dv))
                dk=jnp.where(low,outs[0][0],pltpu.roll(outs[1][0],64,1))
                dv=jnp.where(low,outs[0][1],pltpu.roll(outs[1][1],64,1))
                co=cos_o[ks,:]; si=sin_o[ks,:]
                ds_s[p,ks,128:256]=(dk*co-swap32(dk)*si).astype(BF)
                ds_s[p,ks,256:384]=dv.astype(BF)
                if j==0:
                    @pl.when(p==0)
                    def _(): N.rs(1,2)
                    @pl.when(p==1)
                    def _(): C.first(0); O.rs(0,0)
                    @pl.when(p==2)
                    def _(): C.first(1); C.rs(0,1); N.ag(0,1)
                if j==1:
                    @pl.when(p==0)
                    def _(): O.first(0)
                    @pl.when(p==1)
                    def _(): M.ag(0,0)
                    @pl.when(p==2)
                    def _(): O.rs(0,2)
                if j==3:
                    @pl.when(p==0)
                    def _(): M.rs(0,3); M.agstart(0)
                    @pl.when(p==1)
                    def _(): C.rs(0,0); N.ag(0,0)
                    @pl.when(p==2)
                    def _(): C.rs(1,0); M.ag(0,2)
            for i in range(nb):
                rows=slice(i*B,(i+1)*B)
                dq=dqt[:,rows].T*(HD**-0.5)
                co=cos_o[rows,:]; si=sin_o[rows,:]
                ds_s[p,rows,0:128]=(dq*co-swap32(dq)*si).astype(BF)
            for c in range(2):
                v=dot(nt[c*(Dm//2):(c+1)*(Dm//2),:],ds_s[p])
                for i in range(3): C.g[i][p,c]=v[:,128*i:128*i+128].reshape(RING,Dm//16,128).astype(BF)
            C.start(p)
            @pl.when(p==0)
            def _(): N.rs(1,3); N.agstart(0)
            @pl.when(p==1)
            def _(): O.rs(0,1)
            @pl.when(p==2)
            def _(): C.rs(0,2); N.ag(0,2); O.rs(0,3); O.agstart(0)
            return 0
        lax.fori_loop(0,nh//2,pair,0)
        def c_dn(c): return copy_to(snd.at[blk(c)],rcv.at[blk(c)],sems,2+c,{"mp":1-mp})
        def part(r0,xr,c):
            rows=pl.ds(pl.multiple_of(r0,W),W)
            v=dot(ds_s[0,rows,:],wc[0],NT)+dot(ds_s[1,rows,:],wc[1],NT)+dot(ds_s[2,rows,:],wc[2],NT)
            x=xr[blk(c)].astype(F32)
            xr=x*lax.rsqrt(jnp.mean(x*x,axis=1,keepdims=True)+EPS)
            return v, jnp.sum(v*xr,axis=0,keepdims=True)
        gsum=jnp.zeros((1,Dm),F32)
        for c in range(3):
            v,gs=part(theirs+c*W,x_p,c); gsum=gsum+gs
            snd[blk(c)]=v.astype(BF); c_dn(c).start()
            if c==0: C.rs(0,3); C.agstart(0); C.rs(1,1); M.ag(0,3)
            if c==1: C.first(2); N.ag(0,3); O.ag(0,0)
            if c==2: C.rs(1,2)
        for c in range(3):
            v,gs=part(mine+c*W,x_ref,c); gsum=gsum+gs
            dn[blk(c)]=v
            if c==0: C.rs(2,0); C.ag(0,0)
            if c==1: C.rs(1,3); C.agstart(1); O.ag(0,1)
        gx[0,0:1]=gsum
        c_gc=copy_to(gx.at[0],gx.at[1],sems,6,{"core":1-at.core}); c_gc.start()
        C.rs(2,1); C.ag(0,1); O.ag(0,2)
        c_gc.wait(); gring[0]=gx[0]+gx[1]
        def c_gr(d,t): return copy_to(gring.at[0 if t==0 else 4*d+t],gring.at[4*d+t+1],sems,7+4*d+t,{"chip":at.nxt[d]})
        c_gr(0,0).start(); c_gr(1,0).start()
        gtot=gring[0]
        for t in range(4):
            for d in range(2):
                if t<4-d:
                    c_gr(d,t).wait()
                    if t+1<4-d: c_gr(d,t+1).start()
                    gtot=gtot+gring[4*d+t+1]
            if t==0: C.rs(2,2); C.ag(1,0); C.ag(0,2)
            if t==1: C.rs(2,3); C.agstart(2); C.ag(1,1); C.ag(0,3); O.ag(0,3)
            if t==2: C.ag(2,0); C.ag(1,2)
            if t==3: C.ag(2,1); C.ag(1,3)
        gx[2]=gtot
        c_gx=copy_to(gx.at[2],gx.at[3],sems,5,{"mp":1-mp}); c_gx.start()
        C.ag(2,2); C.ag(2,3)
        for c in range(3):
            c_dn(c).wait()
            r=blk(c)
            d=dn[r]+rcv[r].astype(F32)
            x=x_ref[r].astype(F32)
            i1=lax.rsqrt(jnp.mean(x*x,axis=1,keepdims=True)+EPS)
            s=gain_a[...].astype(F32)*d
            res[r]=res[r]+i1*s-x*(i1*i1*i1)*jnp.mean(s*x,axis=1,keepdims=True)
        c_gx.wait(); gains_out[...]=gx[2]+gx[3]
        c_ig=pltpu.make_async_copy(res,ig_h,lsem.at[11]); c_ig.start()
        M.finish(0); N.finish(0); O.finish(0)
        for v in range(3): C.finish(v)
        c_ig.wait()
    hT=V((nh,T,128),BF)
    pl.run_scoped(attn,hT,hT,hT,V((T,128),F32),V((T,128),F32),V((T,Dm),BF),V((R,Dm),BF),V((nh//2,Dm,H),BF),
                  V((Dm,T),BF),V((2,T,128),BF),V((2,64,T),BF),V((128,T),F32),V((nh//2,T,H),BF),V((R,Dm),F32))

def main_call(x,og,heads,hrecv,wo,wop,gain_a,gain_m,hbm,cid):
    R,Dm=x.shape; T,H=heads.shape
    Vs=pl.BlockSpec(memory_space=pltpu.VMEM); N=pl.BlockSpec(memory_space=pl.ANY); sd=jax.ShapeDtypeStruct; V=pltpu.VMEM
    scs=[s.scratch() for s in (RING_M,RING_N,RING_O,RING_C)]
    local=[V((R,H),BF),V((T,H),BF),V((R,Dm),F32)]+[V((R,Dm),BF)]*2
    local+=[V((4,8,Dm),F32),V((RING,8,Dm),F32),pltpu.SemaphoreType.DMA((2,7+RING)),pltpu.SemaphoreType.DMA((21,)),pltpu.SemaphoreType.DMA((2,3))]
    outs=[sd((R,Dm),F32)]*2+[sd((2,RING,48,1024),BF)]*2+[sd((2,2,RING,32,Dm),BF)]+[sd((2,RING,48,H),BF)]*4+[sd((8,Dm),F32)]
    return pl.pallas_call(functools.partial(main_kernel,*[len(s) for s in scs]),
        out_shape=tuple(outs), in_specs=[Vs]*8+[N]*len(hbm), out_specs=(N,)*9+(Vs,),
        scratch_shapes=sum(scs,[])+local,
        compiler_params=pltpu.CompilerParams(collective_id=cid,has_side_effects=True,vmem_limit_bytes=67043328),
        name="mlp_and_backward")(x,og,heads,hrecv,wo,wop,gain_a.reshape(1,-1),gain_m.reshape(1,-1),*hbm)

def on_device(layer_input, gain_attn, w_query, w_key, w_value, w_out, gain_mlp, w_gate, w_up, w_down,
              segment_start, segment_parent, out_grad):
    weights = (w_out, w_gate, w_up, w_down)
    x_peer, normed, heads, heads_peer, qe, ke, ve, cosine, sine, peer_out, peer_gate, peer_up, peer_down = front(
        layer_input, gain_attn, w_query, w_key, w_value, segment_start, segment_parent, weights, 2
    )
    (output, input_grad, gate_g, up_g, down_g, out_g, query_g, key_g, value_g, gains) = main_call(
        layer_input, out_grad, heads, heads_peer, w_out, peer_out, gain_attn, gain_mlp,
        (w_gate, w_up, w_down, peer_gate, peer_up, peer_down, qe, ke, ve, cosine, sine, normed, x_peer,
         w_query, w_key, w_value), 1,
    )
    sums = [g.reshape(-1, g.shape[-1]) for g in (query_g, key_g, value_g, out_g, gate_g, up_g, down_g)]
    sums += [gains[0], gains[1]]
    if lax.axis_size("grp") > 1:
        sums = lax.psum([s.astype(F32) for s in sums], "grp")
    query_g, key_g, value_g, out_g, gate_g, up_g, down_g, gain_attn_grad, gain_mlp_grad = [s.astype(F32) for s in sums]
    return (
        output, input_grad, gain_attn_grad, query_g, key_g, value_g, out_g.T, gain_mlp_grad, gate_g, up_g, down_g,
    )


def solution(mesh):
    fine = Mesh(mesh.devices.reshape(-1, RING, 2, mesh.shape["mp"]), ("grp", "chip", "core", "mp"))
    dp = ("grp", "chip", "core")
    tok, col, row, tree = P(dp + ("mp",), None), P(None, "mp"), P("mp", None), P(dp, None)
    in_specs = (tok, P(), col, col, col, row, P(), col, col, row, tree, tree, tok)
    out_specs = (tok, tok, P(), col, col, col, row, P(), col, col, row)
    return jax.shard_map(on_device, mesh=fine, in_specs=in_specs, out_specs=out_specs, check_vma=False)
```

```python
import functools
import math

import jax
import jax.numpy as jnp
from jax import lax
from jax.experimental import pallas as pl
from jax.experimental.pallas import tpu as pltpu
from jax.sharding import Mesh
from jax.sharding import PartitionSpec as P

BF = jnp.bfloat16
F32 = jnp.float32
HD=64; EPS=1e-5; BIG=-1e30
C_Q = (HD**-0.5)*math.log2(math.e)
LN2 = math.log(2.0)
NT=(((1,),(1,)),((),())); NN=(((1,),(0,)),((),())); TN=(((0,),(0,)),((),()))
def dot(a,b,dims=NN): return lax.dot_general(a,b,dims,preferred_element_type=F32)
def lanes(shape): return lax.broadcasted_iota(jnp.int32, shape, 1)

def split3(x):
    hi=x.astype(BF).astype(F32); r=x-hi; mid=r.astype(BF).astype(F32); lo=r-mid
    return hi,mid,lo

def tables(starts, parents, row0, rows, nseg, tree_len):
    sh=(rows,128)
    t = row0 + lax.broadcasted_iota(jnp.int32, sh, 0)
    st=[starts[0,s] for s in range(nseg)]+[tree_len]
    par=[parents[0,s] for s in range(nseg)]
    ln=[st[s+1]-st[s] for s in range(nseg)]
    def pick(vals, idx):
        r = vals[0]
        for s in range(1,nseg): r = jnp.where(idx==s, vals[s], r)
        return r
    D=[]
    gps=[]
    for s in range(nseg):
        p=par[s]; gp=pick(par,p); gps.append(gp)
        off=jnp.where(p!=s, pick(ln,p), 0)+jnp.where((gp!=s)&(gp!=p), pick(ln,gp), 0)
        D.append(off-st[s])
    seg=jnp.zeros(sh,jnp.int32); pos=t+D[0]
    for s in range(1,nseg):
        ge=t>=st[s]
        seg=seg+ge.astype(jnp.int32)
        pos=pos+jnp.where(ge, D[s]-D[s-1], 0)
    f=lanes(sh)-64
    parl=jnp.zeros((1,128),jnp.int32)-1; gpl=parl
    fl=lanes((1,128))-64
    for s in range(nseg):
        parl=jnp.where(fl==s, par[s], parl); gpl=jnp.where(fl==s, gps[s], gpl)
    vis=(f==seg)|(parl==seg)|(gpl==seg)|(f<0)|(f>=nseg)
    qf=jnp.where(f==seg,1.0,0.0)
    kf=jnp.where(vis,0.0,BIG)
    kf=jnp.where((f>=8)&(f<11),1.0,kf)
    return pos.astype(F32), qf, kf

def rot_tables(posf):
    l=lax.broadcasted_iota(jnp.int32,(1,128),1)
    fr=jnp.exp((l%32).astype(F32)*(-2.0*math.log(10000.0)/HD))
    ang=posf*fr
    sg=jnp.where((l%64)<32,-1.0,1.0)
    return jnp.cos(ang), jnp.sin(ang)*sg

def swap32(x):
    l=lanes(x.shape)
    return jnp.where((l&32)==0, pltpu.roll(x,96,1), pltpu.roll(x,32,1))


MESH=pl.DeviceIdType.MESH
RING=8
def ring_chip(r):
    return jnp.where(r<RING//2, 2*r, 2*(RING-1-r)+1)
def chip_ring(n):
    return jnp.where(n%2==0, n//2, RING-1-n//2)

class Place:
    def __init__(self):
        self.core=lax.axis_index("core"); self.mp=lax.axis_index("mp")
        self.pos=chip_ring(lax.axis_index("chip"))
        self.nxt=[ring_chip(lax.rem(self.pos+1,RING)), ring_chip(lax.rem(self.pos+RING-1,RING))]
    def barrier(self):
        b=pltpu.get_barrier_semaphore()
        ds=[{"core":1-self.core},{"mp":1-self.mp},{"chip":self.nxt[0]},{"chip":self.nxt[1]}]
        for d in ds: pl.semaphore_signal(b, inc=1, device_id=d, device_id_type=MESH)
        pl.semaphore_wait(b, len(ds))

def copy_to(src,dst,sems,k,dev):
    return pltpu.make_async_remote_copy(src,dst,sems.at[0,k],sems.at[1,k],device_id=dev,device_id_type=MESH)

class Gather:
    def __init__(self,p,src,out,kinds,sems):
        self.p,self.src,self.out,self.kinds,self.sems=p,src,out,kinds,sems
    def ref(self,x,a,ch,core=None):
        n=self.out[a].shape[0]//(2*RING)
        return x[a].at[pl.ds(pl.multiple_of((self.p.core*RING+ch)*n,n),n)]
    def at(self,d,dist): return lax.rem(self.p.pos+(dist if d==0 else RING-dist),RING)
    def hops(self,a,d): return 4-self.kinds[a] if d==0 else 3+self.kinds[a]
    def cp(self,src,dst,a,k,dev):
        return pltpu.make_async_remote_copy(src,dst,self.sems.at[0,a,k],self.sems.at[1,a,k],device_id=dev,device_id_type=MESH)
    def cx(self,a): return self.cp(self.ref(self.src,a,self.p.pos),self.ref(self.out,a,self.p.pos),a,0,{"mp":1-self.p.mp})
    def cag(self,a,d,t):
        r=self.ref(self.out,a,self.at(1-d,t))
        return self.cp(r,r,a,1+4*d+t,{"chip":self.p.nxt[d]})
    def cfc(self,a,d,t):
        r=self.ref(self.out,a,self.at(1-d,t+1))
        return self.cp(r,r,a,9+4*d+t,{"core":1-self.p.core})
    def cfo(self,a):
        r=self.ref(self.out,a,self.p.pos)
        return self.cp(r,r,a,17,{"core":1-self.p.core})
    def agstart(self,a):
        self.cx(a).wait()
        for d in range(2): self.cag(a,d,0).start()
        self.cfo(a).start()
    def ag(self,a,t):
        for d in range(2):
            if t<self.hops(a,d):
                self.cag(a,d,t).wait()
                if t+1<self.hops(a,d): self.cag(a,d,t+1).start()
                self.cfc(a,d,t).start()
    def finish(self,a):
        self.cfo(a).wait()
        for d in range(2):
            for t in range(self.hops(a,d)): self.cfc(a,d,t).wait()

def front_kernel(nseg,starts,parents,x_ref,gain,wq,wk,wv,*refs):
    refs=list(refs)
    def take(n):
        r=refs[:n]; del refs[:n]; return r
    NW=(len(refs)-21)//2
    src=take(NW)
    big=take(7); heads,hrecv=take(2); out=take(NW)
    x_peer,normed,cos_o,sin_o,ke,ve,qe,qf_s,kf_s,sems,wsems,osem=take(12)
    at=Place(); mp=at.mp
    R=x_ref.shape[0]; T=2*R; B=256; nh=wq.shape[1]//HD
    G=Gather(at,src,out,[a%2 for a in range(NW)],wsems)
    mine=pl.multiple_of(mp*R,R); theirs=pl.multiple_of((1-mp)*R,R)
    at.barrier()
    peer={"mp":1-mp}
    NG=NW
    for a in range(NG): G.cx(a).start()
    c_x=copy_to(x_ref,x_peer,sems,0,peer); c_x.start()
    for a in range(NG,NW): G.cx(a).start()
    def tab(c,_):
        r0=pl.multiple_of(c*B,B); rows=pl.ds(r0,B)
        posf,qf,kf=tables(starts,parents,r0,B,nseg,T)
        co,si=rot_tables(posf)
        cos_o[rows,:]=co; sin_o[rows,:]=si
        qf_s[rows,:]=qf.astype(BF); kf_s[rows,:]=kf.astype(BF)
        return 0
    lb=lanes((B,128)); low=lb<64
    vone=jnp.where((lb>=64)&(lb<67),1.0,0.0)
    def proj(xr,base):
        def f(c,_):
            rows=pl.ds(pl.multiple_of(base+c*B,B),B)
            x=xr[pl.ds(pl.multiple_of(c*B,B),B),:].astype(F32)
            r1=lax.rsqrt(jnp.mean(x*x,axis=1,keepdims=True)+EPS)
            n=(x*r1*gain[0:1]).astype(BF)
            normed[rows,:]=n
            co=cos_o[rows,:]; si=sin_o[rows,:]; qf=qf_s[rows,:].astype(F32); kf=kf_s[rows,:].astype(F32)
            qq=dot(n,wq[...]); kk=dot(n,wk[...]); vv=dot(n,wv[...])
            for p in range(nh//2):
                cs=slice(128*p,128*p+128)
                q=qq[:,cs]; k=kk[:,cs]; v=vv[:,cs]
                q=(q*co+swap32(q)*si)*C_Q; k=k*co+swap32(k)*si
                for hh in range(2):
                    if hh: q=pltpu.roll(q,64,1); k=pltpu.roll(k,64,1); v=pltpu.roll(v,64,1)
                    qe[2*p+hh,rows,:]=jnp.where(low,q,qf).astype(BF)
                    ke[2*p+hh,rows,:]=jnp.where(low,k,kf).astype(BF)
                    ve[2*p+hh,rows,:]=jnp.where(low,v,vone).astype(BF)
            return 0
        lax.fori_loop(0,R//B,f,0)
    for a in range(NG): G.agstart(a)
    lax.fori_loop(0,T//B,tab,0)
    for a in range(NG): G.ag(a,0)
    proj(x_ref,mine)
    for a in range(NG): G.ag(a,1)
    c_x.wait()
    proj(x_peer,theirs)
    puts=[pltpu.make_async_copy(s,d,osem.at[i]) for i,(s,d) in enumerate(zip((x_peer,normed,cos_o,sin_o,ke,ve),big))]
    for q in puts: q.start()
    for a in range(NG): G.ag(a,2)
    def put_q(p): return pltpu.make_async_copy(qe.at[pl.ds(2*p,2)],big[6].at[pl.ds(2*p,2)],osem.at[6+p])
    causal=lax.broadcasted_iota(jnp.int32,(B,B),1)<=lax.broadcasted_iota(jnp.int32,(B,B),0)
    def c_h(p):
        cs=pl.ds(pl.multiple_of(p*128,128),128)
        return pltpu.make_async_remote_copy(heads.at[pl.ds(theirs,R),cs],hrecv.at[:,cs],sems.at[0,1+p],sems.at[1,1+p],device_id=peer,device_id_type=MESH)
    def attend(p,_):
        cs=pl.ds(pl.multiple_of(p*128,128),128)
        for i in range(T//B):
            n=(i+1)*B; rows=slice(i*B,(i+1)*B)
            outs=[]
            for hh in range(2):
                h=2*p+hh
                q=qe[h,rows,:]
                s=dot(q,ke[h,0:n,:],NT)
                sd=jnp.where(causal,s[:,n-B:],BIG)
                s=sd if i==0 else jnp.concatenate([s[:,:n-B],sd],axis=1)
                m=jnp.max(s,axis=1,keepdims=True)
                pr=jnp.exp2(s-m).astype(BF)
                o=dot(pr,ve[h,0:n,:])
                den=o[:,64:65]
                o=o*(1.0/den)
                a,b,c=split3(-(m+jnp.log2(den)))
                qe[h,rows,:]=jnp.where(lb==72,a,jnp.where(lb==73,b,jnp.where(lb==74,c,q.astype(F32)))).astype(BF)
                outs.append(o)
            heads[rows,cs]=jnp.where(low,outs[0],pltpu.roll(outs[1],64,1)).astype(BF)
            if i==3:
                @pl.when(p==1)
                def _():
                    for a in range(NG): G.ag(a,3)
        c_h(p).start()
        put_q(p).start()
        return 0
    lax.fori_loop(0,nh//2,attend,0)
    for a in range(NW): G.finish(a)
    for q in puts: q.wait()
    for p in range(nh//2): put_q(p).wait()
    for p in range(nh//2): c_h(p).wait()

def front(x,gain,wq,wk,wv,starts,parents,weights,cid):
    R,Dm=x.shape; T=2*R; H=wq.shape[1]; nh=H//HD; nseg=starts.shape[1]; NW=len(weights)
    Vs=pl.BlockSpec(memory_space=pltpu.VMEM); S=pl.BlockSpec(memory_space=pltpu.SMEM); N=pl.BlockSpec(memory_space=pl.ANY)
    sd=jax.ShapeDtypeStruct; hT=sd((nh,T,128),BF); V=pltpu.VMEM
    return pl.pallas_call(functools.partial(front_kernel,nseg),
        out_shape=(sd((R,Dm),BF),sd((T,Dm),BF),sd((T,128),F32),sd((T,128),F32),hT,hT,hT,sd((T,H),BF),sd((R,H),BF))+tuple(sd(w.shape,BF) for w in weights),
        in_specs=[S,S]+[Vs]*5+[N]*NW, out_specs=(N,)*7+(Vs,)*2+(N,)*NW,
        scratch_shapes=[V((R,Dm),BF),V((T,Dm),BF),V((T,128),F32),V((T,128),F32),V((nh,T,128),BF),V((nh,T,128),BF),V((nh,T,128),BF),V((T,128),BF),V((T,128),BF),
            pltpu.SemaphoreType.DMA((2,1+nh//2)),pltpu.SemaphoreType.DMA((2,NW,18)),pltpu.SemaphoreType.DMA((6+nh//2,))],
        compiler_params=pltpu.CompilerParams(collective_id=cid,has_side_effects=True,vmem_limit_bytes=67043328),
        name="attention_forward")(starts,parents,x,gain,wq,wk,wv,*weights)

class Ring:
    def __init__(self, shapes, kinds, count, gslots, swaps, early=True, slot=None):
        self.shapes,self.count,self.gslots,self.swaps,self.early=shapes,count,gslots,swaps,early
        self.slot=slot or (lambda u: lax.rem(u,gslots))
        self.nr=(len(swaps) if early else count) if swaps else count
        self.na=len(shapes); self.flows=[]
        for a,parts in enumerate(kinds):
            for c0,nc,k in parts:
                self.flows+=[(a,c0,nc,0,4-k),(a,c0,nc,1,3+k)]
        self.nf=len(self.flows)
        self.own=[s[0] for s in swaps] if swaps else list(range(count))
        self.nv=len(self.own)
        na,nf=self.na,self.nf
        self.k_rs=na; self.k_x=0; self.k_ag=na; self.k_fc=self.k_ag+4*nf; self.k_fo=self.k_fc+4*nf; self.k_put=self.k_fo+na
        self.n1=na+4*nf; self.n2=self.k_put+na
    def scratch(self):
        V=pltpu.VMEM; U=self.count
        s=[V((self.gslots,2,RING)+x,BF) for x in self.shapes] if self.gslots else []
        s+=[V((U,RING)+x,BF) for x in self.shapes]
        s+=[V((self.nr,)+x,BF) for x in self.shapes]
        s+=[V((self.nv,)+((RING,)+x if self.early else x),BF) for x in self.shapes] if self.swaps else []
        s+=[V((self.nr,h,self.shapes[a][0],nc),BF) for a,c0,nc,d,h in self.flows]
        return s+[pltpu.SemaphoreType.DMA((2,U,self.n1)),pltpu.SemaphoreType.DMA((2,self.nv,self.n2))]
    def bind(self,p,dst,sc,g=None):
        self.p,self.dst=p,dst
        sc=list(sc); na=self.na
        if g is None: g,sc=sc[:na],sc[na:]
        self.g=g; self.r=sc[:na]; self.fin=sc[na:2*na]; sc=sc[2*na:]
        if self.swaps: self.xr=sc[:na]; sc=sc[na:]
        self.arr=sc[:self.nf]; self.sem,self.sem2=sc[self.nf:]
        return self
    def at(self,d,dist):
        return lax.rem(self.p.pos+(dist if d==0 else RING-dist),RING)
    def cp(self,src,dst,u,k,dev):
        return pltpu.make_async_remote_copy(src,dst,self.sem.at[0,u,k],self.sem.at[1,u,k],device_id=dev,device_id_type=MESH)
    def cp2(self,src,dst,v,k,dev):
        return pltpu.make_async_remote_copy(src,dst,self.sem2.at[0,v,k],self.sem2.at[1,v,k],device_id=dev,device_id_type=MESH)
    def c1(self,u,a): return self.cp(self.g[a].at[self.slot(u),1-self.p.core],self.r[a].at[u],u,a,{"core":1-self.p.core})
    def start(self,u):
        for a in range(self.na): self.c1(u,a).start()
    def uown(self,v): return self.own[v] if self.swaps else v
    def u_of(self,w): return self.uown(w) if self.early else w
    def w_own(self,v): return v if self.early else self.uown(v)
    def crs(self,w,f,t):
        a,c0,nc,d,h=self.flows[f]
        src=self.r[a].at[self.u_of(w),self.at(d,h),:,pl.ds(c0,nc)] if t==0 else self.arr[f].at[w,t-1]
        return self.cp(src,self.arr[f].at[w,t],self.u_of(w),self.k_rs+4*f+t,{"chip":self.p.nxt[d]})
    def cx(self,v,a): return self.cp2(self.r[a].at[self.swaps[v][1]] if self.early else self.fin[a].at[self.swaps[v][1]],self.xr[a].at[v],v,self.k_x+a,{"mp":1-self.p.mp})
    def push(self,v):
        u=self.swaps[v][1]
        for a in range(self.na):
            self.c1(u,a).wait()
            r,g=self.r[a],self.g[a]
            def add(s,_):
                r[u,s]=r[u,s]+g[self.slot(u),self.p.core,s]; return 0
            lax.fori_loop(0,RING,add,0)
            self.cx(v,a).start()
    def xstart(self,v):
        for a in range(self.na): self.cx(v,a).start()
    def first(self,v):
        u=self.u_of(v)
        for a in range(self.na):
            self.c1(u,a).wait()
            if self.swaps and self.early: self.cx(v,a).wait()
            r,g=self.r[a],self.g[a]
            def add(s,_):
                t=r[u,s].astype(F32)+g[self.slot(u),self.p.core,s].astype(F32)
                if self.swaps and self.early: t=t+self.xr[a][v,s].astype(F32)
                r[u,s]=t.astype(BF); return 0
            lax.fori_loop(0,RING,add,0)
            for f in range(self.nf):
                if self.flows[f][0]==a: self.crs(v,f,0).start()
    def rs(self,v,t):
        u=self.u_of(v)
        for f,(a,c0,nc,d,h) in enumerate(self.flows):
            if t<h:
                self.crs(v,f,t).wait()
                if t+1<h:
                    self.arr[f][v,t]=self.arr[f][v,t]+self.r[a][u,self.at(d,h-t-1),:,pl.ds(c0,nc)]
                    self.crs(v,f,t+1).start()
        if t==3:
            for f in range(0,self.nf,2):
                a,c0,nc,d,h=self.flows[f]; h2=self.flows[f+1][4]
                w=self.r[a][u,self.p.pos,:,pl.ds(c0,nc)].astype(F32)+self.arr[f][v,h-1].astype(F32)+self.arr[f+1][v,h2-1].astype(F32)
                self.fin[a][v,:,pl.ds(c0,nc)]=w.astype(BF)
    def cag(self,v,f,t):
        a,c0,nc,d,h=self.flows[f]
        dst=self.dst(v,a,self.at(1-d,t)).at[:,pl.ds(c0,nc)]
        src=self.fin[a].at[self.w_own(v),:,pl.ds(c0,nc)] if t==0 else dst
        return self.cp2(src,dst,v,self.k_ag+4*f+t,{"chip":self.p.nxt[d]})
    def cfc(self,v,f,t):
        a,c0,nc,d,h=self.flows[f]
        ref=self.dst(v,a,self.at(1-d,t+1)).at[:,pl.ds(c0,nc)]
        return self.cp2(ref,ref,v,self.k_fc+4*f+t,{"core":1-self.p.core})
    def cfo(self,v,a): return self.cp2(self.fin[a].at[self.w_own(v)],self.dst(v,a,self.p.pos),v,self.k_fo+a,{"core":1-self.p.core})
    def put(self,v,a): return pltpu.make_async_copy(self.fin[a].at[self.w_own(v)],self.dst(v,a,self.p.pos),self.sem2.at[0,v,self.k_put+a])
    def agstart(self,v):
        for a in range(self.na):
            if not self.early:
                u=self.uown(v)
                self.cx(v,a).wait()
                self.fin[a][u]=self.fin[a][u]+self.xr[a][v]
            for f in range(self.nf):
                if self.flows[f][0]==a: self.cag(v,f,0).start()
            self.cfo(v,a).start(); self.put(v,a).start()
    def ag(self,v,t):
        for f,(a,c0,nc,d,h) in enumerate(self.flows):
            if t<h:
                self.cag(v,f,t).wait()
                if t+1<h: self.cag(v,f,t+1).start()
                self.cfc(v,f,t).start()
    def finish(self,v):
        for a in range(self.na):
            self.put(v,a).wait(); self.cfo(v,a).wait()
        for f,(a,c0,nc,d,h) in enumerate(self.flows):
            for t in range(h): self.cfc(v,f,t).wait()

SHAPES_M,KINDS_M=[(48,1536)],[[(0,768,0),(768,768,1)]]
RING_M=Ring(SHAPES_M,KINDS_M,2,2,[(1,0)],True,lambda u: 0)
RING_N=Ring(SHAPES_M,KINDS_M,2,0,[(1,0)],False,lambda u: 1)
RING_O=Ring([(48,384)],[[(0,256,0),(256,128,1)]],2,2,[(1,0)])
RING_C=Ring([(48,384)],[[(0,256,0),(256,128,1)]],3,3,[])
def main_kernel(nM,nN,nO,nC,*refs):
    refs=list(refs)
    def take(n):
        r=refs[:n]; del refs[:n]; return r
    x_ref,og,heads,hrecv,wo,wop,gain_a,gain_m=take(8)
    wg_h,wu_h,wd_h,wgp_h,wup_h,wdp_h,qe_h,ke_h,ve_h,co_h,si_h,norm_h,xp_h,wq_h,wk_h,wv_h=take(16)
    out_h,ig_h=take(2); outM=take(1); outO=take(1); outC=take(1); gains_out,=take(1)
    scM=take(nM); scN=take(nN); scO=take(nO); scC=take(nC)
    dhs,dh,res,snd,rcv,gx,gring,sems,lsem,wsem=take(10)
    at=Place(); mp=at.mp
    R,Dm=x_ref.shape; T=2*R; nh=qe_h.shape[0]; B=256; nb=T//B; H=wo.shape[0]; F=512
    core=at.core
    def dst_m(q): return lambda v,a,ch: outM[0].at[q,core,ch]
    def dst_c(v,a,ch): return outC[0].at[v,core,ch]
    M=RING_M.bind(at,dst_m(0),scM); N=RING_N.bind(at,dst_m(1),scN,M.g); O=RING_O.bind(at,lambda v,a,ch: outO[0].at[core,ch],scO); C=RING_C.bind(at,dst_c,scC)
    mine=pl.multiple_of(mp*R,R); theirs=pl.multiple_of((1-mp)*R,R)
    W=R//3
    def blk(i): return pl.ds(i*W,W)
    at.barrier()
    c_dh=copy_to(dhs,dh.at[pl.ds(mine,R)],sems,0,{"mp":1-mp})

    def mlp(n2,n2t,ogt,acc,dn2,hid,dg,du,wgb,wub,wdb):
        def loads(g,u,d,q,slot):
            cs=pl.ds(pl.multiple_of(q*F,F),F)
            return [pltpu.make_async_copy(g.at[:,cs],wgb.at[slot],wsem.at[slot,0]),
                    pltpu.make_async_copy(u.at[:,cs],wub.at[slot],wsem.at[slot,1]),
                    pltpu.make_async_copy(d.at[cs,:],wdb.at[slot],wsem.at[slot,2])]
        for q in loads(wgp_h,wup_h,wdp_h,0,0): q.start()
        def pre(i,_):
            rows=pl.ds(pl.multiple_of(i*W,W),W); mr=pl.ds(pl.multiple_of(mine+i*W,W),W)
            r=x_ref[rows,:].astype(F32)+dot(heads[mr,:],wo[...])+dot(hrecv[rows,:],wop[...])
            res[rows,:]=r
            n=(r*lax.rsqrt(jnp.mean(r*r,axis=1,keepdims=True)+EPS)*gain_m[1:2]).astype(BF)
            n2[rows,:]=n
            n2t[:,rows]=n.T
            ogt[:,rows]=og[rows,:].T
            return 0
        lax.fori_loop(0,3,pre,0)
        acc[...]=jnp.zeros_like(acc); dn2[...]=jnp.zeros_like(dn2)
        def step(c,_):
            slot=lax.rem(c,2)
            for q in loads(wg_h,wu_h,wd_h,0,slot): q.wait()
            @pl.when(c==0)
            def _():
                for q in loads(wgp_h,wup_h,wdp_h,1,1): q.start()
            @pl.when((c>0)&(c<3))
            def _():
                for q in loads(wg_h,wu_h,wd_h,c-1,1-slot): q.start()
            wg,wu,wd=wgb[slot],wub[slot],wdb[slot]
            def half(i,_):
                rows=pl.ds(pl.multiple_of(i*W,W),W)
                gate=dot(n2[rows,:],wgb[slot]); up=dot(n2[rows,:],wub[slot]); dhid=dot(og[rows,:],wdb[slot],NT)
                sg=1.0/(1.0+jnp.exp(-gate)); silu=gate*sg
                hid[rows,:]=(silu*up).astype(BF)
                dg[rows,:]=(dhid*up*sg*(1.0+gate*(1.0-sg))).astype(BF)
                du[rows,:]=(dhid*silu).astype(BF)
                return 0
            lax.fori_loop(0,3,half,0)
            @pl.when(c==1)
            def _(): M.push(0)
            @pl.when(c==2)
            def _(): N.first(0)
            def back(i,_):
                rows=pl.ds(pl.multiple_of(i*W,W),W)
                acc[rows,:]=acc[rows,:]+dot(hid[rows,:],wdb[slot])
                dn2[rows,:]=dn2[rows,:]+(dot(dg[rows,:],wgb[slot],NT)+dot(du[rows,:],wub[slot],NT))
                return 0
            lax.fori_loop(0,3,back,0)
            @pl.when(c==3)
            def _(): N.rs(0,1)
            def wgrad(k,_):
                rr=pl.ds(pl.multiple_of(k*(Dm//2),Dm//2),Dm//2)
                M.g[0][slot,k,:,:,0:F]=dot(n2t[rr,:],dg[...]).reshape(RING,48,F).astype(BF)
                M.g[0][slot,k,:,:,F:2*F]=dot(n2t[rr,:],du[...]).reshape(RING,48,F).astype(BF)
                M.g[0][slot,k,:,:,2*F:3*F]=dot(ogt[rr,:],hid[...]).reshape(RING,48,F).astype(BF)
                return 0
            lax.fori_loop(0,2,wgrad,0)
            @pl.when(lax.rem(c,2)==0)
            def _(): M.start(c//2)
            @pl.when(lax.rem(c,2)==1)
            def _(): N.start(c//2)
            @pl.when(c==2)
            def _(): N.rs(0,0)
            return 0
        lax.fori_loop(0,4,step,0)
        gx[...]=jnp.zeros_like(gx)
        def post(i,gpart):
            rows=pl.ds(pl.multiple_of(i*W,W),W)
            r=res[rows,:]; d=dn2[rows,:]
            acc[rows,:]=acc[rows,:]+r
            i2=lax.rsqrt(jnp.mean(r*r,axis=1,keepdims=True)+EPS)
            s=gain_m[1:2]*d
            dr=og[rows,:].astype(F32)+i2*s-r*(i2*i2*i2)*jnp.mean(s*r,axis=1,keepdims=True)
            res[rows,:]=dr
            da=dr.astype(BF)
            n2[rows,:]=da
            dhs[rows,:]=dot(da,wop[...],NT).astype(BF)
            return gpart+jnp.sum(d*r*i2,axis=0,keepdims=True)
        gpart=lax.fori_loop(0,3,post,jnp.zeros((1,Dm),F32))
        c_dh.start()
        c_out=pltpu.make_async_copy(acc,out_h,lsem.at[10]); c_out.start()
        gx[0,1:2]=gpart
        N.rs(0,2); M.first(0)
        def own(i,_):
            rows=pl.ds(pl.multiple_of(i*W,W),W)
            n2t[:,rows]=n2[rows,:].T
            dh[pl.ds(pl.multiple_of(mine+i*W,W),W),:]=dot(n2[rows,:],wo[...],NT).astype(BF)
            return 0
        lax.fori_loop(0,3,own,0)
        def ograd(k,_):
            rr=pl.ds(pl.multiple_of(k*(Dm//2),Dm//2),Dm//2)
            O.g[0][0,k]=dot(n2t[rr,:],hrecv[...]).reshape(RING,48,H).astype(BF)
            O.g[0][1,k]=dot(n2t[rr,:],heads[pl.ds(mine,R),:]).reshape(RING,48,H).astype(BF)
            return 0
        lax.fori_loop(0,2,ograd,0)
        O.start(0); O.start(1)
        N.rs(0,3); N.xstart(0); N.first(1)
        c_out.wait()
    V=pltpu.VMEM
    pl.run_scoped(mlp,V((R,Dm),BF),V((Dm,R),BF),V((Dm,R),BF),V((R,Dm),F32),V((R,Dm),F32),V((R,F),BF),V((R,F),BF),V((R,F),BF),
                  V((2,Dm,F),BF),V((2,Dm,F),BF),V((2,F,Dm),BF))

    def attn(qe,ke,ve,cos_o,sin_o,nrm,x_p,wc,nt,doe,kt,dqt,ds_s,dn):
        ld=[pltpu.make_async_copy(s,d,lsem.at[i]) for i,(s,d) in enumerate(((norm_h,nrm),(ke_h,ke),(qe_h,qe),(ve_h,ve),(co_h,cos_o),(si_h,sin_o),(xp_h,x_p)))]
        ld+=[pltpu.make_async_copy(s.at[:,pl.ds(128*q,128)],wc.at[q,:,pl.ds(128*i,128)],lsem.at[12+3*q+i]) for q in range(nh//2) for i,s in enumerate((wq_h,wk_h,wv_h))]
        for q in ld: q.start()
        M.rs(0,0); O.push(0)
        ld[0].wait()
        def tr(i,_):
            c=pl.ds(pl.multiple_of(i*B,B),B)
            nt[:,c]=nrm[c,:].T
            return 0
        lax.fori_loop(0,nb,tr,0)
        N.rs(1,0); M.rs(0,1)
        for q in ld[1:]: q.wait()
        c_dh.wait(); N.rs(1,1)
        l=lanes((B,128)); low=l<64
        causal=lax.broadcasted_iota(jnp.int32,(B,B),0)<=lax.broadcasted_iota(jnp.int32,(B,B),1)
        def pair(p,_):
            cols=pl.ds(pl.multiple_of(p*128,128),128)
            for i in range(nb):
                rows=slice(i*B,(i+1)*B)
                d=dh[rows,cols].astype(F32); o=heads[rows,cols].astype(F32)
                t=d*o
                for hh in range(2):
                    if hh: t=pltpu.roll(t,64,1); d=pltpu.roll(d,64,1)
                    delta=jnp.sum(jnp.where(low,t,0.0),axis=1,keepdims=True)
                    a,b,c=split3(-delta)
                    doe[hh,rows,:]=jnp.where(low,d,jnp.where(l==64,a,jnp.where(l==65,b,jnp.where(l==66,c,0.0)))).astype(BF)
                    kt[hh,:,rows]=ke[2*p+hh,rows,:].T[0:64]
            dqt[...]=jnp.zeros_like(dqt)
            @pl.when(p==0)
            def _(): M.rs(0,2)
            @pl.when(p==2)
            def _(): M.ag(0,1)
            for j in range(nb):
                ks=slice(j*B,(j+1)*B); n0=j*B
                outs=[]
                for hh in range(2):
                    h=2*p+hh
                    s=dot(ke[h,ks,:],qe[h,n0:,:],NT)
                    dp=dot(ve[h,ks,:],doe[hh,n0:,:],NT)
                    sd=jnp.where(causal,s[:,:B],BIG)
                    s=sd if j==nb-1 else jnp.concatenate([sd,s[:,B:]],axis=1)
                    pt=jnp.exp2(s)
                    ds=(pt*dp).astype(BF)
                    pt=pt.astype(BF)
                    dv=dot(pt,doe[hh,n0:,:])
                    dk=dot(ds,qe[h,n0:,:])*LN2
                    dqt[64*hh:64*hh+64,n0:]+=dot(kt[hh,:,ks],ds)
                    outs.append((dk,dv))
                dk=jnp.where(low,outs[0][0],pltpu.roll(outs[1][0],64,1))
                dv=jnp.where(low,outs[0][1],pltpu.roll(outs[1][1],64,1))
                co=cos_o[ks,:]; si=sin_o[ks,:]
                ds_s[p,ks,128:256]=(dk*co-swap32(dk)*si).astype(BF)
                ds_s[p,ks,256:384]=dv.astype(BF)
                if j==0:
                    @pl.when(p==0)
                    def _(): N.rs(1,2)
                    @pl.when(p==1)
                    def _(): C.first(0); O.rs(0,0)
                    @pl.when(p==2)
                    def _(): C.first(1); C.rs(0,1); N.ag(0,1)
                if j==1:
                    @pl.when(p==0)
                    def _(): O.first(0)
                    @pl.when(p==1)
                    def _(): M.ag(0,0)
                    @pl.when(p==2)
                    def _(): O.rs(0,2)
                if j==3:
                    @pl.when(p==0)
                    def _(): M.rs(0,3); M.agstart(0)
                    @pl.when(p==1)
                    def _(): C.rs(0,0); N.ag(0,0)
                    @pl.when(p==2)
                    def _(): C.rs(1,0); M.ag(0,2)
            for i in range(nb):
                rows=slice(i*B,(i+1)*B)
                dq=dqt[:,rows].T*(HD**-0.5)
                co=cos_o[rows,:]; si=sin_o[rows,:]
                ds_s[p,rows,0:128]=(dq*co-swap32(dq)*si).astype(BF)
            for c in range(2):
                v=dot(nt[c*(Dm//2):(c+1)*(Dm//2),:],ds_s[p])
                C.g[0][p,c]=v.reshape(RING,Dm//16,384).astype(BF)
            C.start(p)
            @pl.when(p==0)
            def _(): N.rs(1,3); N.agstart(0)
            @pl.when(p==1)
            def _(): O.rs(0,1)
            @pl.when(p==2)
            def _(): C.rs(0,2); N.ag(0,2); O.rs(0,3); O.agstart(0)
            return 0
        lax.fori_loop(0,nh//2,pair,0)
        def c_dn(c): return copy_to(snd.at[blk(c)],rcv.at[blk(c)],sems,2+c,{"mp":1-mp})
        def part(r0,xr,c):
            rows=pl.ds(pl.multiple_of(r0,W),W)
            v=dot(ds_s[0,rows,:],wc[0],NT)+dot(ds_s[1,rows,:],wc[1],NT)+dot(ds_s[2,rows,:],wc[2],NT)
            x=xr[blk(c)].astype(F32)
            xr=x*lax.rsqrt(jnp.mean(x*x,axis=1,keepdims=True)+EPS)
            return v, jnp.sum(v*xr,axis=0,keepdims=True)
        gsum=jnp.zeros((1,Dm),F32)
        for c in range(3):
            v,gs=part(theirs+c*W,x_p,c); gsum=gsum+gs
            snd[blk(c)]=v.astype(BF); c_dn(c).start()
            if c==0: C.rs(0,3); C.agstart(0); C.rs(1,1); M.ag(0,3)
            if c==1: C.first(2); N.ag(0,3); O.ag(0,0)
            if c==2: C.rs(1,2)
        for c in range(3):
            v,gs=part(mine+c*W,x_ref,c); gsum=gsum+gs
            dn[blk(c)]=v
            if c==0: C.rs(2,0); C.ag(0,0)
            if c==1: C.rs(1,3); C.agstart(1); O.ag(0,1)
        gx[0,0:1]=gsum
        c_gc=copy_to(gx.at[0],gx.at[1],sems,6,{"core":1-at.core}); c_gc.start()
        C.rs(2,1); C.ag(0,1); O.ag(0,2)
        c_gc.wait(); gring[0]=gx[0]+gx[1]
        def c_gr(d,t): return copy_to(gring.at[0 if t==0 else 4*d+t],gring.at[4*d+t+1],sems,7+4*d+t,{"chip":at.nxt[d]})
        c_gr(0,0).start(); c_gr(1,0).start()
        gtot=gring[0]
        for t in range(4):
            for d in range(2):
                if t<4-d:
                    c_gr(d,t).wait()
                    if t+1<4-d: c_gr(d,t+1).start()
                    gtot=gtot+gring[4*d+t+1]
            if t==0: C.rs(2,2); C.ag(1,0); C.ag(0,2)
            if t==1: C.rs(2,3); C.agstart(2); C.ag(1,1); C.ag(0,3); O.ag(0,3)
            if t==2: C.ag(2,0); C.ag(1,2)
            if t==3: C.ag(2,1); C.ag(1,3)
        gx[2]=gtot
        c_gx=copy_to(gx.at[2],gx.at[3],sems,5,{"mp":1-mp}); c_gx.start()
        C.ag(2,2); C.ag(2,3)
        for c in range(3):
            c_dn(c).wait()
            r=blk(c)
            d=dn[r]+rcv[r].astype(F32)
            x=x_ref[r].astype(F32)
            i1=lax.rsqrt(jnp.mean(x*x,axis=1,keepdims=True)+EPS)
            s=gain_a[0:1]*d
            res[r]=res[r]+i1*s-x*(i1*i1*i1)*jnp.mean(s*x,axis=1,keepdims=True)
        c_gx.wait(); gains_out[...]=gx[2]+gx[3]
        c_ig=pltpu.make_async_copy(res,ig_h,lsem.at[11]); c_ig.start()
        M.finish(0); N.finish(0); O.finish(0)
        for v in range(3): C.finish(v)
        c_ig.wait()
    hT=V((nh,T,128),BF)
    pl.run_scoped(attn,hT,hT,hT,V((T,128),F32),V((T,128),F32),V((T,Dm),BF),V((R,Dm),BF),V((nh//2,Dm,H),BF),
                  V((Dm,T),BF),V((2,T,128),BF),V((2,64,T),BF),V((128,T),F32),V((nh//2,T,H),BF),V((R,Dm),F32))

def main_call(x,og,heads,hrecv,wo,wop,gain_a,gain_m,hbm,cid):
    R,Dm=x.shape; T,H=heads.shape
    Vs=pl.BlockSpec(memory_space=pltpu.VMEM); N=pl.BlockSpec(memory_space=pl.ANY); sd=jax.ShapeDtypeStruct; V=pltpu.VMEM
    scs=[s.scratch() for s in (RING_M,RING_N,RING_O,RING_C)]
    local=[V((R,H),BF),V((T,H),BF),V((R,Dm),F32)]+[V((R,Dm),BF)]*2
    local+=[V((4,8,Dm),F32),V((RING,8,Dm),F32),pltpu.SemaphoreType.DMA((2,7+RING)),pltpu.SemaphoreType.DMA((21,)),pltpu.SemaphoreType.DMA((2,3))]
    outs=[sd((R,Dm),F32)]*2+[sd((2,2,RING,48,1536),BF),sd((2,RING,48,H),BF),sd((3,2,RING,48,384),BF),sd((8,Dm),F32)]
    return pl.pallas_call(functools.partial(main_kernel,*[len(s) for s in scs]),
        out_shape=tuple(outs), in_specs=[Vs]*8+[N]*len(hbm), out_specs=(N,)*5+(Vs,),
        scratch_shapes=sum(scs,[])+local,
        compiler_params=pltpu.CompilerParams(collective_id=cid,has_side_effects=True,vmem_limit_bytes=67043328),
        name="mlp_and_backward")(x,og,heads,hrecv,wo,wop,gain_a,gain_m,*hbm)

def widen_kernel(mlp,wo,qkv,gate,up,down,out,query,key,value):
    F=mlp.shape[2]//3; H=wo.shape[1]; B=mlp.shape[1]
    for q in range(2):
        cs=slice(F*q,F*q+F)
        gate[:,cs]=mlp[q,:,0:F].astype(F32)
        up[:,cs]=mlp[q,:,F:2*F].astype(F32)
        down[cs,:]=mlp[q,:,2*F:3*F].astype(F32).T
    out[...]=wo[...].astype(F32).T
    for p in range(qkv.shape[0]):
        cs=slice(128*p,128*p+128)
        query[:,cs]=qkv[p,:,0:128].astype(F32)
        key[:,cs]=qkv[p,:,128:256].astype(F32)
        value[:,cs]=qkv[p,:,256:384].astype(F32)

def widen(mlp,wo,qkv):
    Dm,H=wo.shape; F=mlp.shape[2]//3; B=128; P3=qkv.shape[0]
    sd=jax.ShapeDtypeStruct
    row=lambda n: pl.BlockSpec((B,n),lambda i:(i,0))
    col=lambda n: pl.BlockSpec((n,B),lambda i:(0,i))
    return pl.pallas_call(widen_kernel,grid=(Dm//B,),
        out_shape=(sd((Dm,2*F),F32),sd((Dm,2*F),F32),sd((2*F,Dm),F32),sd((H,Dm),F32))+(sd((Dm,H),F32),)*3,
        in_specs=[pl.BlockSpec((2,B,3*F),lambda i:(0,i,0)),row(H),pl.BlockSpec((P3,B,H),lambda i:(0,i,0))],
        out_specs=(row(2*F),row(2*F),col(2*F),col(H),row(H),row(H),row(H)),
        compiler_params=pltpu.CompilerParams(vmem_limit_bytes=48*2**20),name="widen")(mlp,wo,qkv)


def on_device(layer_input, gain_attn, w_query, w_key, w_value, w_out, gain_mlp, w_gate, w_up, w_down,
              segment_start, segment_parent, out_grad):
    weights = (w_out, w_gate, w_up, w_down)
    gains = jnp.stack([gain_attn, gain_mlp]).astype(F32)
    x_peer, normed, cosine, sine, ke, ve, qe, heads, heads_peer, peer_out, peer_gate, peer_up, peer_down = front(
        layer_input, gains, w_query, w_key, w_value, segment_start, segment_parent, weights, 2
    )
    output, input_grad, mlp_g, out_g, qkv_g, gain_g = main_call(
        layer_input, out_grad, heads, heads_peer, w_out, peer_out, gains, gains,
        (w_gate, w_up, w_down, peer_gate, peer_up, peer_down, qe, ke, ve, cosine, sine, normed, x_peer,
         w_query, w_key, w_value), 1,
    )
    sums = [mlp_g.reshape(2, -1, mlp_g.shape[-1]), out_g.reshape(-1, out_g.shape[-1]), qkv_g.reshape(3, -1, qkv_g.shape[-1]), gain_g]
    if lax.axis_size("grp") > 1:
        sums = lax.psum([s.astype(F32) for s in sums], "grp")
    mlp_g, out_g, qkv_g, gain_g = sums
    gate_g, up_g, down_g, out_g, query_g, key_g, value_g = widen(mlp_g, out_g, qkv_g)
    return (
        output, input_grad, gain_g[0], query_g, key_g, value_g, out_g, gain_g[1], gate_g, up_g, down_g,
    )


def solution(mesh):
    fine = Mesh(mesh.devices.reshape(-1, RING, 2, mesh.shape["mp"]), ("grp", "chip", "core", "mp"))
    dp = ("grp", "chip", "core")
    tok, col, row, tree = P(dp + ("mp",), None), P(None, "mp"), P("mp", None), P(dp, None)
    in_specs = (tok, P(), col, col, col, row, P(), col, col, row, tree, tree, tok)
    out_specs = (tok, tok, P(), col, col, col, row, P(), col, col, row)
    return jax.shard_map(on_device, mesh=fine, in_specs=in_specs, out_specs=out_specs, check_vma=False)
```

```python
import functools
import math

import jax
import jax.numpy as jnp
from jax import lax
from jax.experimental import pallas as pl
from jax.experimental.pallas import tpu as pltpu
from jax.sharding import Mesh
from jax.sharding import PartitionSpec as P

BF = jnp.bfloat16
F32 = jnp.float32
HD=64; EPS=1e-5; BIG=-1e30
C_Q = (HD**-0.5)*math.log2(math.e)
LN2 = math.log(2.0)
NT=(((1,),(1,)),((),())); NN=(((1,),(0,)),((),())); TN=(((0,),(0,)),((),()))
def dot(a,b,dims=NN): return lax.dot_general(a,b,dims,preferred_element_type=F32)
def lanes(shape): return lax.broadcasted_iota(jnp.int32, shape, 1)

def split3(x):
    hi=x.astype(BF).astype(F32); r=x-hi; mid=r.astype(BF).astype(F32); lo=r-mid
    return hi,mid,lo

def tables(starts, parents, row0, rows, nseg, tree_len):
    sh=(rows,128)
    t = row0 + lax.broadcasted_iota(jnp.int32, sh, 0)
    st=[starts[0,s] for s in range(nseg)]+[tree_len]
    par=[parents[0,s] for s in range(nseg)]
    ln=[st[s+1]-st[s] for s in range(nseg)]
    def pick(vals, idx):
        r = vals[0]
        for s in range(1,nseg): r = jnp.where(idx==s, vals[s], r)
        return r
    D=[]
    gps=[]
    for s in range(nseg):
        p=par[s]; gp=pick(par,p); gps.append(gp)
        off=jnp.where(p!=s, pick(ln,p), 0)+jnp.where((gp!=s)&(gp!=p), pick(ln,gp), 0)
        D.append(off-st[s])
    seg=jnp.zeros(sh,jnp.int32); pos=t+D[0]
    for s in range(1,nseg):
        ge=t>=st[s]
        seg=seg+ge.astype(jnp.int32)
        pos=pos+jnp.where(ge, D[s]-D[s-1], 0)
    f=lanes(sh)-64
    parl=jnp.zeros((1,128),jnp.int32)-1; gpl=parl
    fl=lanes((1,128))-64
    for s in range(nseg):
        parl=jnp.where(fl==s, par[s], parl); gpl=jnp.where(fl==s, gps[s], gpl)
    vis=(f==seg)|(parl==seg)|(gpl==seg)|(f<0)|(f>=nseg)
    qf=jnp.where(f==seg,1.0,0.0)
    kf=jnp.where(vis,0.0,BIG)
    kf=jnp.where((f>=8)&(f<11),1.0,kf)
    return pos.astype(F32), qf, kf

def rot_tables(posf):
    l=lax.broadcasted_iota(jnp.int32,(1,128),1)
    fr=jnp.exp((l%32).astype(F32)*(-2.0*math.log(10000.0)/HD))
    ang=posf*fr
    sg=jnp.where((l%64)<32,-1.0,1.0)
    return jnp.cos(ang), jnp.sin(ang)*sg

def swap32(x):
    l=lanes(x.shape)
    return jnp.where((l&32)==0, pltpu.roll(x,96,1), pltpu.roll(x,32,1))


MESH=pl.DeviceIdType.MESH
RING=8
def ring_chip(r):
    return jnp.where(r<RING//2, 2*r, 2*(RING-1-r)+1)
def chip_ring(n):
    return jnp.where(n%2==0, n//2, RING-1-n//2)

class Place:
    def __init__(self):
        self.core=lax.axis_index("core"); self.mp=lax.axis_index("mp")
        self.pos=chip_ring(lax.axis_index("chip"))
        self.nxt=[ring_chip(lax.rem(self.pos+1,RING)), ring_chip(lax.rem(self.pos+RING-1,RING))]
    def barrier(self):
        b=pltpu.get_barrier_semaphore()
        ds=[{"core":1-self.core},{"mp":1-self.mp},{"chip":self.nxt[0]},{"chip":self.nxt[1]}]
        for d in ds: pl.semaphore_signal(b, inc=1, device_id=d, device_id_type=MESH)
        return lambda: pl.semaphore_wait(b, len(ds))

def copy_to(src,dst,sems,k,dev):
    return pltpu.make_async_remote_copy(src,dst,sems.at[0,k],sems.at[1,k],device_id=dev,device_id_type=MESH)

class Gather:
    def __init__(self,p,src,out,kinds,sems):
        self.p,self.src,self.out,self.kinds,self.sems=p,src,out,kinds,sems
    def ref(self,x,a,ch,core=None):
        n=self.out[a].shape[0]//(2*RING)
        return x[a].at[pl.ds(pl.multiple_of((self.p.core*RING+ch)*n,n),n)]
    def at(self,d,dist): return lax.rem(self.p.pos+(dist if d==0 else RING-dist),RING)
    def hops(self,a,d): return 4-self.kinds[a] if d==0 else 3+self.kinds[a]
    def cp(self,src,dst,a,k,dev):
        return pltpu.make_async_remote_copy(src,dst,self.sems.at[0,a,k],self.sems.at[1,a,k],device_id=dev,device_id_type=MESH)
    def cx(self,a): return self.cp(self.ref(self.src,a,self.p.pos),self.ref(self.out,a,self.p.pos),a,0,{"mp":1-self.p.mp})
    def cag(self,a,d,t):
        r=self.ref(self.out,a,self.at(1-d,t))
        return self.cp(r,r,a,1+4*d+t,{"chip":self.p.nxt[d]})
    def cfc(self,a,d,t):
        r=self.ref(self.out,a,self.at(1-d,t+1))
        return self.cp(r,r,a,9+4*d+t,{"core":1-self.p.core})
    def cfo(self,a):
        r=self.ref(self.out,a,self.p.pos)
        return self.cp(r,r,a,17,{"core":1-self.p.core})
    def agstart(self,a):
        self.cx(a).wait()
        for d in range(2): self.cag(a,d,0).start()
        self.cfo(a).start()
    def ag(self,a,t):
        for d in range(2):
            if t<self.hops(a,d):
                self.cag(a,d,t).wait()
                if t+1<self.hops(a,d): self.cag(a,d,t+1).start()
                self.cfc(a,d,t).start()
    def finish(self,a):
        self.cfo(a).wait()
        for d in range(2):
            for t in range(self.hops(a,d)): self.cfc(a,d,t).wait()

def front_kernel(nseg,starts,parents,x_ref,gain,wq,wk,wv,*refs):
    refs=list(refs)
    def take(n):
        r=refs[:n]; del refs[:n]; return r
    NW=(len(refs)-21)//2
    src=take(NW)
    big=take(7); heads,hrecv=take(2); out=take(NW)
    x_peer,normed,cos_o,sin_o,ke,ve,qe,qf_s,kf_s,sems,wsems,osem=take(12)
    at=Place(); mp=at.mp
    R=x_ref.shape[0]; T=2*R; B=256; nh=wq.shape[1]//HD
    G=Gather(at,src,out,[a%2 for a in range(NW)],wsems)
    mine=pl.multiple_of(mp*R,R); theirs=pl.multiple_of((1-mp)*R,R)
    at.barrier()()
    peer={"mp":1-mp}
    NG=NW
    for a in range(NG): G.cx(a).start()
    c_x=copy_to(x_ref,x_peer,sems,0,peer); c_x.start()
    for a in range(NG,NW): G.cx(a).start()
    def tab(c,_):
        r0=pl.multiple_of(c*B,B); rows=pl.ds(r0,B)
        posf,qf,kf=tables(starts,parents,r0,B,nseg,T)
        co,si=rot_tables(posf)
        cos_o[rows,:]=co; sin_o[rows,:]=si
        qf_s[rows,:]=qf.astype(BF); kf_s[rows,:]=kf.astype(BF)
        return 0
    lb=lanes((B,128)); low=lb<64
    vone=jnp.where((lb>=64)&(lb<67),1.0,0.0)
    def proj(xr,base):
        def f(c,_):
            rows=pl.ds(pl.multiple_of(base+c*B,B),B)
            x=xr[pl.ds(pl.multiple_of(c*B,B),B),:].astype(F32)
            r1=lax.rsqrt(jnp.mean(x*x,axis=1,keepdims=True)+EPS)
            n=(x*r1*gain[...].astype(F32).reshape(1,-1)).astype(BF)
            normed[rows,:]=n
            co=cos_o[rows,:]; si=sin_o[rows,:]; qf=qf_s[rows,:].astype(F32); kf=kf_s[rows,:].astype(F32)
            qq=dot(n,wq[...]); kk=dot(n,wk[...]); vv=dot(n,wv[...])
            for p in range(nh//2):
                cs=slice(128*p,128*p+128)
                q=qq[:,cs]; k=kk[:,cs]; v=vv[:,cs]
                q=(q*co+swap32(q)*si)*C_Q; k=k*co+swap32(k)*si
                for hh in range(2):
                    if hh: q=pltpu.roll(q,64,1); k=pltpu.roll(k,64,1); v=pltpu.roll(v,64,1)
                    qe[2*p+hh,rows,:]=jnp.where(low,q,qf).astype(BF)
                    ke[2*p+hh,rows,:]=jnp.where(low,k,kf).astype(BF)
                    ve[2*p+hh,rows,:]=jnp.where(low,v,vone).astype(BF)
            return 0
        lax.fori_loop(0,R//B,f,0)
    for a in range(NG): G.agstart(a)
    lax.fori_loop(0,T//B,tab,0)
    for a in range(NG): G.ag(a,0)
    proj(x_ref,mine)
    for a in range(NG): G.ag(a,1)
    c_x.wait()
    proj(x_peer,theirs)
    puts=[pltpu.make_async_copy(s,d,osem.at[i]) for i,(s,d) in enumerate(zip((x_peer,normed,cos_o,sin_o,ke,ve),big))]
    for q in puts: q.start()
    for a in range(NG): G.ag(a,2)
    def put_q(p): return pltpu.make_async_copy(qe.at[pl.ds(2*p,2)],big[6].at[pl.ds(2*p,2)],osem.at[6+p])
    causal=lax.broadcasted_iota(jnp.int32,(B,B),1)<=lax.broadcasted_iota(jnp.int32,(B,B),0)
    NB=R//B
    def c_h(p,q):
        cs=pl.ds(pl.multiple_of(p*128,128),128)
        return pltpu.make_async_remote_copy(heads.at[pl.ds(pl.multiple_of(theirs+q*B,B),B),cs],hrecv.at[pl.ds(q*B,B),cs],sems.at[0,1+NB*p+q],sems.at[1,1+NB*p+q],device_id=peer,device_id_type=MESH)
    def attend(p,_):
        cs=pl.ds(pl.multiple_of(p*128,128),128)
        for i in range(T//B):
            n=(i+1)*B; rows=slice(i*B,(i+1)*B)
            outs=[]
            for hh in range(2):
                h=2*p+hh
                q=qe[h,rows,:]
                s=dot(q,ke[h,0:n,:],NT)
                sd=jnp.where(causal,s[:,n-B:],BIG)
                s=sd if i==0 else jnp.concatenate([s[:,:n-B],sd],axis=1)
                m=jnp.max(s,axis=1,keepdims=True)
                pr=jnp.exp2(s-m).astype(BF)
                o=dot(pr,ve[h,0:n,:])
                den=o[:,64:65]
                o=o*(1.0/den)
                a,b,c=split3(-(m+jnp.log2(den)))
                qe[h,rows,:]=jnp.where(lb==72,a,jnp.where(lb==73,b,jnp.where(lb==74,c,q.astype(F32)))).astype(BF)
                outs.append(o)
            heads[rows,cs]=jnp.where(low,outs[0],pltpu.roll(outs[1],64,1)).astype(BF)
            @pl.when(1-mp==i//NB)
            def _(): c_h(p,i%NB).start()
            if i==3:
                @pl.when(p==2)
                def _():
                    for a in range(NG): G.ag(a,3)
        put_q(p).start()
        return 0
    lax.fori_loop(0,nh//2,attend,0)
    for a in range(NW): G.finish(a)
    for q in puts: q.wait()
    for p in range(nh//2): put_q(p).wait()
    for p in range(nh//2):
        for q in range(NB): c_h(p,q).wait()

def front(x,gain,wq,wk,wv,starts,parents,weights,cid):
    R,Dm=x.shape; T=2*R; H=wq.shape[1]; nh=H//HD; nseg=starts.shape[1]; NW=len(weights)
    Vs=pl.BlockSpec(memory_space=pltpu.VMEM); S=pl.BlockSpec(memory_space=pltpu.SMEM); N=pl.BlockSpec(memory_space=pl.ANY)
    sd=jax.ShapeDtypeStruct; hT=sd((nh,T,128),BF); V=pltpu.VMEM
    return pl.pallas_call(functools.partial(front_kernel,nseg),
        out_shape=(sd((R,Dm),BF),sd((T,Dm),BF),sd((T,128),F32),sd((T,128),F32),hT,hT,hT,sd((T,H),BF),sd((R,H),BF))+tuple(sd(w.shape,BF) for w in weights),
        in_specs=[S,S]+[Vs]*5+[N]*NW, out_specs=(N,)*7+(Vs,)*2+(N,)*NW,
        scratch_shapes=[V((R,Dm),BF),V((T,Dm),BF),V((T,128),F32),V((T,128),F32),V((nh,T,128),BF),V((nh,T,128),BF),V((nh,T,128),BF),V((T,128),BF),V((T,128),BF),
            pltpu.SemaphoreType.DMA((2,1+(nh//2)*(R//256))),pltpu.SemaphoreType.DMA((2,NW,18)),pltpu.SemaphoreType.DMA((6+nh//2,))],
        compiler_params=pltpu.CompilerParams(collective_id=cid,has_side_effects=True,vmem_limit_bytes=67043328),
        name="attention_forward")(starts,parents,x,gain,wq,wk,wv,*weights)

class Ring:
    def __init__(self, shapes, kinds, count, gslots, swaps, early=True, slot=None):
        self.shapes,self.count,self.gslots,self.swaps,self.early=shapes,count,gslots,swaps,early
        self.slot=slot or (lambda u: lax.rem(u,gslots))
        self.nr=(len(swaps) if early else count) if swaps else count
        self.na=len(shapes); self.flows=[]
        for a,parts in enumerate(kinds):
            for c0,nc,k in parts:
                self.flows+=[(a,c0,nc,0,4-k),(a,c0,nc,1,3+k)]
        self.nf=len(self.flows)
        self.own=[s[0] for s in swaps] if swaps else list(range(count))
        self.nv=len(self.own)
        na,nf=self.na,self.nf
        self.k_rs=na; self.k_x=0; self.k_ag=na; self.k_fc=self.k_ag+4*nf; self.k_fo=self.k_fc+4*nf; self.k_put=self.k_fo+na
        self.n1=na+4*nf; self.n2=self.k_put+na
    def scratch(self):
        V=pltpu.VMEM; U=self.count
        s=[V((self.gslots,2,RING)+x,BF) for x in self.shapes] if self.gslots else []
        s+=[V((U,RING)+x,BF) for x in self.shapes]
        s+=[V((self.nr,)+x,BF) for x in self.shapes]
        s+=[V((self.nv,)+((RING,)+x if self.early else x),BF) for x in self.shapes] if self.swaps else []
        s+=[V((self.nr,h,self.shapes[a][0],nc),BF) for a,c0,nc,d,h in self.flows]
        return s+[pltpu.SemaphoreType.DMA((2,U,self.n1)),pltpu.SemaphoreType.DMA((2,self.nv,self.n2))]
    def bind(self,p,dst,sc,g=None):
        self.p,self.dst=p,dst
        sc=list(sc); na=self.na
        if g is None: g,sc=sc[:na],sc[na:]
        self.g=g; self.r=sc[:na]; self.fin=sc[na:2*na]; sc=sc[2*na:]
        if self.swaps: self.xr=sc[:na]; sc=sc[na:]
        self.arr=sc[:self.nf]; self.sem,self.sem2=sc[self.nf:]
        return self
    def at(self,d,dist):
        return lax.rem(self.p.pos+(dist if d==0 else RING-dist),RING)
    def cp(self,src,dst,u,k,dev):
        return pltpu.make_async_remote_copy(src,dst,self.sem.at[0,u,k],self.sem.at[1,u,k],device_id=dev,device_id_type=MESH)
    def cp2(self,src,dst,v,k,dev):
        return pltpu.make_async_remote_copy(src,dst,self.sem2.at[0,v,k],self.sem2.at[1,v,k],device_id=dev,device_id_type=MESH)
    def c1(self,u,a): return self.cp(self.g[a].at[self.slot(u),1-self.p.core],self.r[a].at[u],u,a,{"core":1-self.p.core})
    def start(self,u):
        for a in range(self.na): self.c1(u,a).start()
    def uown(self,v): return self.own[v] if self.swaps else v
    def u_of(self,w): return self.uown(w) if self.early else w
    def w_own(self,v): return v if self.early else self.uown(v)
    def crs(self,w,f,t):
        a,c0,nc,d,h=self.flows[f]
        src=self.r[a].at[self.u_of(w),self.at(d,h),:,pl.ds(c0,nc)] if t==0 else self.arr[f].at[w,t-1]
        return self.cp(src,self.arr[f].at[w,t],self.u_of(w),self.k_rs+4*f+t,{"chip":self.p.nxt[d]})
    def cx(self,v,a): return self.cp2(self.r[a].at[self.swaps[v][1]] if self.early else self.fin[a].at[self.swaps[v][1]],self.xr[a].at[v],v,self.k_x+a,{"mp":1-self.p.mp})
    def push(self,v):
        u=self.swaps[v][1]
        for a in range(self.na):
            self.c1(u,a).wait()
            r,g=self.r[a],self.g[a]
            def add(s,_):
                r[u,s]=r[u,s]+g[self.slot(u),self.p.core,s]; return 0
            lax.fori_loop(0,RING,add,0)
            self.cx(v,a).start()
    def xstart(self,v):
        for a in range(self.na): self.cx(v,a).start()
    def first(self,v):
        u=self.u_of(v)
        for a in range(self.na):
            self.c1(u,a).wait()
            if self.swaps and self.early: self.cx(v,a).wait()
            r,g=self.r[a],self.g[a]
            def add(s,_):
                t=r[u,s].astype(F32)+g[self.slot(u),self.p.core,s].astype(F32)
                if self.swaps and self.early: t=t+self.xr[a][v,s].astype(F32)
                r[u,s]=t.astype(BF); return 0
            lax.fori_loop(0,RING,add,0)
            for f in range(self.nf):
                if self.flows[f][0]==a: self.crs(v,f,0).start()
    def rs(self,v,t):
        u=self.u_of(v)
        for f,(a,c0,nc,d,h) in enumerate(self.flows):
            if t<h:
                self.crs(v,f,t).wait()
                if t+1<h:
                    self.arr[f][v,t]=self.arr[f][v,t]+self.r[a][u,self.at(d,h-t-1),:,pl.ds(c0,nc)]
                    self.crs(v,f,t+1).start()
        if t==3:
            for f in range(0,self.nf,2):
                a,c0,nc,d,h=self.flows[f]; h2=self.flows[f+1][4]
                w=self.r[a][u,self.p.pos,:,pl.ds(c0,nc)].astype(F32)+self.arr[f][v,h-1].astype(F32)+self.arr[f+1][v,h2-1].astype(F32)
                self.fin[a][v,:,pl.ds(c0,nc)]=w.astype(BF)
    def cag(self,v,f,t):
        a,c0,nc,d,h=self.flows[f]
        dst=self.dst(v,a,self.at(1-d,t)).at[:,pl.ds(c0,nc)]
        src=self.fin[a].at[self.w_own(v),:,pl.ds(c0,nc)] if t==0 else dst
        return self.cp2(src,dst,v,self.k_ag+4*f+t,{"chip":self.p.nxt[d]})
    def cfc(self,v,f,t):
        a,c0,nc,d,h=self.flows[f]
        ref=self.dst(v,a,self.at(1-d,t+1)).at[:,pl.ds(c0,nc)]
        return self.cp2(ref,ref,v,self.k_fc+4*f+t,{"core":1-self.p.core})
    def cfo(self,v,a): return self.cp2(self.fin[a].at[self.w_own(v)],self.dst(v,a,self.p.pos),v,self.k_fo+a,{"core":1-self.p.core})
    def put(self,v,a): return pltpu.make_async_copy(self.fin[a].at[self.w_own(v)],self.dst(v,a,self.p.pos),self.sem2.at[0,v,self.k_put+a])
    def agstart(self,v):
        for a in range(self.na):
            if not self.early:
                u=self.uown(v)
                self.cx(v,a).wait()
                self.fin[a][u]=self.fin[a][u]+self.xr[a][v]
            for f in range(self.nf):
                if self.flows[f][0]==a: self.cag(v,f,0).start()
            self.cfo(v,a).start(); self.put(v,a).start()
    def ag(self,v,t):
        for f,(a,c0,nc,d,h) in enumerate(self.flows):
            if t<h:
                self.cag(v,f,t).wait()
                if t+1<h: self.cag(v,f,t+1).start()
                self.cfc(v,f,t).start()
    def finish(self,v):
        for a in range(self.na):
            self.put(v,a).wait(); self.cfo(v,a).wait()
        for f,(a,c0,nc,d,h) in enumerate(self.flows):
            for t in range(h): self.cfc(v,f,t).wait()

SHAPES_M,KINDS_M=[(48,1536)],[[(0,768,0),(768,768,1)]]
RING_M=Ring(SHAPES_M,KINDS_M,2,2,[(1,0)],True,lambda u: 0)
RING_N=Ring(SHAPES_M,KINDS_M,2,0,[(1,0)],False,lambda u: 1)
RING_O=Ring([(48,384)],[[(0,256,0),(256,128,1)]],2,2,[(1,0)])
RING_C=Ring([(48,384)],[[(0,256,0),(256,128,1)]],3,3,[])
SCHEDULE={
"m1":[("N","rs",0,2),("M","first",0)],
"m2":[("N","rs",0,3),("N","xstart",0),("N","first",1)],
"a0":[("M","rs",0,0),("O","push",0)],
"a1":[("N","rs",1,0),("M","rs",0,1)],
"a2":[("N","rs",1,1)],
"p0s":[("M","rs",0,2)],
"p0j0":[("N","rs",1,2)],
"p0j1":[("O","first",0)],
"p0j3":[("M","rs",0,3),("M","agstart",0)],
"p0e":[("N","rs",1,3),("N","agstart",0)],
"p1j0":[("C","first",0),("O","rs",0,0)],
"p1j1":[("M","ag",0,0)],
"p1j3":[("C","rs",0,0),("N","ag",0,0)],
"p1e":[("O","rs",0,1)],
"p2s":[("M","ag",0,1)],
"p2j0":[("C","first",1),("C","rs",0,1),("N","ag",0,1)],
"p2j1":[("O","rs",0,2)],
"p2j3":[("C","rs",1,0),("M","ag",0,2)],
"p2e":[("C","rs",0,2),("N","ag",0,2),("O","rs",0,3),("O","agstart",0)],
"t0":[("C","rs",0,3),("C","agstart",0),("C","rs",1,1),("M","ag",0,3)],
"t1":[("C","first",2),("N","ag",0,3),("O","ag",0,0)],
"t2":[("C","rs",1,2)],
"u0":[("C","rs",2,0),("C","ag",0,0)],
"u1":[("C","rs",1,3),("C","agstart",1),("O","ag",0,1)],
"g":[("C","rs",2,1),("C","ag",0,1),("O","ag",0,2)],
"g0":[("C","rs",2,2),("C","ag",1,0),("C","ag",0,2)],
"g1":[("C","rs",2,3),("C","agstart",2),("C","ag",1,1),("C","ag",0,3),("O","ag",0,3)],
"g2":[("C","ag",2,0),("C","ag",1,2)],
"g3":[("C","ag",2,1),("C","ag",1,3)],
"z":[("C","ag",2,2),("C","ag",2,3)],
}
def main_kernel(nM,nN,nO,nC,*refs):
    refs=list(refs)
    def take(n):
        r=refs[:n]; del refs[:n]; return r
    x_ref,og,heads,hrecv,wo,wop,gain_a,gain_m=take(8)
    wg_h,wu_h,wd_h,wgp_h,wup_h,wdp_h,qe_h,ke_h,ve_h,co_h,si_h,norm_h,xp_h,wq_h,wk_h,wv_h=take(16)
    out_h,ig_h=take(2); outM=take(1); outO=take(1); outC=take(1); gains_out,=take(1)
    scM=take(nM); scN=take(nN); scO=take(nO); scC=take(nC)
    dhs,dh,res,snd,rcv,gx,gring,sems,lsem,wsem=take(10)
    at=Place(); mp=at.mp
    R,Dm=x_ref.shape; T=2*R; nh=qe_h.shape[0]; B=256; nb=T//B; H=wo.shape[0]; F=512
    core=at.core
    rings={}
    def tick(site):
        for name,op,*args in SCHEDULE.get(site,()): getattr(rings[name],op)(*args)
    def dst_m(q): return lambda v,a,ch: outM[0].at[q,core,ch]
    def dst_c(v,a,ch): return outC[0].at[v,core,ch]
    M=RING_M.bind(at,dst_m(0),scM); N=RING_N.bind(at,dst_m(1),scN,M.g); O=RING_O.bind(at,lambda v,a,ch: outO[0].at[core,ch],scO); C=RING_C.bind(at,dst_c,scC)
    rings.update(M=M,N=N,O=O,C=C)
    mine=pl.multiple_of(mp*R,R); theirs=pl.multiple_of((1-mp)*R,R)
    W=R//3
    def blk(i): return pl.ds(i*W,W)
    arrived=at.barrier()
    c_dh=copy_to(dhs,dh.at[pl.ds(mine,R)],sems,0,{"mp":1-mp})

    def mlp(n2,n2t,ogt,acc,dn2,hid,dg,du,wgb,wub,wdb):
        def loads(g,u,d,q,slot):
            cs=pl.ds(pl.multiple_of(q*F,F),F)
            return [pltpu.make_async_copy(g.at[:,cs],wgb.at[slot],wsem.at[slot,0]),
                    pltpu.make_async_copy(u.at[:,cs],wub.at[slot],wsem.at[slot,1]),
                    pltpu.make_async_copy(d.at[cs,:],wdb.at[slot],wsem.at[slot,2])]
        for q in loads(wgp_h,wup_h,wdp_h,0,0): q.start()
        def pre(i,_):
            rows=pl.ds(pl.multiple_of(i*W,W),W); mr=pl.ds(pl.multiple_of(mine+i*W,W),W)
            r=x_ref[rows,:].astype(F32)+dot(heads[mr,:],wo[...])+dot(hrecv[rows,:],wop[...])
            res[rows,:]=r
            n=(r*lax.rsqrt(jnp.mean(r*r,axis=1,keepdims=True)+EPS)*gain_m[...].astype(F32).reshape(1,-1)).astype(BF)
            n2[rows,:]=n
            n2t[:,rows]=n.T
            ogt[:,rows]=og[rows,:].T
            return 0
        lax.fori_loop(0,3,pre,0)
        arrived()
        acc[...]=jnp.zeros_like(acc); dn2[...]=jnp.zeros_like(dn2)
        def step(c,_):
            slot=lax.rem(c,2)
            for q in loads(wg_h,wu_h,wd_h,0,slot): q.wait()
            @pl.when(c==0)
            def _():
                for q in loads(wgp_h,wup_h,wdp_h,1,1): q.start()
            @pl.when((c>0)&(c<3))
            def _():
                for q in loads(wg_h,wu_h,wd_h,c-1,1-slot): q.start()
            wg,wu,wd=wgb[slot],wub[slot],wdb[slot]
            def half(i,_):
                rows=pl.ds(pl.multiple_of(i*W,W),W)
                gate=dot(n2[rows,:],wgb[slot]); up=dot(n2[rows,:],wub[slot]); dhid=dot(og[rows,:],wdb[slot],NT)
                sg=1.0/(1.0+jnp.exp(-gate)); silu=gate*sg
                hid[rows,:]=(silu*up).astype(BF)
                dg[rows,:]=(dhid*up*sg*(1.0+gate*(1.0-sg))).astype(BF)
                du[rows,:]=(dhid*silu).astype(BF)
                return 0
            lax.fori_loop(0,3,half,0)
            @pl.when(c==1)
            def _(): M.push(0)
            @pl.when(c==2)
            def _(): N.first(0)
            def back(i,_):
                rows=pl.ds(pl.multiple_of(i*W,W),W)
                acc[rows,:]=acc[rows,:]+dot(hid[rows,:],wdb[slot])
                dn2[rows,:]=dn2[rows,:]+(dot(dg[rows,:],wgb[slot],NT)+dot(du[rows,:],wub[slot],NT))
                return 0
            lax.fori_loop(0,3,back,0)
            @pl.when(c==3)
            def _(): N.rs(0,1)
            def wgrad(k,_):
                rr=pl.ds(pl.multiple_of(k*(Dm//2),Dm//2),Dm//2)
                M.g[0][slot,k,:,:,0:F]=dot(n2t[rr,:],dg[...]).reshape(RING,48,F).astype(BF)
                M.g[0][slot,k,:,:,F:2*F]=dot(n2t[rr,:],du[...]).reshape(RING,48,F).astype(BF)
                M.g[0][slot,k,:,:,2*F:3*F]=dot(ogt[rr,:],hid[...]).reshape(RING,48,F).astype(BF)
                return 0
            lax.fori_loop(0,2,wgrad,0)
            @pl.when(lax.rem(c,2)==0)
            def _(): M.start(c//2)
            @pl.when(lax.rem(c,2)==1)
            def _(): N.start(c//2)
            @pl.when(c==2)
            def _(): N.rs(0,0)
            return 0
        lax.fori_loop(0,4,step,0)
        tick("m0")
        gx[...]=jnp.zeros_like(gx)
        def post(i,gpart):
            rows=pl.ds(pl.multiple_of(i*W,W),W)
            r=res[rows,:]; d=dn2[rows,:]
            acc[rows,:]=acc[rows,:]+r
            i2=lax.rsqrt(jnp.mean(r*r,axis=1,keepdims=True)+EPS)
            s=gain_m[...].astype(F32).reshape(1,-1)*d
            dr=og[rows,:].astype(F32)+i2*s-r*(i2*i2*i2)*jnp.mean(s*r,axis=1,keepdims=True)
            res[rows,:]=dr
            da=dr.astype(BF)
            n2[rows,:]=da
            dhs[rows,:]=dot(da,wop[...],NT).astype(BF)
            return gpart+jnp.sum(d*r*i2,axis=0,keepdims=True)
        gpart=lax.fori_loop(0,3,post,jnp.zeros((1,Dm),F32))
        c_dh.start()
        c_out=pltpu.make_async_copy(acc,out_h,lsem.at[10]); c_out.start()
        gx[0,1:2]=gpart
        tick("m1")
        def own(i,_):
            rows=pl.ds(pl.multiple_of(i*W,W),W)
            n2t[:,rows]=n2[rows,:].T
            dh[pl.ds(pl.multiple_of(mine+i*W,W),W),:]=dot(n2[rows,:],wo[...],NT).astype(BF)
            return 0
        lax.fori_loop(0,3,own,0)
        def ograd(k,_):
            rr=pl.ds(pl.multiple_of(k*(Dm//2),Dm//2),Dm//2)
            O.g[0][0,k]=dot(n2t[rr,:],hrecv[...]).reshape(RING,48,H).astype(BF)
            O.g[0][1,k]=dot(n2t[rr,:],heads[pl.ds(mine,R),:]).reshape(RING,48,H).astype(BF)
            return 0
        lax.fori_loop(0,2,ograd,0)
        O.start(0); O.start(1)
        tick("m2")
        c_out.wait()
    V=pltpu.VMEM
    pl.run_scoped(mlp,V((R,Dm),BF),V((Dm,R),BF),V((Dm,R),BF),V((R,Dm),F32),V((R,Dm),F32),V((R,F),BF),V((R,F),BF),V((R,F),BF),
                  V((2,Dm,F),BF),V((2,Dm,F),BF),V((2,F,Dm),BF))

    def attn(qe,ke,ve,cos_o,sin_o,nrm,x_p,wc,nt,doe,kt,dqt,ds_s,dn):
        ld=[pltpu.make_async_copy(s,d,lsem.at[i]) for i,(s,d) in enumerate(((norm_h,nrm),(ke_h,ke),(qe_h,qe),(ve_h,ve),(co_h,cos_o),(si_h,sin_o),(xp_h,x_p)))]
        ld+=[pltpu.make_async_copy(s.at[:,pl.ds(128*q,128)],wc.at[q,:,pl.ds(128*i,128)],lsem.at[12+3*q+i]) for q in range(nh//2) for i,s in enumerate((wq_h,wk_h,wv_h))]
        for q in ld: q.start()
        tick("a0")
        ld[0].wait()
        def tr(i,_):
            c=pl.ds(pl.multiple_of(i*B,B),B)
            nt[:,c]=nrm[c,:].T
            return 0
        lax.fori_loop(0,nb,tr,0)
        tick("a1")
        for q in ld[1:]: q.wait()
        c_dh.wait(); tick("a2")
        l=lanes((B,128)); low=l<64
        causal=lax.broadcasted_iota(jnp.int32,(B,B),0)<=lax.broadcasted_iota(jnp.int32,(B,B),1)
        def pair(p,_):
            cols=pl.ds(pl.multiple_of(p*128,128),128)
            for i in range(nb):
                rows=slice(i*B,(i+1)*B)
                d=dh[rows,cols].astype(F32); o=heads[rows,cols].astype(F32)
                t=d*o
                for hh in range(2):
                    if hh: t=pltpu.roll(t,64,1); d=pltpu.roll(d,64,1)
                    delta=jnp.sum(jnp.where(low,t,0.0),axis=1,keepdims=True)
                    a,b,c=split3(-delta)
                    doe[hh,rows,:]=jnp.where(low,d,jnp.where(l==64,a,jnp.where(l==65,b,jnp.where(l==66,c,0.0)))).astype(BF)
                    kt[hh,:,rows]=ke[2*p+hh,rows,:].T[0:64]
            dqt[...]=jnp.zeros_like(dqt)
            for q in range(3):
                if "p%ds"%q in SCHEDULE:
                    @pl.when(p==q)
                    def _(): tick("p%ds"%q)
            for j in range(nb):
                ks=slice(j*B,(j+1)*B); n0=j*B
                outs=[]
                for hh in range(2):
                    h=2*p+hh
                    s=dot(ke[h,ks,:],qe[h,n0:,:],NT)
                    dp=dot(ve[h,ks,:],doe[hh,n0:,:],NT)
                    sd=jnp.where(causal,s[:,:B],BIG)
                    s=sd if j==nb-1 else jnp.concatenate([sd,s[:,B:]],axis=1)
                    pt=jnp.exp2(s)
                    ds=(pt*dp).astype(BF)
                    pt=pt.astype(BF)
                    dv=dot(pt,doe[hh,n0:,:])
                    dk=dot(ds,qe[h,n0:,:])*LN2
                    dqt[64*hh:64*hh+64,n0:]+=dot(kt[hh,:,ks],ds)
                    outs.append((dk,dv))
                dk=jnp.where(low,outs[0][0],pltpu.roll(outs[1][0],64,1))
                dv=jnp.where(low,outs[0][1],pltpu.roll(outs[1][1],64,1))
                co=cos_o[ks,:]; si=sin_o[ks,:]
                ds_s[p,ks,128:256]=(dk*co-swap32(dk)*si).astype(BF)
                ds_s[p,ks,256:384]=dv.astype(BF)
                for q in range(3):
                    if "p%dj%d"%(q,j) in SCHEDULE:
                        @pl.when(p==q)
                        def _(): tick("p%dj%d"%(q,j))
            for i in range(nb):
                rows=slice(i*B,(i+1)*B)
                dq=dqt[:,rows].T*(HD**-0.5)
                co=cos_o[rows,:]; si=sin_o[rows,:]
                ds_s[p,rows,0:128]=(dq*co-swap32(dq)*si).astype(BF)
            for c in range(2):
                v=dot(nt[c*(Dm//2):(c+1)*(Dm//2),:],ds_s[p])
                C.g[0][p,c]=v.reshape(RING,Dm//16,384).astype(BF)
            C.start(p)
            for q in range(3):
                if "p%de"%q in SCHEDULE:
                    @pl.when(p==q)
                    def _(): tick("p%de"%q)
            return 0
        lax.fori_loop(0,nh//2,pair,0)
        def c_dn(c): return copy_to(snd.at[blk(c)],rcv.at[blk(c)],sems,2+c,{"mp":1-mp})
        def part(r0,xr,c):
            rows=pl.ds(pl.multiple_of(r0,W),W)
            v=dot(ds_s[0,rows,:],wc[0],NT)+dot(ds_s[1,rows,:],wc[1],NT)+dot(ds_s[2,rows,:],wc[2],NT)
            x=xr[blk(c)].astype(F32)
            xr=x*lax.rsqrt(jnp.mean(x*x,axis=1,keepdims=True)+EPS)
            return v, jnp.sum(v*xr,axis=0,keepdims=True)
        gsum=jnp.zeros((1,Dm),F32)
        for c in range(3):
            v,gs=part(theirs+c*W,x_p,c); gsum=gsum+gs
            snd[blk(c)]=v.astype(BF); c_dn(c).start()
            tick("t%d"%c)
        for c in range(3):
            v,gs=part(mine+c*W,x_ref,c); gsum=gsum+gs
            dn[blk(c)]=v
            tick("u%d"%c)
        gx[0,0:1]=gsum
        c_gc=copy_to(gx.at[0],gx.at[1],sems,6,{"core":1-at.core}); c_gc.start()
        tick("g")
        c_gc.wait(); gring[0]=gx[0]+gx[1]
        def c_gr(d,t): return copy_to(gring.at[0 if t==0 else 4*d+t],gring.at[4*d+t+1],sems,7+4*d+t,{"chip":at.nxt[d]})
        c_gr(0,0).start(); c_gr(1,0).start()
        gtot=gring[0]
        for t in range(4):
            for d in range(2):
                if t<4-d:
                    c_gr(d,t).wait()
                    if t+1<4-d: c_gr(d,t+1).start()
                    gtot=gtot+gring[4*d+t+1]
            tick("g%d"%t)
        gx[2]=gtot
        c_gx=copy_to(gx.at[2],gx.at[3],sems,5,{"mp":1-mp}); c_gx.start()
        tick("z")
        for c in range(3):
            c_dn(c).wait()
            r=blk(c)
            d=dn[r]+rcv[r].astype(F32)
            x=x_ref[r].astype(F32)
            i1=lax.rsqrt(jnp.mean(x*x,axis=1,keepdims=True)+EPS)
            s=gain_a[...].astype(F32).reshape(1,-1)*d
            res[r]=res[r]+i1*s-x*(i1*i1*i1)*jnp.mean(s*x,axis=1,keepdims=True)
        c_gx.wait(); gains_out[...]=gx[2]+gx[3]
        c_ig=pltpu.make_async_copy(res,ig_h,lsem.at[11]); c_ig.start()
        M.finish(0); N.finish(0); O.finish(0)
        for v in range(3): C.finish(v)
        c_ig.wait()
    hT=V((nh,T,128),BF)
    pl.run_scoped(attn,hT,hT,hT,V((T,128),F32),V((T,128),F32),V((T,Dm),BF),V((R,Dm),BF),V((nh//2,Dm,H),BF),
                  V((Dm,T),BF),V((2,T,128),BF),V((2,64,T),BF),V((128,T),F32),V((nh//2,T,H),BF),V((R,Dm),F32))

def main_call(x,og,heads,hrecv,wo,wop,gain_a,gain_m,hbm,cid):
    R,Dm=x.shape; T,H=heads.shape
    Vs=pl.BlockSpec(memory_space=pltpu.VMEM); N=pl.BlockSpec(memory_space=pl.ANY); sd=jax.ShapeDtypeStruct; V=pltpu.VMEM
    scs=[s.scratch() for s in (RING_M,RING_N,RING_O,RING_C)]
    local=[V((R,H),BF),V((T,H),BF),V((R,Dm),F32)]+[V((R,Dm),BF)]*2
    local+=[V((4,8,Dm),F32),V((RING,8,Dm),F32),pltpu.SemaphoreType.DMA((2,7+RING)),pltpu.SemaphoreType.DMA((21,)),pltpu.SemaphoreType.DMA((2,3))]
    outs=[sd((R,Dm),F32)]*2+[sd((2,2,RING,48,1536),BF),sd((2,RING,48,H),BF),sd((3,2,RING,48,384),BF),sd((8,Dm),F32)]
    return pl.pallas_call(functools.partial(main_kernel,*[len(s) for s in scs]),
        out_shape=tuple(outs), in_specs=[Vs]*8+[N]*len(hbm), out_specs=(N,)*5+(Vs,),
        scratch_shapes=sum(scs,[])+local,
        compiler_params=pltpu.CompilerParams(collective_id=cid,has_side_effects=True,vmem_limit_bytes=67043328),
        name="mlp_and_backward")(x,og,heads,hrecv,wo,wop,gain_a,gain_m,*hbm)

def widen_kernel(mlp,wo,qkv,y,dx,gains,gate,up,down,out,query,key,value,y_out,dx_out,ga,gm):
    ga[...]=gains[0]; gm[...]=gains[1]
    y_out[...]=y[...]; dx_out[...]=dx[...]
    F=mlp.shape[2]//3; H=wo.shape[1]; B=mlp.shape[1]
    for q in range(2):
        cs=slice(F*q,F*q+F)
        gate[:,cs]=mlp[q,:,0:F].astype(F32)
        up[:,cs]=mlp[q,:,F:2*F].astype(F32)
        down[cs,:]=mlp[q,:,2*F:3*F].astype(F32).T
    out[...]=wo[...].astype(F32).T
    for p in range(qkv.shape[0]):
        cs=slice(128*p,128*p+128)
        query[:,cs]=qkv[p,:,0:128].astype(F32)
        key[:,cs]=qkv[p,:,128:256].astype(F32)
        value[:,cs]=qkv[p,:,256:384].astype(F32)

def widen(mlp,wo,qkv,y,dx,gains):
    Dm,H=wo.shape; F=mlp.shape[2]//3; B=128; P3=qkv.shape[0]
    sd=jax.ShapeDtypeStruct
    row=lambda n: pl.BlockSpec((B,n),lambda i:(i,0))
    rows_spec=pl.BlockSpec((y.shape[0]//(Dm//B),y.shape[1]),lambda i:(i,0))
    col=lambda n: pl.BlockSpec((n,B),lambda i:(0,i))
    return pl.pallas_call(widen_kernel,grid=(Dm//B,),
        out_shape=(sd((Dm,2*F),F32),sd((Dm,2*F),F32),sd((2*F,Dm),F32),sd((H,Dm),F32))+(sd((Dm,H),F32),)*3+(sd(y.shape,F32),)*2+(sd((Dm,),F32),)*2,
        in_specs=[pl.BlockSpec((2,B,3*F),lambda i:(0,i,0)),row(H),pl.BlockSpec((P3,B,H),lambda i:(0,i,0)),rows_spec,rows_spec,pl.BlockSpec((8,Dm),lambda i:(0,0))],
        out_specs=(row(2*F),row(2*F),col(2*F),col(H),row(H),row(H),row(H),rows_spec,rows_spec)+(pl.BlockSpec((Dm,),lambda i:(0,)),)*2,
        compiler_params=pltpu.CompilerParams(vmem_limit_bytes=67043328),name="widen")(mlp,wo,qkv,y,dx,gains)


def on_device(layer_input, gain_attn, w_query, w_key, w_value, w_out, gain_mlp, w_gate, w_up, w_down,
              segment_start, segment_parent, out_grad):
    weights = (w_out, w_gate, w_up, w_down)
    x_peer, normed, cosine, sine, ke, ve, qe, heads, heads_peer, peer_out, peer_gate, peer_up, peer_down = front(
        layer_input, gain_attn, w_query, w_key, w_value, segment_start, segment_parent, weights, 2
    )
    output, input_grad, mlp_g, out_g, qkv_g, gain_g = main_call(
        layer_input, out_grad, heads, heads_peer, w_out, peer_out, gain_attn, gain_mlp,
        (w_gate, w_up, w_down, peer_gate, peer_up, peer_down, qe, ke, ve, cosine, sine, normed, x_peer,
         w_query, w_key, w_value), 1,
    )
    sums = [mlp_g.reshape(2, -1, mlp_g.shape[-1]), out_g.reshape(-1, out_g.shape[-1]), qkv_g.reshape(3, -1, qkv_g.shape[-1]), gain_g]
    if lax.axis_size("grp") > 1:
        sums = lax.psum([s.astype(F32) for s in sums], "grp")
    mlp_g, out_g, qkv_g, gain_g = sums
    gate_g, up_g, down_g, out_g, query_g, key_g, value_g, output, input_grad, gain_attn_grad, gain_mlp_grad = widen(
        mlp_g, out_g, qkv_g, output, input_grad, gain_g
    )
    return (
        output, input_grad, gain_attn_grad, query_g, key_g, value_g, out_g, gain_mlp_grad, gate_g, up_g, down_g,
    )


def solution(mesh):
    fine = Mesh(mesh.devices.reshape(-1, RING, 2, mesh.shape["mp"]), ("grp", "chip", "core", "mp"))
    dp = ("grp", "chip", "core")
    tok, col, row, tree = P(dp + ("mp",), None), P(None, "mp"), P("mp", None), P(dp, None)
    in_specs = (tok, P(), col, col, col, row, P(), col, col, row, tree, tree, tok)
    out_specs = (tok, tok, P(), col, col, col, row, P(), col, col, row)
    return jax.shard_map(on_device, mesh=fine, in_specs=in_specs, out_specs=out_specs, check_vma=False)
```

```python
import functools
import math

import jax
import jax.numpy as jnp
from jax import lax
from jax.experimental import pallas as pl
from jax.experimental.pallas import tpu as pltpu
from jax.sharding import Mesh
from jax.sharding import PartitionSpec as P

BF = jnp.bfloat16
F32 = jnp.float32
HD=64; EPS=1e-5; BIG=-1e30
C_Q = (HD**-0.5)*math.log2(math.e)
LN2 = math.log(2.0)
NT=(((1,),(1,)),((),())); NN=(((1,),(0,)),((),())); TN=(((0,),(0,)),((),()))
def dot(a,b,dims=NN): return lax.dot_general(a,b,dims,preferred_element_type=F32)
def lanes(shape): return lax.broadcasted_iota(jnp.int32, shape, 1)

def split3(x):
    hi=x.astype(BF).astype(F32); r=x-hi; mid=r.astype(BF).astype(F32); lo=r-mid
    return hi,mid,lo

def tables(starts, parents, row0, rows, nseg, tree_len):
    sh=(rows,128)
    t = row0 + lax.broadcasted_iota(jnp.int32, sh, 0)
    st=[starts[0,s] for s in range(nseg)]+[tree_len]
    par=[parents[0,s] for s in range(nseg)]
    ln=[st[s+1]-st[s] for s in range(nseg)]
    def pick(vals, idx):
        r = vals[0]
        for s in range(1,nseg): r = jnp.where(idx==s, vals[s], r)
        return r
    D=[]
    gps=[]
    for s in range(nseg):
        p=par[s]; gp=pick(par,p); gps.append(gp)
        off=jnp.where(p!=s, pick(ln,p), 0)+jnp.where((gp!=s)&(gp!=p), pick(ln,gp), 0)
        D.append(off-st[s])
    seg=jnp.zeros(sh,jnp.int32); pos=t+D[0]
    for s in range(1,nseg):
        ge=t>=st[s]
        seg=seg+ge.astype(jnp.int32)
        pos=pos+jnp.where(ge, D[s]-D[s-1], 0)
    f=lanes(sh)-64
    parl=jnp.zeros((1,128),jnp.int32)-1; gpl=parl
    fl=lanes((1,128))-64
    for s in range(nseg):
        parl=jnp.where(fl==s, par[s], parl); gpl=jnp.where(fl==s, gps[s], gpl)
    vis=(f==seg)|(parl==seg)|(gpl==seg)|(f<0)|(f>=nseg)
    qf=jnp.where(f==seg,1.0,0.0)
    kf=jnp.where(vis,0.0,BIG)
    kf=jnp.where((f>=8)&(f<11),1.0,kf)
    return pos.astype(F32), qf, kf

def rot_tables(posf):
    l=lax.broadcasted_iota(jnp.int32,(1,128),1)
    fr=jnp.exp((l%32).astype(F32)*(-2.0*math.log(10000.0)/HD))
    ang=posf*fr
    sg=jnp.where((l%64)<32,-1.0,1.0)
    return jnp.cos(ang), jnp.sin(ang)*sg

def swap32(x):
    l=lanes(x.shape)
    return jnp.where((l&32)==0, pltpu.roll(x,96,1), pltpu.roll(x,32,1))


MESH=pl.DeviceIdType.MESH
RING=8
def ring_chip(r):
    return jnp.where(r<RING//2, 2*r, 2*(RING-1-r)+1)
def chip_ring(n):
    return jnp.where(n%2==0, n//2, RING-1-n//2)

class Place:
    def __init__(self):
        self.core=lax.axis_index("core"); self.mp=lax.axis_index("mp")
        self.pos=chip_ring(lax.axis_index("chip"))
        self.nxt=[ring_chip(lax.rem(self.pos+1,RING)), ring_chip(lax.rem(self.pos+RING-1,RING))]
    def barrier(self):
        b=pltpu.get_barrier_semaphore()
        ds=[{"core":1-self.core},{"mp":1-self.mp},{"chip":self.nxt[0]},{"chip":self.nxt[1]}]
        for d in ds: pl.semaphore_signal(b, inc=1, device_id=d, device_id_type=MESH)
        return lambda: pl.semaphore_wait(b, len(ds))

def copy_to(src,dst,sems,k,dev):
    return pltpu.make_async_remote_copy(src,dst,sems.at[0,k],sems.at[1,k],device_id=dev,device_id_type=MESH)

class Gather:
    def __init__(self,p,src,out,kinds,sems):
        self.p,self.src,self.out,self.kinds,self.sems=p,src,out,kinds,sems
    def ref(self,x,a,ch,core=None):
        n=self.out[a].shape[0]//(2*RING)
        return x[a].at[pl.ds(pl.multiple_of((self.p.core*RING+ch)*n,n),n)]
    def at(self,d,dist): return lax.rem(self.p.pos+(dist if d==0 else RING-dist),RING)
    def hops(self,a,d): return 4-self.kinds[a] if d==0 else 3+self.kinds[a]
    def cp(self,src,dst,a,k,dev):
        return pltpu.make_async_remote_copy(src,dst,self.sems.at[0,a,k],self.sems.at[1,a,k],device_id=dev,device_id_type=MESH)
    def cx(self,a): return self.cp(self.ref(self.src,a,self.p.pos),self.ref(self.out,a,self.p.pos),a,0,{"mp":1-self.p.mp})
    def cag(self,a,d,t):
        r=self.ref(self.out,a,self.at(1-d,t))
        return self.cp(r,r,a,1+4*d+t,{"chip":self.p.nxt[d]})
    def cfc(self,a,d,t):
        r=self.ref(self.out,a,self.at(1-d,t+1))
        return self.cp(r,r,a,9+4*d+t,{"core":1-self.p.core})
    def cfo(self,a):
        r=self.ref(self.out,a,self.p.pos)
        return self.cp(r,r,a,17,{"core":1-self.p.core})
    def agstart(self,a):
        self.cx(a).wait()
        for d in range(2): self.cag(a,d,0).start()
        self.cfo(a).start()
    def ag(self,a,t):
        for d in range(2):
            if t<self.hops(a,d):
                self.cag(a,d,t).wait()
                if t+1<self.hops(a,d): self.cag(a,d,t+1).start()
                self.cfc(a,d,t).start()
    def finish(self,a):
        self.cfo(a).wait()
        for d in range(2):
            for t in range(self.hops(a,d)): self.cfc(a,d,t).wait()

def front_kernel(nseg,starts,parents,x_ref,gain,wq,wk,wv,*refs):
    refs=list(refs)
    def take(n):
        r=refs[:n]; del refs[:n]; return r
    NW=(len(refs)-21)//2
    src=take(NW)
    big=take(7); heads,hrecv=take(2); out=take(NW)
    x_peer,normed,cos_o,sin_o,ke,ve,qe,qf_s,kf_s,sems,wsems,osem=take(12)
    at=Place(); mp=at.mp
    R=x_ref.shape[0]; T=2*R; B=256; nh=wq.shape[1]//HD
    G=Gather(at,src,out,[a%2 for a in range(NW)],wsems)
    mine=pl.multiple_of(mp*R,R); theirs=pl.multiple_of((1-mp)*R,R)
    at.barrier()()
    peer={"mp":1-mp}
    NG=NW
    for a in range(NG): G.cx(a).start()
    c_x=copy_to(x_ref,x_peer,sems,0,peer); c_x.start()
    for a in range(NG,NW): G.cx(a).start()
    def tab(c,_):
        r0=pl.multiple_of(c*B,B); rows=pl.ds(r0,B)
        posf,qf,kf=tables(starts,parents,r0,B,nseg,T)
        co,si=rot_tables(posf)
        cos_o[rows,:]=co; sin_o[rows,:]=si
        qf_s[rows,:]=qf.astype(BF); kf_s[rows,:]=kf.astype(BF)
        return 0
    lb=lanes((B,128)); low=lb<64
    vone=jnp.where((lb>=64)&(lb<67),1.0,0.0)
    def proj(xr,base):
        def f(c,_):
            rows=pl.ds(pl.multiple_of(base+c*B,B),B)
            x=xr[pl.ds(pl.multiple_of(c*B,B),B),:].astype(F32)
            r1=lax.rsqrt(jnp.mean(x*x,axis=1,keepdims=True)+EPS)
            n=(x*r1*gain[...].astype(F32).reshape(1,-1)).astype(BF)
            normed[rows,:]=n
            co=cos_o[rows,:]; si=sin_o[rows,:]; qf=qf_s[rows,:].astype(F32); kf=kf_s[rows,:].astype(F32)
            qq=dot(n,wq[...]); kk=dot(n,wk[...]); vv=dot(n,wv[...])
            for p in range(nh//2):
                cs=slice(128*p,128*p+128)
                q=qq[:,cs]; k=kk[:,cs]; v=vv[:,cs]
                q=(q*co+swap32(q)*si)*C_Q; k=k*co+swap32(k)*si
                for hh in range(2):
                    if hh: q=pltpu.roll(q,64,1); k=pltpu.roll(k,64,1); v=pltpu.roll(v,64,1)
                    qe[2*p+hh,rows,:]=jnp.where(low,q,qf).astype(BF)
                    ke[2*p+hh,rows,:]=jnp.where(low,k,kf).astype(BF)
                    ve[2*p+hh,rows,:]=jnp.where(low,v,vone).astype(BF)
            return 0
        lax.fori_loop(0,R//B,f,0)
    for a in range(NG): G.agstart(a)
    lax.fori_loop(0,T//B,tab,0)
    for a in range(NG): G.ag(a,0)
    proj(x_ref,mine)
    for a in range(NG): G.ag(a,1)
    c_x.wait()
    proj(x_peer,theirs)
    puts=[pltpu.make_async_copy(s,d,osem.at[i]) for i,(s,d) in enumerate(zip((x_peer,normed,cos_o,sin_o,ke,ve),big))]
    for q in puts: q.start()
    for a in range(NG): G.ag(a,2)
    def put_q(p): return pltpu.make_async_copy(qe.at[pl.ds(2*p,2)],big[6].at[pl.ds(2*p,2)],osem.at[6+p])
    causal=lax.broadcasted_iota(jnp.int32,(B,B),1)<=lax.broadcasted_iota(jnp.int32,(B,B),0)
    NB=R//B
    def c_h(p,q):
        cs=pl.ds(pl.multiple_of(p*128,128),128)
        return pltpu.make_async_remote_copy(heads.at[pl.ds(pl.multiple_of(theirs+q*B,B),B),cs],hrecv.at[pl.ds(q*B,B),cs],sems.at[0,1+NB*p+q],sems.at[1,1+NB*p+q],device_id=peer,device_id_type=MESH)
    def attend(p,_):
        cs=pl.ds(pl.multiple_of(p*128,128),128)
        for i in range(T//B):
            n=(i+1)*B; rows=slice(i*B,(i+1)*B)
            outs=[]
            for hh in range(2):
                h=2*p+hh
                q=qe[h,rows,:]
                s=dot(q,ke[h,0:n,:],NT)
                sd=jnp.where(causal,s[:,n-B:],BIG)
                s=sd if i==0 else jnp.concatenate([s[:,:n-B],sd],axis=1)
                m=jnp.max(s,axis=1,keepdims=True)
                pr=jnp.exp2(s-m).astype(BF)
                o=dot(pr,ve[h,0:n,:])
                den=o[:,64:65]
                o=o*(1.0/den)
                a,b,c=split3(-(m+jnp.log2(den)))
                qe[h,rows,:]=jnp.where(lb==72,a,jnp.where(lb==73,b,jnp.where(lb==74,c,q.astype(F32)))).astype(BF)
                outs.append(o)
            heads[rows,cs]=jnp.where(low,outs[0],pltpu.roll(outs[1],64,1)).astype(BF)
            @pl.when(1-mp==i//NB)
            def _(): c_h(p,i%NB).start()
            if i==3:
                @pl.when(p==2)
                def _():
                    for a in range(NG): G.ag(a,3)
        put_q(p).start()
        return 0
    lax.fori_loop(0,nh//2,attend,0)
    for a in range(NW): G.finish(a)
    for q in puts: q.wait()
    for p in range(nh//2): put_q(p).wait()
    for p in range(nh//2):
        for q in range(NB): c_h(p,q).wait()

def front(x,gain,wq,wk,wv,starts,parents,weights,cid):
    R,Dm=x.shape; T=2*R; H=wq.shape[1]; nh=H//HD; nseg=starts.shape[1]; NW=len(weights)
    Vs=pl.BlockSpec(memory_space=pltpu.VMEM); S=pl.BlockSpec(memory_space=pltpu.SMEM); N=pl.BlockSpec(memory_space=pl.ANY)
    sd=jax.ShapeDtypeStruct; hT=sd((nh,T,128),BF); V=pltpu.VMEM
    return pl.pallas_call(functools.partial(front_kernel,nseg),
        out_shape=(sd((R,Dm),BF),sd((T,Dm),BF),sd((T,128),F32),sd((T,128),F32),hT,hT,hT,sd((T,H),BF),sd((R,H),BF))+tuple(sd(w.shape,BF) for w in weights),
        in_specs=[S,S]+[Vs]*5+[N]*NW, out_specs=(N,)*7+(Vs,)*2+(N,)*NW,
        scratch_shapes=[V((R,Dm),BF),V((T,Dm),BF),V((T,128),F32),V((T,128),F32),V((nh,T,128),BF),V((nh,T,128),BF),V((nh,T,128),BF),V((T,128),BF),V((T,128),BF),
            pltpu.SemaphoreType.DMA((2,1+(nh//2)*(R//256))),pltpu.SemaphoreType.DMA((2,NW,18)),pltpu.SemaphoreType.DMA((6+nh//2,))],
        compiler_params=pltpu.CompilerParams(collective_id=cid,has_side_effects=True,vmem_limit_bytes=67043328),
        name="attention_forward")(starts,parents,x,gain,wq,wk,wv,*weights)

class Ring:
    def __init__(self, shapes, kinds, count, gslots, swaps, early=True, slot=None):
        self.shapes,self.count,self.gslots,self.swaps,self.early=shapes,count,gslots,swaps,early
        self.slot=slot or (lambda u: lax.rem(u,gslots))
        self.nr=(len(swaps) if early else count) if swaps else count
        self.na=len(shapes); self.flows=[]
        for a,parts in enumerate(kinds):
            for c0,nc,k in parts:
                self.flows+=[(a,c0,nc,0,4-k),(a,c0,nc,1,3+k)]
        self.nf=len(self.flows)
        self.own=[s[0] for s in swaps] if swaps else list(range(count))
        self.nv=len(self.own)
        na,nf=self.na,self.nf
        self.k_rs=na; self.k_x=0; self.k_ag=na; self.k_fc=self.k_ag+4*nf; self.k_fo=self.k_fc+4*nf; self.k_put=self.k_fo+na
        self.n1=na+4*nf; self.n2=self.k_put+na
    def scratch(self):
        V=pltpu.VMEM; U=self.count
        s=[V((self.gslots,2,RING)+x,BF) for x in self.shapes] if self.gslots else []
        s+=[V((U,RING)+x,BF) for x in self.shapes]
        s+=[V((self.nr,)+x,BF) for x in self.shapes]
        s+=[V((self.nv,)+((RING,)+x if self.early else x),BF) for x in self.shapes] if self.swaps else []
        s+=[V((self.nr,h,self.shapes[a][0],nc),BF) for a,c0,nc,d,h in self.flows]
        return s+[pltpu.SemaphoreType.DMA((2,U,self.n1)),pltpu.SemaphoreType.DMA((2,self.nv,self.n2))]
    def bind(self,p,dst,sc,g=None):
        self.p,self.dst=p,dst
        sc=list(sc); na=self.na
        if g is None: g,sc=sc[:na],sc[na:]
        self.g=g; self.r=sc[:na]; self.fin=sc[na:2*na]; sc=sc[2*na:]
        if self.swaps: self.xr=sc[:na]; sc=sc[na:]
        self.arr=sc[:self.nf]; self.sem,self.sem2=sc[self.nf:]
        return self
    def at(self,d,dist):
        return lax.rem(self.p.pos+(dist if d==0 else RING-dist),RING)
    def cp(self,src,dst,u,k,dev):
        return pltpu.make_async_remote_copy(src,dst,self.sem.at[0,u,k],self.sem.at[1,u,k],device_id=dev,device_id_type=MESH)
    def cp2(self,src,dst,v,k,dev):
        return pltpu.make_async_remote_copy(src,dst,self.sem2.at[0,v,k],self.sem2.at[1,v,k],device_id=dev,device_id_type=MESH)
    def c1(self,u,a): return self.cp(self.g[a].at[self.slot(u),1-self.p.core],self.r[a].at[u],u,a,{"core":1-self.p.core})
    def start(self,u):
        for a in range(self.na): self.c1(u,a).start()
    def uown(self,v): return self.own[v] if self.swaps else v
    def u_of(self,w): return self.uown(w) if self.early else w
    def w_own(self,v): return v if self.early else self.uown(v)
    def crs(self,w,f,t):
        a,c0,nc,d,h=self.flows[f]
        src=self.r[a].at[self.u_of(w),self.at(d,h),:,pl.ds(c0,nc)] if t==0 else self.arr[f].at[w,t-1]
        return self.cp(src,self.arr[f].at[w,t],self.u_of(w),self.k_rs+4*f+t,{"chip":self.p.nxt[d]})
    def cx(self,v,a): return self.cp2(self.r[a].at[self.swaps[v][1]] if self.early else self.fin[a].at[self.swaps[v][1]],self.xr[a].at[v],v,self.k_x+a,{"mp":1-self.p.mp})
    def push(self,v):
        u=self.swaps[v][1]
        for a in range(self.na):
            self.c1(u,a).wait()
            r,g=self.r[a],self.g[a]
            def add(s,_):
                r[u,s]=r[u,s]+g[self.slot(u),self.p.core,s]; return 0
            lax.fori_loop(0,RING,add,0)
            self.cx(v,a).start()
    def xstart(self,v):
        for a in range(self.na): self.cx(v,a).start()
    def first(self,v):
        u=self.u_of(v)
        for a in range(self.na):
            self.c1(u,a).wait()
            if self.swaps and self.early: self.cx(v,a).wait()
            r,g=self.r[a],self.g[a]
            def add(s,_):
                t=r[u,s].astype(F32)+g[self.slot(u),self.p.core,s].astype(F32)
                if self.swaps and self.early: t=t+self.xr[a][v,s].astype(F32)
                r[u,s]=t.astype(BF); return 0
            lax.fori_loop(0,RING,add,0)
            for f in range(self.nf):
                if self.flows[f][0]==a: self.crs(v,f,0).start()
    def rs(self,v,t):
        u=self.u_of(v)
        for f,(a,c0,nc,d,h) in enumerate(self.flows):
            if t<h:
                self.crs(v,f,t).wait()
                if t+1<h:
                    self.arr[f][v,t]=self.arr[f][v,t]+self.r[a][u,self.at(d,h-t-1),:,pl.ds(c0,nc)]
                    self.crs(v,f,t+1).start()
        if t==3:
            for f in range(0,self.nf,2):
                a,c0,nc,d,h=self.flows[f]; h2=self.flows[f+1][4]
                w=self.r[a][u,self.p.pos,:,pl.ds(c0,nc)].astype(F32)+self.arr[f][v,h-1].astype(F32)+self.arr[f+1][v,h2-1].astype(F32)
                self.fin[a][v,:,pl.ds(c0,nc)]=w.astype(BF)
    def cag(self,v,f,t):
        a,c0,nc,d,h=self.flows[f]
        dst=self.dst(v,a,self.at(1-d,t)).at[:,pl.ds(c0,nc)]
        src=self.fin[a].at[self.w_own(v),:,pl.ds(c0,nc)] if t==0 else dst
        return self.cp2(src,dst,v,self.k_ag+4*f+t,{"chip":self.p.nxt[d]})
    def cfc(self,v,f,t):
        a,c0,nc,d,h=self.flows[f]
        ref=self.dst(v,a,self.at(1-d,t+1)).at[:,pl.ds(c0,nc)]
        return self.cp2(ref,ref,v,self.k_fc+4*f+t,{"core":1-self.p.core})
    def cfo(self,v,a): return self.cp2(self.fin[a].at[self.w_own(v)],self.dst(v,a,self.p.pos),v,self.k_fo+a,{"core":1-self.p.core})
    def put(self,v,a): return pltpu.make_async_copy(self.fin[a].at[self.w_own(v)],self.dst(v,a,self.p.pos),self.sem2.at[0,v,self.k_put+a])
    def agstart(self,v):
        for a in range(self.na):
            if not self.early:
                u=self.uown(v)
                self.cx(v,a).wait()
                self.fin[a][u]=self.fin[a][u]+self.xr[a][v]
            for f in range(self.nf):
                if self.flows[f][0]==a: self.cag(v,f,0).start()
            self.cfo(v,a).start(); self.put(v,a).start()
    def ag(self,v,t):
        for f,(a,c0,nc,d,h) in enumerate(self.flows):
            if t<h:
                self.cag(v,f,t).wait()
                if t+1<h: self.cag(v,f,t+1).start()
                self.cfc(v,f,t).start()
    def finish(self,v):
        for a in range(self.na):
            self.put(v,a).wait(); self.cfo(v,a).wait()
        for f,(a,c0,nc,d,h) in enumerate(self.flows):
            for t in range(h): self.cfc(v,f,t).wait()

SHAPES_M,KINDS_M=[(48,1536)],[[(0,768,0),(768,768,1)]]
RING_M=Ring(SHAPES_M,KINDS_M,2,2,[(1,0)],True,lambda u: 0)
RING_N=Ring(SHAPES_M,KINDS_M,2,0,[(1,0)],False,lambda u: 1)
RING_O=Ring([(48,384)],[[(0,256,0),(256,128,1)]],2,2,[(1,0)])
RING_C=Ring([(48,384)],[[(0,256,0),(256,128,1)]],3,3,[])
SCHEDULE={
"m1":[("N","rs",0,2),("M","first",0)],
"m2":[("N","rs",0,3),("N","xstart",0),("N","first",1)],
"a0":[("M","rs",0,0),("O","push",0)],
"a1":[("N","rs",1,0),("M","rs",0,1)],
"a2":[("N","rs",1,1)],
"p0s":[("M","rs",0,2)],
"p0j0":[("N","rs",1,2)],
"p0j1":[("O","first",0)],
"p0j3":[("M","rs",0,3),("M","agstart",0)],
"p0e":[("N","rs",1,3),("N","agstart",0)],
"p1j0":[("C","first",0),("O","rs",0,0)],
"p1j1":[("M","ag",0,0)],
"p1j3":[("C","rs",0,0),("N","ag",0,0)],
"p1e":[("O","rs",0,1)],
"p2s":[("M","ag",0,1)],
"p2j0":[("C","first",1),("C","rs",0,1),("N","ag",0,1)],
"p2j1":[("O","rs",0,2)],
"p2j3":[("C","rs",1,0),("M","ag",0,2)],
"p2e":[("C","rs",0,2),("O","rs",0,3),("O","agstart",0)],
"t0":[("C","rs",0,3),("C","agstart",0),("C","rs",1,1),("N","ag",0,2)],
"t1":[("C","first",2),("O","ag",0,0)],
"t2":[("C","rs",1,2)],
"u0":[("C","rs",2,0),("C","ag",0,0)],
"u1":[("C","rs",1,3),("C","agstart",1),("O","ag",0,1)],
"g":[("C","rs",2,1),("C","ag",0,1),("O","ag",0,2)],
"g0":[("C","rs",2,2),("C","ag",1,0),("C","ag",0,2)],
"g1":[("C","rs",2,3),("C","agstart",2),("C","ag",1,1)],
"g2":[("C","ag",2,0),("C","ag",1,2),("M","ag",0,3)],
"g3":[("C","ag",2,1),("N","ag",0,3)],
"z":[("C","ag",2,2),("C","ag",0,3),("C","ag",1,3),("O","ag",0,3),("C","ag",2,3)],
}
def main_kernel(nM,nN,nO,nC,*refs):
    refs=list(refs)
    def take(n):
        r=refs[:n]; del refs[:n]; return r
    x_ref,og,heads,hrecv,wo,wop,gain_a,gain_m=take(8)
    wg_h,wu_h,wd_h,wgp_h,wup_h,wdp_h,qe_h,ke_h,ve_h,co_h,si_h,norm_h,xp_h,wq_h,wk_h,wv_h=take(16)
    out_h,ig_h=take(2); outM=take(1); outO=take(1); outC=take(1); gains_out,=take(1)
    scM=take(nM); scN=take(nN); scO=take(nO); scC=take(nC)
    dhs,dh,res,snd,rcv,gx,gring,sems,lsem,wsem=take(10)
    at=Place(); mp=at.mp
    R,Dm=x_ref.shape; T=2*R; nh=qe_h.shape[0]; B=256; nb=T//B; H=wo.shape[0]; F=512
    core=at.core
    rings={}
    def tick(site):
        for name,op,*args in SCHEDULE.get(site,()): getattr(rings[name],op)(*args)
    def dst_m(q): return lambda v,a,ch: outM[0].at[q,core,ch]
    def dst_c(v,a,ch): return outC[0].at[v,core,ch]
    M=RING_M.bind(at,dst_m(0),scM); N=RING_N.bind(at,dst_m(1),scN,M.g); O=RING_O.bind(at,lambda v,a,ch: outO[0].at[core,ch],scO); C=RING_C.bind(at,dst_c,scC)
    rings.update(M=M,N=N,O=O,C=C)
    mine=pl.multiple_of(mp*R,R); theirs=pl.multiple_of((1-mp)*R,R)
    W=R//3
    def blk(i): return pl.ds(i*W,W)
    arrived=at.barrier()
    c_dh=copy_to(dhs,dh.at[pl.ds(mine,R)],sems,0,{"mp":1-mp})

    def mlp(n2,n2t,ogt,acc,dn2,hid,dg,du,wgb,wub,wdb):
        def loads(g,u,d,q,slot):
            cs=pl.ds(pl.multiple_of(q*F,F),F)
            return [pltpu.make_async_copy(g.at[:,cs],wgb.at[slot],wsem.at[slot,0]),
                    pltpu.make_async_copy(u.at[:,cs],wub.at[slot],wsem.at[slot,1]),
                    pltpu.make_async_copy(d.at[cs,:],wdb.at[slot],wsem.at[slot,2])]
        for q in loads(wgp_h,wup_h,wdp_h,0,0): q.start()
        def pre(i,_):
            rows=pl.ds(pl.multiple_of(i*W,W),W); mr=pl.ds(pl.multiple_of(mine+i*W,W),W)
            r=x_ref[rows,:].astype(F32)+dot(heads[mr,:],wo[...])+dot(hrecv[rows,:],wop[...])
            res[rows,:]=r
            n=(r*lax.rsqrt(jnp.mean(r*r,axis=1,keepdims=True)+EPS)*gain_m[...].astype(F32).reshape(1,-1)).astype(BF)
            n2[rows,:]=n
            n2t[:,rows]=n.T
            ogt[:,rows]=og[rows,:].T
            return 0
        lax.fori_loop(0,3,pre,0)
        arrived()
        acc[...]=jnp.zeros_like(acc); dn2[...]=jnp.zeros_like(dn2)
        def step(c,_):
            slot=lax.rem(c,2)
            for q in loads(wg_h,wu_h,wd_h,0,slot): q.wait()
            @pl.when(c==0)
            def _():
                for q in loads(wgp_h,wup_h,wdp_h,1,1): q.start()
            @pl.when((c>0)&(c<3))
            def _():
                for q in loads(wg_h,wu_h,wd_h,c-1,1-slot): q.start()
            wg,wu,wd=wgb[slot],wub[slot],wdb[slot]
            def half(i,_):
                rows=pl.ds(pl.multiple_of(i*W,W),W)
                gate=dot(n2[rows,:],wgb[slot]); up=dot(n2[rows,:],wub[slot]); dhid=dot(og[rows,:],wdb[slot],NT)
                sg=1.0/(1.0+jnp.exp(-gate)); silu=gate*sg
                hid[rows,:]=(silu*up).astype(BF)
                dg[rows,:]=(dhid*up*sg*(1.0+gate*(1.0-sg))).astype(BF)
                du[rows,:]=(dhid*silu).astype(BF)
                return 0
            lax.fori_loop(0,3,half,0)
            @pl.when(c==1)
            def _(): M.push(0)
            @pl.when(c==2)
            def _(): N.first(0)
            def back(i,_):
                rows=pl.ds(pl.multiple_of(i*W,W),W)
                acc[rows,:]=acc[rows,:]+dot(hid[rows,:],wdb[slot])
                dn2[rows,:]=dn2[rows,:]+(dot(dg[rows,:],wgb[slot],NT)+dot(du[rows,:],wub[slot],NT))
                return 0
            lax.fori_loop(0,3,back,0)
            @pl.when(c==3)
            def _(): N.rs(0,1)
            def wgrad(k,_):
                rr=pl.ds(pl.multiple_of(k*(Dm//2),Dm//2),Dm//2)
                M.g[0][slot,k,:,:,0:F]=dot(n2t[rr,:],dg[...]).reshape(RING,48,F).astype(BF)
                M.g[0][slot,k,:,:,F:2*F]=dot(n2t[rr,:],du[...]).reshape(RING,48,F).astype(BF)
                M.g[0][slot,k,:,:,2*F:3*F]=dot(ogt[rr,:],hid[...]).reshape(RING,48,F).astype(BF)
                return 0
            lax.fori_loop(0,2,wgrad,0)
            @pl.when(lax.rem(c,2)==0)
            def _(): M.start(c//2)
            @pl.when(lax.rem(c,2)==1)
            def _(): N.start(c//2)
            @pl.when(c==2)
            def _(): N.rs(0,0)
            return 0
        lax.fori_loop(0,4,step,0)
        tick("m0")
        gx[...]=jnp.zeros_like(gx)
        def post(i,gpart):
            rows=pl.ds(pl.multiple_of(i*W,W),W)
            r=res[rows,:]; d=dn2[rows,:]
            snd[rows,:]=(acc[rows,:]+r).astype(BF)
            i2=lax.rsqrt(jnp.mean(r*r,axis=1,keepdims=True)+EPS)
            s=gain_m[...].astype(F32).reshape(1,-1)*d
            dr=og[rows,:].astype(F32)+i2*s-r*(i2*i2*i2)*jnp.mean(s*r,axis=1,keepdims=True)
            res[rows,:]=dr
            da=dr.astype(BF)
            n2[rows,:]=da
            dhs[rows,:]=dot(da,wop[...],NT).astype(BF)
            return gpart+jnp.sum(d*r*i2,axis=0,keepdims=True)
        gpart=lax.fori_loop(0,3,post,jnp.zeros((1,Dm),F32))
        c_dh.start()
        c_out=pltpu.make_async_copy(snd,out_h,lsem.at[10]); c_out.start()
        gx[0,1:2]=gpart
        tick("m1")
        def own(i,_):
            rows=pl.ds(pl.multiple_of(i*W,W),W)
            n2t[:,rows]=n2[rows,:].T
            dh[pl.ds(pl.multiple_of(mine+i*W,W),W),:]=dot(n2[rows,:],wo[...],NT).astype(BF)
            return 0
        lax.fori_loop(0,3,own,0)
        def ograd(k,_):
            rr=pl.ds(pl.multiple_of(k*(Dm//2),Dm//2),Dm//2)
            O.g[0][0,k]=dot(n2t[rr,:],hrecv[...]).reshape(RING,48,H).astype(BF)
            O.g[0][1,k]=dot(n2t[rr,:],heads[pl.ds(mine,R),:]).reshape(RING,48,H).astype(BF)
            return 0
        lax.fori_loop(0,2,ograd,0)
        O.start(0); O.start(1)
        tick("m2")
        c_out.wait()
    V=pltpu.VMEM
    pl.run_scoped(mlp,V((R,Dm),BF),V((Dm,R),BF),V((Dm,R),BF),V((R,Dm),F32),V((R,Dm),F32),V((R,F),BF),V((R,F),BF),V((R,F),BF),
                  V((2,Dm,F),BF),V((2,Dm,F),BF),V((2,F,Dm),BF))

    def attn(qe,ke,ve,cos_o,sin_o,nrm,x_p,wc,nt,doe,kt,dqt,ds_s,dn):
        ld=[pltpu.make_async_copy(s,d,lsem.at[i]) for i,(s,d) in enumerate(((norm_h,nrm),(ke_h,ke),(qe_h,qe),(ve_h,ve),(co_h,cos_o),(si_h,sin_o),(xp_h,x_p)))]
        ld+=[pltpu.make_async_copy(s.at[:,pl.ds(128*q,128)],wc.at[q,:,pl.ds(128*i,128)],lsem.at[12+3*q+i]) for q in range(nh//2) for i,s in enumerate((wq_h,wk_h,wv_h))]
        for q in ld: q.start()
        tick("a0")
        ld[0].wait()
        def tr(i,_):
            c=pl.ds(pl.multiple_of(i*B,B),B)
            nt[:,c]=nrm[c,:].T
            return 0
        lax.fori_loop(0,nb,tr,0)
        tick("a1")
        for q in ld[1:]: q.wait()
        c_dh.wait(); tick("a2")
        l=lanes((B,128)); low=l<64
        causal=lax.broadcasted_iota(jnp.int32,(B,B),0)<=lax.broadcasted_iota(jnp.int32,(B,B),1)
        def pair(p,_):
            cols=pl.ds(pl.multiple_of(p*128,128),128)
            for i in range(nb):
                rows=slice(i*B,(i+1)*B)
                d=dh[rows,cols].astype(F32); o=heads[rows,cols].astype(F32)
                t=d*o
                for hh in range(2):
                    if hh: t=pltpu.roll(t,64,1); d=pltpu.roll(d,64,1)
                    delta=jnp.sum(jnp.where(low,t,0.0),axis=1,keepdims=True)
                    a,b,c=split3(-delta)
                    doe[hh,rows,:]=jnp.where(low,d,jnp.where(l==64,a,jnp.where(l==65,b,jnp.where(l==66,c,0.0)))).astype(BF)
                    kt[hh,:,rows]=ke[2*p+hh,rows,:].T[0:64]
            dqt[...]=jnp.zeros_like(dqt)
            for q in range(3):
                if "p%ds"%q in SCHEDULE:
                    @pl.when(p==q)
                    def _(): tick("p%ds"%q)
            for j in range(nb):
                ks=slice(j*B,(j+1)*B); n0=j*B
                outs=[]
                for hh in range(2):
                    h=2*p+hh
                    s=dot(ke[h,ks,:],qe[h,n0:,:],NT)
                    dp=dot(ve[h,ks,:],doe[hh,n0:,:],NT)
                    sd=jnp.where(causal,s[:,:B],BIG)
                    s=sd if j==nb-1 else jnp.concatenate([sd,s[:,B:]],axis=1)
                    pt=jnp.exp2(s)
                    ds=(pt*dp).astype(BF)
                    pt=pt.astype(BF)
                    dv=dot(pt,doe[hh,n0:,:])
                    dk=dot(ds,qe[h,n0:,:])*LN2
                    dqt[64*hh:64*hh+64,n0:]+=dot(kt[hh,:,ks],ds)
                    outs.append((dk,dv))
                dk=jnp.where(low,outs[0][0],pltpu.roll(outs[1][0],64,1))
                dv=jnp.where(low,outs[0][1],pltpu.roll(outs[1][1],64,1))
                co=cos_o[ks,:]; si=sin_o[ks,:]
                ds_s[p,ks,128:256]=(dk*co-swap32(dk)*si).astype(BF)
                ds_s[p,ks,256:384]=dv.astype(BF)
                for q in range(3):
                    if "p%dj%d"%(q,j) in SCHEDULE:
                        @pl.when(p==q)
                        def _(): tick("p%dj%d"%(q,j))
            for i in range(nb):
                rows=slice(i*B,(i+1)*B)
                dq=dqt[:,rows].T*(HD**-0.5)
                co=cos_o[rows,:]; si=sin_o[rows,:]
                ds_s[p,rows,0:128]=(dq*co-swap32(dq)*si).astype(BF)
            for c in range(2):
                v=dot(nt[c*(Dm//2):(c+1)*(Dm//2),:],ds_s[p])
                C.g[0][p,c]=v.reshape(RING,Dm//16,384).astype(BF)
            C.start(p)
            for q in range(3):
                if "p%de"%q in SCHEDULE:
                    @pl.when(p==q)
                    def _(): tick("p%de"%q)
            return 0
        lax.fori_loop(0,nh//2,pair,0)
        def c_dn(c): return copy_to(snd.at[blk(c)],rcv.at[blk(c)],sems,2+c,{"mp":1-mp})
        def part(r0,xr,c):
            rows=pl.ds(pl.multiple_of(r0,W),W)
            v=dot(ds_s[0,rows,:],wc[0],NT)+dot(ds_s[1,rows,:],wc[1],NT)+dot(ds_s[2,rows,:],wc[2],NT)
            x=xr[blk(c)].astype(F32)
            xr=x*lax.rsqrt(jnp.mean(x*x,axis=1,keepdims=True)+EPS)
            return v, jnp.sum(v*xr,axis=0,keepdims=True)
        gsum=jnp.zeros((1,Dm),F32)
        for c in range(3):
            v,gs=part(theirs+c*W,x_p,c); gsum=gsum+gs
            snd[blk(c)]=v.astype(BF); c_dn(c).start()
            tick("t%d"%c)
        for c in range(3):
            v,gs=part(mine+c*W,x_ref,c); gsum=gsum+gs
            dn[blk(c)]=v
            tick("u%d"%c)
        gx[0,0:1]=gsum
        c_gc=copy_to(gx.at[0],gx.at[1],sems,6,{"core":1-at.core}); c_gc.start()
        tick("g")
        c_gc.wait(); gring[0]=gx[0]+gx[1]
        def c_gr(d,t): return copy_to(gring.at[0 if t==0 else 4*d+t],gring.at[4*d+t+1],sems,7+4*d+t,{"chip":at.nxt[d]})
        c_gr(0,0).start(); c_gr(1,0).start()
        gtot=gring[0]
        for t in range(4):
            for d in range(2):
                if t<4-d:
                    c_gr(d,t).wait()
                    if t+1<4-d: c_gr(d,t+1).start()
                    gtot=gtot+gring[4*d+t+1]
            tick("g%d"%t)
        gx[2]=gtot
        c_gx=copy_to(gx.at[2],gx.at[3],sems,5,{"mp":1-mp}); c_gx.start()
        tick("z")
        for c in range(3):
            c_dn(c).wait()
            r=blk(c)
            d=dn[r]+rcv[r].astype(F32)
            x=x_ref[r].astype(F32)
            i1=lax.rsqrt(jnp.mean(x*x,axis=1,keepdims=True)+EPS)
            s=gain_a[...].astype(F32).reshape(1,-1)*d
            snd[r]=(res[r]+i1*s-x*(i1*i1*i1)*jnp.mean(s*x,axis=1,keepdims=True)).astype(BF)
        c_gx.wait(); gains_out[...]=gx[2]+gx[3]
        c_ig=pltpu.make_async_copy(snd,ig_h,lsem.at[11]); c_ig.start()
        M.finish(0); N.finish(0); O.finish(0)
        for v in range(3): C.finish(v)
        c_ig.wait()
    hT=V((nh,T,128),BF)
    pl.run_scoped(attn,hT,hT,hT,V((T,128),F32),V((T,128),F32),V((T,Dm),BF),V((R,Dm),BF),V((nh//2,Dm,H),BF),
                  V((Dm,T),BF),V((2,T,128),BF),V((2,64,T),BF),V((128,T),F32),V((nh//2,T,H),BF),V((R,Dm),F32))

def main_call(x,og,heads,hrecv,wo,wop,gain_a,gain_m,hbm,cid):
    R,Dm=x.shape; T,H=heads.shape
    Vs=pl.BlockSpec(memory_space=pltpu.VMEM); N=pl.BlockSpec(memory_space=pl.ANY); sd=jax.ShapeDtypeStruct; V=pltpu.VMEM
    scs=[s.scratch() for s in (RING_M,RING_N,RING_O,RING_C)]
    local=[V((R,H),BF),V((T,H),BF),V((R,Dm),F32)]+[V((R,Dm),BF)]*2
    local+=[V((4,8,Dm),F32),V((RING,8,Dm),F32),pltpu.SemaphoreType.DMA((2,7+RING)),pltpu.SemaphoreType.DMA((21,)),pltpu.SemaphoreType.DMA((2,3))]
    outs=[sd((R,Dm),BF)]*2+[sd((2,2,RING,48,1536),BF),sd((2,RING,48,H),BF),sd((3,2,RING,48,384),BF),sd((8,Dm),F32)]
    return pl.pallas_call(functools.partial(main_kernel,*[len(s) for s in scs]),
        out_shape=tuple(outs), in_specs=[Vs]*8+[N]*len(hbm), out_specs=(N,)*5+(Vs,),
        scratch_shapes=sum(scs,[])+local,
        compiler_params=pltpu.CompilerParams(collective_id=cid,has_side_effects=True,vmem_limit_bytes=67043328),
        name="mlp_and_backward")(x,og,heads,hrecv,wo,wop,gain_a,gain_m,*hbm)

def widen_kernel(mlp,wo,qkv,y,dx,gains,gate,up,down,out,query,key,value,y_out,dx_out,ga,gm):
    ga[...]=gains[0]; gm[...]=gains[1]
    y_out[...]=y[...].astype(F32); dx_out[...]=dx[...].astype(F32)
    F=mlp.shape[2]//3; H=wo.shape[1]; B=mlp.shape[1]
    for q in range(2):
        cs=slice(F*q,F*q+F)
        gate[:,cs]=mlp[q,:,0:F].astype(F32)
        up[:,cs]=mlp[q,:,F:2*F].astype(F32)
        down[cs,:]=mlp[q,:,2*F:3*F].astype(F32).T
    out[...]=wo[...].astype(F32).T
    for p in range(qkv.shape[0]):
        cs=slice(128*p,128*p+128)
        query[:,cs]=qkv[p,:,0:128].astype(F32)
        key[:,cs]=qkv[p,:,128:256].astype(F32)
        value[:,cs]=qkv[p,:,256:384].astype(F32)

def widen(mlp,wo,qkv,y,dx,gains):
    Dm,H=wo.shape; F=mlp.shape[2]//3; B=128; P3=qkv.shape[0]
    sd=jax.ShapeDtypeStruct
    row=lambda n: pl.BlockSpec((B,n),lambda i:(i,0))
    rows_spec=pl.BlockSpec((y.shape[0]//(Dm//B),y.shape[1]),lambda i:(i,0))
    col=lambda n: pl.BlockSpec((n,B),lambda i:(0,i))
    return pl.pallas_call(widen_kernel,grid=(Dm//B,),
        out_shape=(sd((Dm,2*F),F32),sd((Dm,2*F),F32),sd((2*F,Dm),F32),sd((H,Dm),F32))+(sd((Dm,H),F32),)*3+(sd(y.shape,F32),)*2+(sd((Dm,),F32),)*2,
        in_specs=[pl.BlockSpec((2,B,3*F),lambda i:(0,i,0)),row(H),pl.BlockSpec((P3,B,H),lambda i:(0,i,0)),rows_spec,rows_spec,pl.BlockSpec((8,Dm),lambda i:(0,0))],
        out_specs=(row(2*F),row(2*F),col(2*F),col(H),row(H),row(H),row(H),rows_spec,rows_spec)+(pl.BlockSpec((Dm,),lambda i:(0,)),)*2,
        compiler_params=pltpu.CompilerParams(vmem_limit_bytes=67043328),name="widen")(mlp,wo,qkv,y,dx,gains)


def on_device(layer_input, gain_attn, w_query, w_key, w_value, w_out, gain_mlp, w_gate, w_up, w_down,
              segment_start, segment_parent, out_grad):
    weights = (w_out, w_gate, w_up, w_down)
    x_peer, normed, cosine, sine, ke, ve, qe, heads, heads_peer, peer_out, peer_gate, peer_up, peer_down = front(
        layer_input, gain_attn, w_query, w_key, w_value, segment_start, segment_parent, weights, 2
    )
    output, input_grad, mlp_g, out_g, qkv_g, gain_g = main_call(
        layer_input, out_grad, heads, heads_peer, w_out, peer_out, gain_attn, gain_mlp,
        (w_gate, w_up, w_down, peer_gate, peer_up, peer_down, qe, ke, ve, cosine, sine, normed, x_peer,
         w_query, w_key, w_value), 1,
    )
    sums = [mlp_g.reshape(2, -1, mlp_g.shape[-1]), out_g.reshape(-1, out_g.shape[-1]), qkv_g.reshape(3, -1, qkv_g.shape[-1]), gain_g]
    if lax.axis_size("grp") > 1:
        sums = lax.psum([s.astype(F32) for s in sums], "grp")
    mlp_g, out_g, qkv_g, gain_g = sums
    gate_g, up_g, down_g, out_g, query_g, key_g, value_g, output, input_grad, gain_attn_grad, gain_mlp_grad = widen(
        mlp_g, out_g, qkv_g, output, input_grad, gain_g
    )
    return (
        output, input_grad, gain_attn_grad, query_g, key_g, value_g, out_g, gain_mlp_grad, gate_g, up_g, down_g,
    )


def solution(mesh):
    fine = Mesh(mesh.devices.reshape(-1, RING, 2, mesh.shape["mp"]), ("grp", "chip", "core", "mp"))
    dp = ("grp", "chip", "core")
    tok, col, row, tree = P(dp + ("mp",), None), P(None, "mp"), P("mp", None), P(dp, None)
    in_specs = (tok, P(), col, col, col, row, P(), col, col, row, tree, tree, tok)
    out_specs = (tok, tok, P(), col, col, col, row, P(), col, col, row)
    return jax.shard_map(on_device, mesh=fine, in_specs=in_specs, out_specs=out_specs, check_vma=False)
```

```python
import functools
import math

import jax
import jax.numpy as jnp
from jax import lax
from jax.experimental import pallas as pl
from jax.experimental.pallas import tpu as pltpu
from jax.sharding import Mesh
from jax.sharding import PartitionSpec as P

BF = jnp.bfloat16
F32 = jnp.float32
HD=64; EPS=1e-5; BIG=-1e30
C_Q = (HD**-0.5)*math.log2(math.e)
LN2 = math.log(2.0)
NT=(((1,),(1,)),((),())); NN=(((1,),(0,)),((),())); TN=(((0,),(0,)),((),()))
def dot(a,b,dims=NN): return lax.dot_general(a,b,dims,preferred_element_type=F32)
def lanes(shape): return lax.broadcasted_iota(jnp.int32, shape, 1)

def split3(x):
    hi=x.astype(BF).astype(F32); r=x-hi; mid=r.astype(BF).astype(F32); lo=r-mid
    return hi,mid,lo

def tables(starts, parents, row0, rows, nseg, tree_len):
    sh=(rows,128)
    t = row0 + lax.broadcasted_iota(jnp.int32, sh, 0)
    st=[starts[0,s] for s in range(nseg)]+[tree_len]
    par=[parents[0,s] for s in range(nseg)]
    ln=[st[s+1]-st[s] for s in range(nseg)]
    def pick(vals, idx):
        r = vals[0]
        for s in range(1,nseg): r = jnp.where(idx==s, vals[s], r)
        return r
    D=[]
    gps=[]
    for s in range(nseg):
        p=par[s]; gp=pick(par,p); gps.append(gp)
        off=jnp.where(p!=s, pick(ln,p), 0)+jnp.where((gp!=s)&(gp!=p), pick(ln,gp), 0)
        D.append(off-st[s])
    seg=jnp.zeros(sh,jnp.int32); pos=t+D[0]
    for s in range(1,nseg):
        ge=t>=st[s]
        seg=seg+ge.astype(jnp.int32)
        pos=pos+jnp.where(ge, D[s]-D[s-1], 0)
    f=lanes(sh)-64
    parl=jnp.zeros((1,128),jnp.int32)-1; gpl=parl
    fl=lanes((1,128))-64
    for s in range(nseg):
        parl=jnp.where(fl==s, par[s], parl); gpl=jnp.where(fl==s, gps[s], gpl)
    vis=(f==seg)|(parl==seg)|(gpl==seg)|(f<0)|(f>=nseg)
    qf=jnp.where(f==seg,1.0,0.0)
    kf=jnp.where(vis,0.0,BIG)
    kf=jnp.where((f>=8)&(f<11),1.0,kf)
    return pos.astype(F32), qf, kf

def rot_tables(posf):
    l=lax.broadcasted_iota(jnp.int32,(1,128),1)
    fr=jnp.exp((l%32).astype(F32)*(-2.0*math.log(10000.0)/HD))
    ang=posf*fr
    sg=jnp.where((l%64)<32,-1.0,1.0)
    return jnp.cos(ang), jnp.sin(ang)*sg

def swap32(x):
    l=lanes(x.shape)
    return jnp.where((l&32)==0, pltpu.roll(x,96,1), pltpu.roll(x,32,1))


MESH=pl.DeviceIdType.MESH
RING=8
def ring_chip(r):
    return jnp.where(r<RING//2, 2*r, 2*(RING-1-r)+1)
def chip_ring(n):
    return jnp.where(n%2==0, n//2, RING-1-n//2)

class Place:
    def __init__(self):
        self.core=lax.axis_index("core"); self.mp=lax.axis_index("mp")
        self.pos=chip_ring(lax.axis_index("chip"))
        self.nxt=[ring_chip(lax.rem(self.pos+1,RING)), ring_chip(lax.rem(self.pos+RING-1,RING))]
    def barrier(self):
        b=pltpu.get_barrier_semaphore()
        ds=[{"core":1-self.core},{"mp":1-self.mp},{"chip":self.nxt[0]},{"chip":self.nxt[1]}]
        for d in ds: pl.semaphore_signal(b, inc=1, device_id=d, device_id_type=MESH)
        return lambda: pl.semaphore_wait(b, len(ds))

def copy_to(src,dst,sems,k,dev):
    return pltpu.make_async_remote_copy(src,dst,sems.at[0,k],sems.at[1,k],device_id=dev,device_id_type=MESH)

class Gather:
    def __init__(self,p,src,out,kinds,sems):
        self.p,self.src,self.out,self.kinds,self.sems=p,src,out,kinds,sems
    def ref(self,x,a,ch,core=None):
        n=self.out[a].shape[0]//(2*RING)
        return x[a].at[pl.ds(pl.multiple_of((self.p.core*RING+ch)*n,n),n)]
    def at(self,d,dist): return lax.rem(self.p.pos+(dist if d==0 else RING-dist),RING)
    def hops(self,a,d): return 4-self.kinds[a] if d==0 else 3+self.kinds[a]
    def cp(self,src,dst,a,k,dev):
        return pltpu.make_async_remote_copy(src,dst,self.sems.at[0,a,k],self.sems.at[1,a,k],device_id=dev,device_id_type=MESH)
    def cx(self,a): return self.cp(self.ref(self.src,a,self.p.pos),self.ref(self.out,a,self.p.pos),a,0,{"mp":1-self.p.mp})
    def cag(self,a,d,t):
        r=self.ref(self.out,a,self.at(1-d,t))
        return self.cp(r,r,a,1+4*d+t,{"chip":self.p.nxt[d]})
    def cfc(self,a,d,t):
        r=self.ref(self.out,a,self.at(1-d,t+1))
        return self.cp(r,r,a,9+4*d+t,{"core":1-self.p.core})
    def cfo(self,a):
        r=self.ref(self.out,a,self.p.pos)
        return self.cp(r,r,a,17,{"core":1-self.p.core})
    def agstart(self,a):
        self.cx(a).wait()
        for d in range(2): self.cag(a,d,0).start()
        self.cfo(a).start()
    def ag(self,a,t):
        for d in range(2):
            if t<self.hops(a,d):
                self.cag(a,d,t).wait()
                if t+1<self.hops(a,d): self.cag(a,d,t+1).start()
                self.cfc(a,d,t).start()
    def finish(self,a):
        self.cfo(a).wait()
        for d in range(2):
            for t in range(self.hops(a,d)): self.cfc(a,d,t).wait()

def front_kernel(nseg,starts,parents,x_ref,gain,wq,wk,wv,*refs):
    refs=list(refs)
    def take(n):
        r=refs[:n]; del refs[:n]; return r
    NW=(len(refs)-21)//2
    src=take(NW)
    big=take(7); heads,hrecv=take(2); out=take(NW)
    x_peer,normed,cos_o,sin_o,ke,ve,qe,qf_s,kf_s,sems,wsems,osem=take(12)
    at=Place(); mp=at.mp
    R=x_ref.shape[0]; T=2*R; B=256; nh=wq.shape[1]//HD
    G=Gather(at,src,out,[a%2 for a in range(NW)],wsems)
    mine=pl.multiple_of(mp*R,R); theirs=pl.multiple_of((1-mp)*R,R)
    at.barrier()()
    peer={"mp":1-mp}
    NG=NW
    for a in range(NG): G.cx(a).start()
    c_x=copy_to(x_ref,x_peer,sems,0,peer); c_x.start()
    for a in range(NG,NW): G.cx(a).start()
    def tab(c,_):
        r0=pl.multiple_of(c*B,B); rows=pl.ds(r0,B)
        posf,qf,kf=tables(starts,parents,r0,B,nseg,T)
        co,si=rot_tables(posf)
        cos_o[rows,:]=co; sin_o[rows,:]=si
        qf_s[rows,:]=qf.astype(BF); kf_s[rows,:]=kf.astype(BF)
        return 0
    lb=lanes((B,128)); low=lb<64
    vone=jnp.where((lb>=64)&(lb<67),1.0,0.0)
    def proj(xr,base):
        def f(c,_):
            rows=pl.ds(pl.multiple_of(base+c*B,B),B)
            x=xr[pl.ds(pl.multiple_of(c*B,B),B),:].astype(F32)
            r1=lax.rsqrt(jnp.mean(x*x,axis=1,keepdims=True)+EPS)
            n=(x*r1*gain[...].astype(F32).reshape(1,-1)).astype(BF)
            normed[rows,:]=n
            co=cos_o[rows,:]; si=sin_o[rows,:]; qf=qf_s[rows,:].astype(F32); kf=kf_s[rows,:].astype(F32)
            qq=dot(n,wq[...]); kk=dot(n,wk[...]); vv=dot(n,wv[...])
            for p in range(nh//2):
                cs=slice(128*p,128*p+128)
                q=qq[:,cs]; k=kk[:,cs]; v=vv[:,cs]
                q=(q*co+swap32(q)*si)*C_Q; k=k*co+swap32(k)*si
                for hh in range(2):
                    if hh: q=pltpu.roll(q,64,1); k=pltpu.roll(k,64,1); v=pltpu.roll(v,64,1)
                    qe[2*p+hh,rows,:]=jnp.where(low,q,qf).astype(BF)
                    ke[2*p+hh,rows,:]=jnp.where(low,k,kf).astype(BF)
                    ve[2*p+hh,rows,:]=jnp.where(low,v,vone).astype(BF)
            return 0
        lax.fori_loop(0,R//B,f,0)
    for a in range(NG): G.agstart(a)
    lax.fori_loop(0,T//B,tab,0)
    for a in range(NG): G.ag(a,0)
    proj(x_ref,mine)
    for a in range(NG): G.ag(a,1)
    c_x.wait()
    proj(x_peer,theirs)
    puts=[pltpu.make_async_copy(s,d,osem.at[i]) for i,(s,d) in enumerate(zip((x_peer,normed,cos_o,sin_o,ke,ve),big))]
    for q in puts: q.start()
    for a in range(NG): G.ag(a,2)
    def put_q(p): return pltpu.make_async_copy(qe.at[pl.ds(2*p,2)],big[6].at[pl.ds(2*p,2)],osem.at[6+p])
    causal=lax.broadcasted_iota(jnp.int32,(B,B),1)<=lax.broadcasted_iota(jnp.int32,(B,B),0)
    NB=R//B
    def c_h(p,q):
        cs=pl.ds(pl.multiple_of(p*128,128),128)
        return pltpu.make_async_remote_copy(heads.at[pl.ds(pl.multiple_of(theirs+q*B,B),B),cs],hrecv.at[pl.ds(q*B,B),cs],sems.at[0,1+NB*p+q],sems.at[1,1+NB*p+q],device_id=peer,device_id_type=MESH)
    def attend(p,_):
        cs=pl.ds(pl.multiple_of(p*128,128),128)
        for i in range(T//B):
            n=(i+1)*B; rows=slice(i*B,(i+1)*B)
            outs=[]
            for hh in range(2):
                h=2*p+hh
                q=qe[h,rows,:]
                s=dot(q,ke[h,0:n,:],NT)
                sd=jnp.where(causal,s[:,n-B:],BIG)
                s=sd if i==0 else jnp.concatenate([s[:,:n-B],sd],axis=1)
                m=jnp.max(s,axis=1,keepdims=True)
                pr=jnp.exp2(s-m).astype(BF)
                o=dot(pr,ve[h,0:n,:])
                den=o[:,64:65]
                o=o*(1.0/den)
                a,b,c=split3(-(m+jnp.log2(den)))
                qe[h,rows,:]=jnp.where(lb==72,a,jnp.where(lb==73,b,jnp.where(lb==74,c,q.astype(F32)))).astype(BF)
                outs.append(o)
            heads[rows,cs]=jnp.where(low,outs[0],pltpu.roll(outs[1],64,1)).astype(BF)
            @pl.when(1-mp==i//NB)
            def _(): c_h(p,i%NB).start()
            if i==3:
                @pl.when(p==2)
                def _():
                    for a in range(NG): G.ag(a,3)
        put_q(p).start()
        return 0
    lax.fori_loop(0,nh//2,attend,0)
    for a in range(NW): G.finish(a)
    for q in puts: q.wait()
    for p in range(nh//2): put_q(p).wait()
    for p in range(nh//2):
        for q in range(NB): c_h(p,q).wait()

def front(x,gain,wq,wk,wv,starts,parents,weights,cid):
    R,Dm=x.shape; T=2*R; H=wq.shape[1]; nh=H//HD; nseg=starts.shape[1]; NW=len(weights)
    Vs=pl.BlockSpec(memory_space=pltpu.VMEM); S=pl.BlockSpec(memory_space=pltpu.SMEM); N=pl.BlockSpec(memory_space=pl.ANY)
    sd=jax.ShapeDtypeStruct; hT=sd((nh,T,128),BF); V=pltpu.VMEM
    return pl.pallas_call(functools.partial(front_kernel,nseg),
        out_shape=(sd((R,Dm),BF),sd((T,Dm),BF),sd((T,128),F32),sd((T,128),F32),hT,hT,hT,sd((T,H),BF),sd((R,H),BF))+tuple(sd(w.shape,BF) for w in weights),
        in_specs=[S,S]+[Vs]*5+[N]*NW, out_specs=(N,)*7+(Vs,)*2+(N,)*NW,
        scratch_shapes=[V((R,Dm),BF),V((T,Dm),BF),V((T,128),F32),V((T,128),F32),V((nh,T,128),BF),V((nh,T,128),BF),V((nh,T,128),BF),V((T,128),BF),V((T,128),BF),
            pltpu.SemaphoreType.DMA((2,1+(nh//2)*(R//256))),pltpu.SemaphoreType.DMA((2,NW,18)),pltpu.SemaphoreType.DMA((6+nh//2,))],
        compiler_params=pltpu.CompilerParams(collective_id=cid,has_side_effects=True,vmem_limit_bytes=67043328),
        name="attention_forward")(starts,parents,x,gain,wq,wk,wv,*weights)

class Ring:
    def __init__(self, shapes, kinds, count, gslots, swaps, early=True, slot=None):
        self.shapes,self.count,self.gslots,self.swaps,self.early=shapes,count,gslots,swaps,early
        self.slot=slot or (lambda u: lax.rem(u,gslots))
        self.nr=(len(swaps) if early else count) if swaps else count
        self.na=len(shapes); self.flows=[]
        for a,parts in enumerate(kinds):
            for c0,nc,k in parts:
                self.flows+=[(a,c0,nc,0,4-k),(a,c0,nc,1,3+k)]
        self.nf=len(self.flows)
        self.own=[s[0] for s in swaps] if swaps else list(range(count))
        self.nv=len(self.own)
        na,nf=self.na,self.nf
        self.k_rs=na; self.k_x=0; self.k_ag=na; self.k_fc=self.k_ag+4*nf; self.k_fo=self.k_fc+4*nf; self.k_put=self.k_fo+na
        self.n1=na+4*nf; self.n2=self.k_put+na
    def scratch(self):
        V=pltpu.VMEM; U=self.count
        s=[V((self.gslots,2,RING)+x,BF) for x in self.shapes] if self.gslots else []
        s+=[V((U,RING)+x,BF) for x in self.shapes]
        s+=[V((self.nr,)+x,BF) for x in self.shapes]
        s+=[V((self.nv,)+((RING,)+x if self.early else x),BF) for x in self.shapes] if self.swaps else []
        s+=[V((self.nr,h,self.shapes[a][0],nc),BF) for a,c0,nc,d,h in self.flows]
        return s+[pltpu.SemaphoreType.DMA((2,U,self.n1)),pltpu.SemaphoreType.DMA((2,self.nv,self.n2))]
    def bind(self,p,dst,sc,g=None):
        self.p,self.dst=p,dst
        sc=list(sc); na=self.na
        if g is None: g,sc=sc[:na],sc[na:]
        self.g=g; self.r=sc[:na]; self.fin=sc[na:2*na]; sc=sc[2*na:]
        if self.swaps: self.xr=sc[:na]; sc=sc[na:]
        self.arr=sc[:self.nf]; self.sem,self.sem2=sc[self.nf:]
        return self
    def at(self,d,dist):
        return lax.rem(self.p.pos+(dist if d==0 else RING-dist),RING)
    def cp(self,src,dst,u,k,dev):
        return pltpu.make_async_remote_copy(src,dst,self.sem.at[0,u,k],self.sem.at[1,u,k],device_id=dev,device_id_type=MESH)
    def cp2(self,src,dst,v,k,dev):
        return pltpu.make_async_remote_copy(src,dst,self.sem2.at[0,v,k],self.sem2.at[1,v,k],device_id=dev,device_id_type=MESH)
    def c1(self,u,a): return self.cp(self.g[a].at[self.slot(u),1-self.p.core],self.r[a].at[u],u,a,{"core":1-self.p.core})
    def start(self,u):
        for a in range(self.na): self.c1(u,a).start()
    def uown(self,v): return self.own[v] if self.swaps else v
    def u_of(self,w): return self.uown(w) if self.early else w
    def w_own(self,v): return v if self.early else self.uown(v)
    def crs(self,w,f,t):
        a,c0,nc,d,h=self.flows[f]
        src=self.r[a].at[self.u_of(w),self.at(d,h),:,pl.ds(c0,nc)] if t==0 else self.arr[f].at[w,t-1]
        return self.cp(src,self.arr[f].at[w,t],self.u_of(w),self.k_rs+4*f+t,{"chip":self.p.nxt[d]})
    def cx(self,v,a): return self.cp2(self.r[a].at[self.swaps[v][1]] if self.early else self.fin[a].at[self.swaps[v][1]],self.xr[a].at[v],v,self.k_x+a,{"mp":1-self.p.mp})
    def push(self,v):
        u=self.swaps[v][1]
        for a in range(self.na):
            self.c1(u,a).wait()
            r,g=self.r[a],self.g[a]
            def add(s,_):
                r[u,s]=r[u,s]+g[self.slot(u),self.p.core,s]; return 0
            lax.fori_loop(0,RING,add,0)
            self.cx(v,a).start()
    def xstart(self,v):
        for a in range(self.na): self.cx(v,a).start()
    def first(self,v):
        u=self.u_of(v)
        for a in range(self.na):
            self.c1(u,a).wait()
            if self.swaps and self.early: self.cx(v,a).wait()
            r,g=self.r[a],self.g[a]
            def add(s,_):
                t=r[u,s].astype(F32)+g[self.slot(u),self.p.core,s].astype(F32)
                if self.swaps and self.early: t=t+self.xr[a][v,s].astype(F32)
                r[u,s]=t.astype(BF); return 0
            lax.fori_loop(0,RING,add,0)
            for f in range(self.nf):
                if self.flows[f][0]==a: self.crs(v,f,0).start()
    def rs(self,v,t):
        u=self.u_of(v)
        for f,(a,c0,nc,d,h) in enumerate(self.flows):
            if t<h:
                self.crs(v,f,t).wait()
                if t+1<h:
                    self.arr[f][v,t]=self.arr[f][v,t]+self.r[a][u,self.at(d,h-t-1),:,pl.ds(c0,nc)]
                    self.crs(v,f,t+1).start()
        if t==3:
            for f in range(0,self.nf,2):
                a,c0,nc,d,h=self.flows[f]; h2=self.flows[f+1][4]
                w=self.r[a][u,self.p.pos,:,pl.ds(c0,nc)].astype(F32)+self.arr[f][v,h-1].astype(F32)+self.arr[f+1][v,h2-1].astype(F32)
                self.fin[a][v,:,pl.ds(c0,nc)]=w.astype(BF)
    def cag(self,v,f,t):
        a,c0,nc,d,h=self.flows[f]
        dst=self.dst(v,a,self.at(1-d,t)).at[:,pl.ds(c0,nc)]
        src=self.fin[a].at[self.w_own(v),:,pl.ds(c0,nc)] if t==0 else dst
        return self.cp2(src,dst,v,self.k_ag+4*f+t,{"chip":self.p.nxt[d]})
    def cfc(self,v,f,t):
        a,c0,nc,d,h=self.flows[f]
        ref=self.dst(v,a,self.at(1-d,t+1)).at[:,pl.ds(c0,nc)]
        return self.cp2(ref,ref,v,self.k_fc+4*f+t,{"core":1-self.p.core})
    def cfo(self,v,a): return self.cp2(self.fin[a].at[self.w_own(v)],self.dst(v,a,self.p.pos),v,self.k_fo+a,{"core":1-self.p.core})
    def put(self,v,a): return pltpu.make_async_copy(self.fin[a].at[self.w_own(v)],self.dst(v,a,self.p.pos),self.sem2.at[0,v,self.k_put+a])
    def agstart(self,v):
        for a in range(self.na):
            if not self.early:
                u=self.uown(v)
                self.cx(v,a).wait()
                self.fin[a][u]=self.fin[a][u]+self.xr[a][v]
            for f in range(self.nf):
                if self.flows[f][0]==a: self.cag(v,f,0).start()
            self.cfo(v,a).start(); self.put(v,a).start()
    def ag(self,v,t):
        for f,(a,c0,nc,d,h) in enumerate(self.flows):
            if t<h:
                self.cag(v,f,t).wait()
                if t+1<h: self.cag(v,f,t+1).start()
                self.cfc(v,f,t).start()
    def finish(self,v):
        for a in range(self.na):
            self.put(v,a).wait(); self.cfo(v,a).wait()
        for f,(a,c0,nc,d,h) in enumerate(self.flows):
            for t in range(h): self.cfc(v,f,t).wait()

SHAPES_M,KINDS_M=[(48,1536)],[[(0,768,0),(768,768,1)]]
RING_M=Ring(SHAPES_M,KINDS_M,2,2,[(1,0)],True,lambda u: 0)
RING_N=Ring(SHAPES_M,KINDS_M,2,0,[(1,0)],False,lambda u: 1)
RING_O=Ring([(48,384)],[[(0,256,0),(256,128,1)]],2,2,[(1,0)])
RING_C=Ring([(48,384)],[[(0,256,0),(256,128,1)]],3,3,[])
SCHEDULE={
"m1":[("N","rs",0,2),("M","first",0)],
"m2":[("N","rs",0,3),("N","xstart",0),("N","first",1)],
"a0":[("M","rs",0,0),("O","push",0)],
"a1":[("N","rs",1,0),("M","rs",0,1)],
"a2":[("N","rs",1,1)],
"p0s":[("M","rs",0,2)],
"p0j0":[("N","rs",1,2)],
"p0j1":[("O","first",0)],
"p0j3":[("M","rs",0,3),("M","agstart",0)],
"p0e":[("N","rs",1,3),("N","agstart",0)],
"p1j0":[("C","first",0),("O","rs",0,0)],
"p1j1":[("M","ag",0,0)],
"p1j3":[("C","rs",0,0),("N","ag",0,0)],
"p1e":[("O","rs",0,1)],
"p2s":[("M","ag",0,1)],
"p2j0":[("C","first",1),("C","rs",0,1),("N","ag",0,1)],
"p2j1":[("O","rs",0,2)],
"p2j3":[("C","rs",1,0),("M","ag",0,2)],
"p2e":[("C","rs",0,2),("O","rs",0,3),("O","agstart",0)],
"t0":[("C","rs",0,3),("C","agstart",0),("N","ag",0,2)],
"t1":[("C","first",2),("C","rs",1,1)],
"u0":[("C","rs",2,0),("C","rs",1,2),("O","ag",0,0)],
"u1":[("C","rs",2,1),("C","ag",0,0)],
"u2":[("C","rs",1,3),("C","agstart",1)],
"g":[("C","rs",2,2),("O","ag",0,1)],
"g0":[("C","rs",2,3),("C","agstart",2),("C","ag",0,1)],
"g1":[("C","ag",1,0),("O","ag",0,2)],
"g2":[("C","ag",2,0),("C","ag",1,1),("C","ag",0,2)],
"g3":[("C","ag",2,1),("C","ag",1,2),("M","ag",0,3)],
"z":[("C","ag",2,2),("N","ag",0,3),("C","ag",0,3),("C","ag",1,3),("O","ag",0,3),("C","ag",2,3)],
}
def main_kernel(nM,nN,nO,nC,*refs):
    refs=list(refs)
    def take(n):
        r=refs[:n]; del refs[:n]; return r
    x_ref,og,heads,hrecv,wo,wop,gain_a,gain_m=take(8)
    wg_h,wu_h,wd_h,wgp_h,wup_h,wdp_h,qe_h,ke_h,ve_h,co_h,si_h,norm_h,xp_h,wq_h,wk_h,wv_h=take(16)
    out_h,ig_h=take(2); outM=take(1); outO=take(1); outC=take(1); gains_out,=take(1)
    scM=take(nM); scN=take(nN); scO=take(nO); scC=take(nC)
    dhs,dh,res,snd,rcv,gx,gring,sems,lsem,wsem=take(10)
    at=Place(); mp=at.mp
    R,Dm=x_ref.shape; T=2*R; nh=qe_h.shape[0]; B=256; nb=T//B; H=wo.shape[0]; F=512
    core=at.core
    rings={}
    def tick(site):
        for name,op,*args in SCHEDULE.get(site,()): getattr(rings[name],op)(*args)
    def dst_m(q): return lambda v,a,ch: outM[0].at[q,core,ch]
    def dst_c(v,a,ch): return outC[0].at[v,core,ch]
    M=RING_M.bind(at,dst_m(0),scM); N=RING_N.bind(at,dst_m(1),scN,M.g); O=RING_O.bind(at,lambda v,a,ch: outO[0].at[core,ch],scO); C=RING_C.bind(at,dst_c,scC)
    rings.update(M=M,N=N,O=O,C=C)
    mine=pl.multiple_of(mp*R,R); theirs=pl.multiple_of((1-mp)*R,R)
    W=R//3
    def blk(i): return pl.ds(i*W,W)
    arrived=at.barrier()
    c_dh=copy_to(dhs,dh.at[pl.ds(mine,R)],sems,0,{"mp":1-mp})

    def mlp(n2,n2t,ogt,acc,dn2,hid,dg,du,wgb,wub,wdb):
        def loads(g,u,d,q,slot):
            cs=pl.ds(pl.multiple_of(q*F,F),F)
            return [pltpu.make_async_copy(g.at[:,cs],wgb.at[slot],wsem.at[slot,0]),
                    pltpu.make_async_copy(u.at[:,cs],wub.at[slot],wsem.at[slot,1]),
                    pltpu.make_async_copy(d.at[cs,:],wdb.at[slot],wsem.at[slot,2])]
        for q in loads(wgp_h,wup_h,wdp_h,0,0): q.start()
        def pre(i,_):
            rows=pl.ds(pl.multiple_of(i*W,W),W); mr=pl.ds(pl.multiple_of(mine+i*W,W),W)
            r=x_ref[rows,:].astype(F32)+dot(heads[mr,:],wo[...])+dot(hrecv[rows,:],wop[...])
            res[rows,:]=r
            n=(r*lax.rsqrt(jnp.mean(r*r,axis=1,keepdims=True)+EPS)*gain_m[...].astype(F32).reshape(1,-1)).astype(BF)
            n2[rows,:]=n
            n2t[:,rows]=n.T
            ogt[:,rows]=og[rows,:].T
            return 0
        lax.fori_loop(0,3,pre,0)
        arrived()
        acc[...]=jnp.zeros_like(acc); dn2[...]=jnp.zeros_like(dn2)
        def step(c,_):
            slot=lax.rem(c,2)
            for q in loads(wg_h,wu_h,wd_h,0,slot): q.wait()
            @pl.when(c==0)
            def _():
                for q in loads(wgp_h,wup_h,wdp_h,1,1): q.start()
            @pl.when((c>0)&(c<3))
            def _():
                for q in loads(wg_h,wu_h,wd_h,c-1,1-slot): q.start()
            wg,wu,wd=wgb[slot],wub[slot],wdb[slot]
            def half(i,_):
                rows=pl.ds(pl.multiple_of(i*W,W),W)
                gate=dot(n2[rows,:],wgb[slot]); up=dot(n2[rows,:],wub[slot]); dhid=dot(og[rows,:],wdb[slot],NT)
                sg=1.0/(1.0+jnp.exp(-gate)); silu=gate*sg
                hid[rows,:]=(silu*up).astype(BF)
                dg[rows,:]=(dhid*up*sg*(1.0+gate*(1.0-sg))).astype(BF)
                du[rows,:]=(dhid*silu).astype(BF)
                return 0
            lax.fori_loop(0,3,half,0)
            @pl.when(c==1)
            def _(): M.push(0)
            @pl.when(c==2)
            def _(): N.first(0)
            def back(i,_):
                rows=pl.ds(pl.multiple_of(i*W,W),W)
                acc[rows,:]=acc[rows,:]+dot(hid[rows,:],wdb[slot])
                dn2[rows,:]=dn2[rows,:]+(dot(dg[rows,:],wgb[slot],NT)+dot(du[rows,:],wub[slot],NT))
                return 0
            lax.fori_loop(0,3,back,0)
            @pl.when(c==3)
            def _(): N.rs(0,1)
            def wgrad(k,_):
                rr=pl.ds(pl.multiple_of(k*(Dm//2),Dm//2),Dm//2)
                M.g[0][slot,k,:,:,0:F]=dot(n2t[rr,:],dg[...]).reshape(RING,48,F).astype(BF)
                M.g[0][slot,k,:,:,F:2*F]=dot(n2t[rr,:],du[...]).reshape(RING,48,F).astype(BF)
                M.g[0][slot,k,:,:,2*F:3*F]=dot(ogt[rr,:],hid[...]).reshape(RING,48,F).astype(BF)
                return 0
            lax.fori_loop(0,2,wgrad,0)
            @pl.when(lax.rem(c,2)==0)
            def _(): M.start(c//2)
            @pl.when(lax.rem(c,2)==1)
            def _(): N.start(c//2)
            @pl.when(c==2)
            def _(): N.rs(0,0)
            return 0
        lax.fori_loop(0,4,step,0)
        tick("m0")
        gx[...]=jnp.zeros_like(gx)
        def post(i,gpart):
            rows=pl.ds(pl.multiple_of(i*W,W),W)
            r=res[rows,:]; d=dn2[rows,:]
            snd[rows,:]=(acc[rows,:]+r).astype(BF)
            i2=lax.rsqrt(jnp.mean(r*r,axis=1,keepdims=True)+EPS)
            s=gain_m[...].astype(F32).reshape(1,-1)*d
            dr=og[rows,:].astype(F32)+i2*s-r*(i2*i2*i2)*jnp.mean(s*r,axis=1,keepdims=True)
            res[rows,:]=dr
            da=dr.astype(BF)
            n2[rows,:]=da
            dhs[rows,:]=dot(da,wop[...],NT).astype(BF)
            return gpart+jnp.sum(d*r*i2,axis=0,keepdims=True)
        gpart=lax.fori_loop(0,3,post,jnp.zeros((1,Dm),F32))
        c_dh.start()
        c_out=pltpu.make_async_copy(snd,out_h,lsem.at[10]); c_out.start()
        gx[0,1:2]=gpart
        tick("m1")
        def own(i,_):
            rows=pl.ds(pl.multiple_of(i*W,W),W)
            n2t[:,rows]=n2[rows,:].T
            dh[pl.ds(pl.multiple_of(mine+i*W,W),W),:]=dot(n2[rows,:],wo[...],NT).astype(BF)
            return 0
        lax.fori_loop(0,3,own,0)
        def ograd(k,_):
            rr=pl.ds(pl.multiple_of(k*(Dm//2),Dm//2),Dm//2)
            O.g[0][0,k]=dot(n2t[rr,:],hrecv[...]).reshape(RING,48,H).astype(BF)
            O.g[0][1,k]=dot(n2t[rr,:],heads[pl.ds(mine,R),:]).reshape(RING,48,H).astype(BF)
            return 0
        lax.fori_loop(0,2,ograd,0)
        O.start(0); O.start(1)
        tick("m2")
        c_out.wait()
    V=pltpu.VMEM
    pl.run_scoped(mlp,V((R,Dm),BF),V((Dm,R),BF),V((Dm,R),BF),V((R,Dm),F32),V((R,Dm),F32),V((R,F),BF),V((R,F),BF),V((R,F),BF),
                  V((2,Dm,F),BF),V((2,Dm,F),BF),V((2,F,Dm),BF))

    def attn(qe,ke,ve,cos_o,sin_o,nrm,x_p,wc,nt,doe,kt,dqt,ds_s,dn):
        ld=[pltpu.make_async_copy(s,d,lsem.at[i]) for i,(s,d) in enumerate(((norm_h,nrm),(ke_h,ke),(qe_h,qe),(ve_h,ve),(co_h,cos_o),(si_h,sin_o),(xp_h,x_p)))]
        ld+=[pltpu.make_async_copy(s.at[:,pl.ds(128*q,128)],wc.at[q,:,pl.ds(128*i,128)],lsem.at[12+3*q+i]) for q in range(nh//2) for i,s in enumerate((wq_h,wk_h,wv_h))]
        for q in ld: q.start()
        tick("a0")
        ld[0].wait()
        def tr(i,_):
            c=pl.ds(pl.multiple_of(i*B,B),B)
            nt[:,c]=nrm[c,:].T
            return 0
        lax.fori_loop(0,nb,tr,0)
        tick("a1")
        for q in ld[1:]: q.wait()
        c_dh.wait(); tick("a2")
        l=lanes((B,128)); low=l<64
        causal=lax.broadcasted_iota(jnp.int32,(B,B),0)<=lax.broadcasted_iota(jnp.int32,(B,B),1)
        def pair(p,_):
            cols=pl.ds(pl.multiple_of(p*128,128),128)
            for i in range(nb):
                rows=slice(i*B,(i+1)*B)
                d=dh[rows,cols].astype(F32); o=heads[rows,cols].astype(F32)
                t=d*o
                for hh in range(2):
                    if hh: t=pltpu.roll(t,64,1); d=pltpu.roll(d,64,1)
                    delta=jnp.sum(jnp.where(low,t,0.0),axis=1,keepdims=True)
                    a,b,c=split3(-delta)
                    doe[hh,rows,:]=jnp.where(low,d,jnp.where(l==64,a,jnp.where(l==65,b,jnp.where(l==66,c,0.0)))).astype(BF)
                    kt[hh,:,rows]=ke[2*p+hh,rows,:].T[0:64]
            dqt[...]=jnp.zeros_like(dqt)
            for q in range(3):
                if "p%ds"%q in SCHEDULE:
                    @pl.when(p==q)
                    def _(): tick("p%ds"%q)
            for j in range(nb):
                ks=slice(j*B,(j+1)*B); n0=j*B
                outs=[]
                for hh in range(2):
                    h=2*p+hh
                    s=dot(ke[h,ks,:],qe[h,n0:,:],NT)
                    dp=dot(ve[h,ks,:],doe[hh,n0:,:],NT)
                    sd=jnp.where(causal,s[:,:B],BIG)
                    s=sd if j==nb-1 else jnp.concatenate([sd,s[:,B:]],axis=1)
                    pt=jnp.exp2(s)
                    ds=(pt*dp).astype(BF)
                    pt=pt.astype(BF)
                    dv=dot(pt,doe[hh,n0:,:])
                    dk=dot(ds,qe[h,n0:,:])*LN2
                    dqt[64*hh:64*hh+64,n0:]+=dot(kt[hh,:,ks],ds)
                    outs.append((dk,dv))
                dk=jnp.where(low,outs[0][0],pltpu.roll(outs[1][0],64,1))
                dv=jnp.where(low,outs[0][1],pltpu.roll(outs[1][1],64,1))
                co=cos_o[ks,:]; si=sin_o[ks,:]
                ds_s[p,ks,128:256]=(dk*co-swap32(dk)*si).astype(BF)
                ds_s[p,ks,256:384]=dv.astype(BF)
                for q in range(3):
                    if "p%dj%d"%(q,j) in SCHEDULE:
                        @pl.when(p==q)
                        def _(): tick("p%dj%d"%(q,j))
            for i in range(nb):
                rows=slice(i*B,(i+1)*B)
                dq=dqt[:,rows].T*(HD**-0.5)
                co=cos_o[rows,:]; si=sin_o[rows,:]
                ds_s[p,rows,0:128]=(dq*co-swap32(dq)*si).astype(BF)
            for c in range(2):
                v=dot(nt[c*(Dm//2):(c+1)*(Dm//2),:],ds_s[p])
                C.g[0][p,c]=v.reshape(RING,Dm//16,384).astype(BF)
            C.start(p)
            for q in range(3):
                if "p%de"%q in SCHEDULE:
                    @pl.when(p==q)
                    def _(): tick("p%de"%q)
            return 0
        lax.fori_loop(0,nh//2,pair,0)
        def c_dn(c): return copy_to(snd.at[blk(c)],rcv.at[blk(c)],sems,2+c,{"mp":1-mp})
        def part(r0,xr,c):
            rows=pl.ds(pl.multiple_of(r0,W),W)
            v=dot(ds_s[0,rows,:],wc[0],NT)+dot(ds_s[1,rows,:],wc[1],NT)+dot(ds_s[2,rows,:],wc[2],NT)
            x=xr[blk(c)].astype(F32)
            xr=x*lax.rsqrt(jnp.mean(x*x,axis=1,keepdims=True)+EPS)
            return v, jnp.sum(v*xr,axis=0,keepdims=True)
        gsum=jnp.zeros((1,Dm),F32)
        for c in range(3):
            v,gs=part(theirs+c*W,x_p,c); gsum=gsum+gs
            snd[blk(c)]=v.astype(BF); c_dn(c).start()
            tick("t%d"%c)
        for c in range(3):
            v,gs=part(mine+c*W,x_ref,c); gsum=gsum+gs
            dn[blk(c)]=v
            tick("u%d"%c)
        gx[0,0:1]=gsum
        c_gc=copy_to(gx.at[0],gx.at[1],sems,6,{"core":1-at.core}); c_gc.start()
        tick("g")
        c_gc.wait(); gring[0]=gx[0]+gx[1]
        def c_gr(d,t): return copy_to(gring.at[0 if t==0 else 4*d+t],gring.at[4*d+t+1],sems,7+4*d+t,{"chip":at.nxt[d]})
        c_gr(0,0).start(); c_gr(1,0).start()
        gtot=gring[0]
        for t in range(4):
            for d in range(2):
                if t<4-d:
                    c_gr(d,t).wait()
                    if t+1<4-d: c_gr(d,t+1).start()
                    gtot=gtot+gring[4*d+t+1]
            tick("g%d"%t)
        gx[2]=gtot
        c_gx=copy_to(gx.at[2],gx.at[3],sems,5,{"mp":1-mp}); c_gx.start()
        tick("z")
        for c in range(3):
            c_dn(c).wait()
            r=blk(c)
            d=dn[r]+rcv[r].astype(F32)
            x=x_ref[r].astype(F32)
            i1=lax.rsqrt(jnp.mean(x*x,axis=1,keepdims=True)+EPS)
            s=gain_a[...].astype(F32).reshape(1,-1)*d
            snd[r]=(res[r]+i1*s-x*(i1*i1*i1)*jnp.mean(s*x,axis=1,keepdims=True)).astype(BF)
        c_gx.wait(); gains_out[...]=gx[2]+gx[3]
        c_ig=pltpu.make_async_copy(snd,ig_h,lsem.at[11]); c_ig.start()
        M.finish(0); N.finish(0); O.finish(0)
        for v in range(3): C.finish(v)
        c_ig.wait()
    hT=V((nh,T,128),BF)
    pl.run_scoped(attn,hT,hT,hT,V((T,128),F32),V((T,128),F32),V((T,Dm),BF),V((R,Dm),BF),V((nh//2,Dm,H),BF),
                  V((Dm,T),BF),V((2,T,128),BF),V((2,64,T),BF),V((128,T),F32),V((nh//2,T,H),BF),V((R,Dm),F32))

def main_call(x,og,heads,hrecv,wo,wop,gain_a,gain_m,hbm,cid):
    R,Dm=x.shape; T,H=heads.shape
    Vs=pl.BlockSpec(memory_space=pltpu.VMEM); N=pl.BlockSpec(memory_space=pl.ANY); sd=jax.ShapeDtypeStruct; V=pltpu.VMEM
    scs=[s.scratch() for s in (RING_M,RING_N,RING_O,RING_C)]
    local=[V((R,H),BF),V((T,H),BF),V((R,Dm),F32)]+[V((R,Dm),BF)]*2
    local+=[V((4,8,Dm),F32),V((RING,8,Dm),F32),pltpu.SemaphoreType.DMA((2,7+RING)),pltpu.SemaphoreType.DMA((21,)),pltpu.SemaphoreType.DMA((2,3))]
    outs=[sd((R,Dm),BF)]*2+[sd((2,2,RING,48,1536),BF),sd((2,RING,48,H),BF),sd((3,2,RING,48,384),BF),sd((8,Dm),F32)]
    return pl.pallas_call(functools.partial(main_kernel,*[len(s) for s in scs]),
        out_shape=tuple(outs), in_specs=[Vs]*8+[N]*len(hbm), out_specs=(N,)*5+(Vs,),
        scratch_shapes=sum(scs,[])+local,
        compiler_params=pltpu.CompilerParams(collective_id=cid,has_side_effects=True,vmem_limit_bytes=67043328),
        name="mlp_and_backward")(x,og,heads,hrecv,wo,wop,gain_a,gain_m,*hbm)

def widen_kernel(mlp,wo,qkv,y,dx,gains,gate,up,down,out,query,key,value,y_out,dx_out,ga,gm):
    ga[...]=gains[0]; gm[...]=gains[1]
    y_out[...]=y[...].astype(F32); dx_out[...]=dx[...].astype(F32)
    F=mlp.shape[2]//3; H=wo.shape[1]; B=mlp.shape[1]
    for q in range(2):
        cs=slice(F*q,F*q+F)
        gate[:,cs]=mlp[q,:,0:F].astype(F32)
        up[:,cs]=mlp[q,:,F:2*F].astype(F32)
        down[cs,:]=mlp[q,:,2*F:3*F].astype(F32).T
    out[...]=wo[...].astype(F32).T
    for p in range(qkv.shape[0]):
        cs=slice(128*p,128*p+128)
        query[:,cs]=qkv[p,:,0:128].astype(F32)
        key[:,cs]=qkv[p,:,128:256].astype(F32)
        value[:,cs]=qkv[p,:,256:384].astype(F32)

def widen(mlp,wo,qkv,y,dx,gains):
    Dm,H=wo.shape; F=mlp.shape[2]//3; B=128; P3=qkv.shape[0]
    sd=jax.ShapeDtypeStruct
    row=lambda n: pl.BlockSpec((B,n),lambda i:(i,0))
    rows_spec=pl.BlockSpec((y.shape[0]//(Dm//B),y.shape[1]),lambda i:(i,0))
    col=lambda n: pl.BlockSpec((n,B),lambda i:(0,i))
    return pl.pallas_call(widen_kernel,grid=(Dm//B,),
        out_shape=(sd((Dm,2*F),F32),sd((Dm,2*F),F32),sd((2*F,Dm),F32),sd((H,Dm),F32))+(sd((Dm,H),F32),)*3+(sd(y.shape,F32),)*2+(sd((Dm,),F32),)*2,
        in_specs=[pl.BlockSpec((2,B,3*F),lambda i:(0,i,0)),row(H),pl.BlockSpec((P3,B,H),lambda i:(0,i,0)),rows_spec,rows_spec,pl.BlockSpec((8,Dm),lambda i:(0,0))],
        out_specs=(row(2*F),row(2*F),col(2*F),col(H),row(H),row(H),row(H),rows_spec,rows_spec)+(pl.BlockSpec((Dm,),lambda i:(0,)),)*2,
        compiler_params=pltpu.CompilerParams(vmem_limit_bytes=67043328),name="widen")(mlp,wo,qkv,y,dx,gains)


def on_device(layer_input, gain_attn, w_query, w_key, w_value, w_out, gain_mlp, w_gate, w_up, w_down,
              segment_start, segment_parent, out_grad):
    weights = (w_out, w_gate, w_up, w_down)
    x_peer, normed, cosine, sine, ke, ve, qe, heads, heads_peer, peer_out, peer_gate, peer_up, peer_down = front(
        layer_input, gain_attn, w_query, w_key, w_value, segment_start, segment_parent, weights, 2
    )
    output, input_grad, mlp_g, out_g, qkv_g, gain_g = main_call(
        layer_input, out_grad, heads, heads_peer, w_out, peer_out, gain_attn, gain_mlp,
        (w_gate, w_up, w_down, peer_gate, peer_up, peer_down, qe, ke, ve, cosine, sine, normed, x_peer,
         w_query, w_key, w_value), 1,
    )
    sums = [mlp_g.reshape(2, -1, mlp_g.shape[-1]), out_g.reshape(-1, out_g.shape[-1]), qkv_g.reshape(3, -1, qkv_g.shape[-1]), gain_g]
    if lax.axis_size("grp") > 1:
        sums = lax.psum([s.astype(F32) for s in sums], "grp")
    mlp_g, out_g, qkv_g, gain_g = sums
    gate_g, up_g, down_g, out_g, query_g, key_g, value_g, output, input_grad, gain_attn_grad, gain_mlp_grad = widen(
        mlp_g, out_g, qkv_g, output, input_grad, gain_g
    )
    return (
        output, input_grad, gain_attn_grad, query_g, key_g, value_g, out_g, gain_mlp_grad, gate_g, up_g, down_g,
    )


def solution(mesh):
    fine = Mesh(mesh.devices.reshape(-1, RING, 2, mesh.shape["mp"]), ("grp", "chip", "core", "mp"))
    dp = ("grp", "chip", "core")
    tok, col, row, tree = P(dp + ("mp",), None), P(None, "mp"), P("mp", None), P(dp, None)
    in_specs = (tok, P(), col, col, col, row, P(), col, col, row, tree, tree, tok)
    out_specs = (tok, tok, P(), col, col, col, row, P(), col, col, row)
    return jax.shard_map(on_device, mesh=fine, in_specs=in_specs, out_specs=out_specs, check_vma=False)
```
